32 devices in a mesh: wide: 16 (over z, y, core), narrow: 2 (over x).
Axes of the slice: x: 2, y: 2, z: 4, core: 2. Of those that a mesh axis runs over, the one named last changes fastest.
Arguments:
- inputs: bfloat16 [32, 1024, 512], P('narrow', 'wide'), may hold values from -6 to 6
- segment_ids: int32 [1024], replicated, may hold values from 0 to 31, never falling along the last dimension, each value on 1 to 64 neighbouring positions
- norm1_gain: float32 [512], replicated, may hold values from 0.5 to 1.5
- norm1_shift: float32 [512], replicated, may hold values from -1.2 to 1.2
- w_qkv: bfloat16 [512, 3, 512], P(None, None, 'narrow'), may hold values from -0.375 to 0.375
- w_out: bfloat16 [512, 512], P('narrow'), may hold values from -1.5 to 1.5
- norm2_gain: float32 [512], replicated, may hold values from 0.5 to 1.5
- norm2_shift: float32 [512], replicated, may hold values from -1.2 to 1.2
- w_up: bfloat16 [512, 2048], P(None, 'narrow'), may hold values from -0.25 to 0.25
- w_down: bfloat16 [2048, 512], P('narrow'), may hold values from -0.125 to 0.125
- cotangent: bfloat16 [32, 1024, 512], P('narrow', 'wide'), may hold values from -6 to 6
Outputs:
- block_out: bfloat16 [32, 1024, 512], P('narrow', 'wide')
- input_grad: float32 [32, 1024, 512], P('narrow', 'wide')
- norm1_gain_grad: float32 [512], replicated
- norm1_shift_grad: float32 [512], replicated
- w_qkv_grad: float32 [512, 3, 512], P(None, None, 'narrow')
- w_out_grad: float32 [512, 512], P('narrow')
- norm2_gain_grad: float32 [512], replicated
- norm2_shift_grad: float32 [512], replicated
- w_up_grad: float32 [512, 2048], P(None, 'narrow')
- w_down_grad: float32 [2048, 512], P('narrow')
The draws below stay inside these ranges and needn't reach their ends.
Inputs may be any that keep to these rules, and one draw needn't show every extreme that they name: `segment_ids`: segment ids never fall along the samples; each task spans 1 to 64 samples, and some task spans exactly 64.
All inputs are finite; a program needn't handle non-finite values.
Results may differ from the reference program's by a relative error of at most 0.017.
The reference program's roundings to bfloat16 on the way count: a program that leaves them out, or rounds other values in their place, can miss the bound.
Values may be sent and summed in bfloat16 or wider, within the bound.
No kernel may reach another device: no remote copies, remote signals or barrier semaphores. Data moves between devices by JAX's collectives and lax.ppermute only.
A program may use at most 128 MiB of HBM per device.

```python
import math
import jax
import jax.numpy as jnp
import numpy as np
from jax import lax

D = 512
HEADS = 8
HEAD_DIM = 64
FF = 2048
FEATS = 32
SAMP_DEV = 64
TASKS = 32
SAMPLES = 1024


def block_scale(own_key, dims, split, smallest, high):
    gain = 1.0
    for position, blocks in split:
        draws = jax.random.uniform(jax.random.fold_in(jax.random.fold_in(own_key, 6), position), (blocks,), jnp.float32, smallest / len(split), high / len(split))
        gain = gain * jnp.repeat(jnp.exp(draws), dims[position] // blocks).reshape((-1,) + (1,) * (len(dims) - 1 - position))
    return gain


def length_profile(number_of, total, bound, skew):
    loads = [(1 << 20) // math.isqrt(standing ** skew) + 1 for standing in range(2, number_of + 1)]
    rest, given = total - bound - (number_of - 1), [1] * (number_of - 1)
    while rest > 0:
        candidates = [i for i in range(number_of - 1) if given[i] < bound]
        mass, left = sum([loads[i] for i in candidates]), rest
        for i in candidates:
            extra = min(bound - given[i], max(1, left * loads[i] // mass), rest)
            given[i] = given[i] + extra
            rest = rest - extra
    return np.array([bound] + given)


def uneven_parts(key, count, total, most, lean):
    if count == 2:
        one = jax.random.randint(key, (), max(1, total - most), min(most, total - 1) + 1)
        return jnp.stack([one, total - one])
    sizes = jnp.asarray(length_profile(count, total, most, lean), jnp.int32)
    couples = (count - 1) // 2
    donor, taker = sizes[1:1 + 2 * couples:2], sizes[2:2 + 2 * couples:2]
    margin = jnp.minimum(donor - 1, most - taker)
    moved = jax.random.randint(jax.random.fold_in(key, 1), (couples,), 0, 1 << 20) % (margin + 1)
    sizes = sizes.at[1:1 + 2 * couples:2].set(donor - moved).at[2:2 + 2 * couples:2].set(taker + moved)
    return sizes[jax.random.permutation(jax.random.fold_in(key, 2), count)]


def gaussian(stream_key, extent, scale, reach, split=(), held_as=jnp.bfloat16):
    level = block_scale(stream_key, extent, split, -0.22, 0.18) if split else 1.0
    values = jax.random.normal(stream_key, extent, jnp.float32) * scale * level
    return jnp.minimum(jnp.maximum(values, -reach), reach).astype(held_as)


def setup_inputs(seed: int = 0) -> dict:
    seeds = jax.random.split(jax.random.key(seed), 12)
    inputs = gaussian(seeds[0], (FEATS, SAMPLES, D), 1.0, 6.0, ((0, 2), (1, 16)))
    segment_ids = jnp.searchsorted(jnp.cumsum(uneven_parts(seeds[1], TASKS, SAMPLES, SAMP_DEV, 1)), jnp.arange(SAMPLES), side="right").astype(jnp.int32)
    norm1_gain = jnp.clip(1.0 + 0.1 * jax.random.normal(seeds[2], (D,), jnp.float32), 0.5, 1.5)
    norm1_shift = gaussian(seeds[3], (D,), 0.3, 1.2, (), jnp.float32)
    w_qkv = gaussian(seeds[4], (D, 3, D), (D // 2) ** -0.5, 0.375, ((2, 2),))
    w_out = gaussian(seeds[5], (D, D), (max(1, 2 * D // SAMP_DEV)) ** -0.5, 1.5, ((0, 2),))
    norm2_gain = jnp.clip(1.0 + 0.1 * jax.random.normal(seeds[6], (D,), jnp.float32), 0.5, 1.5)
    norm2_shift = gaussian(seeds[7], (D,), 0.3, 1.2, (), jnp.float32)
    w_up = gaussian(seeds[8], (D, FF), D ** -0.5, 0.25, ((1, 2),))
    w_down = gaussian(seeds[9], (FF, D), FF ** -0.5, 0.125, ((0, 2),))
    cotangent = gaussian(seeds[10], (FEATS, SAMPLES, D), 1.0, 6.0, ((0, 2), (1, 16)))
    return dict(inputs=inputs, segment_ids=segment_ids, norm1_gain=norm1_gain, norm1_shift=norm1_shift, w_qkv=w_qkv, w_out=w_out, norm2_gain=norm2_gain, norm2_shift=norm2_shift, w_up=w_up, w_down=w_down, cotangent=cotangent)


epsilon = 1e-05
highest = lax.Precision.HIGHEST

@jax.custom_vjp
def low(v):
    return lax.optimization_barrier(v.astype(jnp.bfloat16)).astype(jnp.float32)

@jax.custom_vjp
def low_back(v):
    return v

def low_keep(v):
    return (low(v), None)

def low_pass(kept, grad):
    return (grad,)

def back_keep(v):
    return (v, None)

def back_low(kept, grad):
    return (low(grad),)
low.defvjp(low_keep, low_pass)
low_back.defvjp(back_keep, back_low)

def layer_norm(features, norm_gain, norm_shift):
    row_mean = lax.optimization_barrier(jnp.mean(features, axis=-1, keepdims=True))
    centred = features - row_mean
    row_var = lax.optimization_barrier(jnp.mean(centred * centred, axis=-1, keepdims=True))
    return centred * lax.rsqrt(row_var + epsilon) * norm_gain + norm_shift

def block_attention(query_block, key_block, value_block, query_ids, key_ids):
    score_scale = HEAD_DIM ** (-0.5)
    allowed = query_ids[:, None] == key_ids[None, :]
    scores = low_back(jnp.einsum('qhd,khd->hqk', query_block, key_block, precision=highest) * score_scale)
    scores = jnp.where(allowed[None, :, :], scores, -1e+30)
    row_top = lax.optimization_barrier(jnp.max(scores, axis=-1, keepdims=True))
    expo_terms = jnp.exp(scores - row_top)
    attn_probs = low(expo_terms / lax.optimization_barrier(jnp.sum(expo_terms, axis=-1, keepdims=True)))
    return jnp.einsum('hqk,khd->qhd', attn_probs, value_block, precision=highest)

def column_layer(features, norm1_gain, norm1_shift, w_qkv, w_out, norm2_gain, norm2_shift, w_up, w_down, padded_ids):
    normed_one = low(layer_norm(features, norm1_gain, norm1_shift))
    query_rows = low_back(low(jnp.dot(normed_one, w_qkv[:, 0, :], precision=highest)))
    key_rows = low_back(low(jnp.dot(normed_one, w_qkv[:, 1, :], precision=highest)))
    value_rows = low_back(low(jnp.dot(normed_one, w_qkv[:, 2, :], precision=highest)))
    blocks = SAMPLES // SAMP_DEV
    zero_rim = jnp.zeros((SAMP_DEV, D), jnp.float32)
    key_padded = jnp.concatenate([zero_rim, key_rows, zero_rim], axis=0).reshape(SAMPLES + 2 * SAMP_DEV, HEADS, HEAD_DIM)
    value_padded = jnp.concatenate([zero_rim, value_rows, zero_rim], axis=0).reshape(SAMPLES + 2 * SAMP_DEV, HEADS, HEAD_DIM)
    query_blocks = query_rows.reshape(blocks, SAMP_DEV, HEADS, HEAD_DIM)

    def one_block(block_pair):
        query_block, block_index = block_pair
        first_row = block_index * SAMP_DEV
        key_block = lax.dynamic_slice_in_dim(key_padded, first_row, 3 * SAMP_DEV, 0)
        value_block = lax.dynamic_slice_in_dim(value_padded, first_row, 3 * SAMP_DEV, 0)
        key_ids = lax.dynamic_slice_in_dim(padded_ids, first_row, 3 * SAMP_DEV, 0)
        query_ids = lax.dynamic_slice_in_dim(padded_ids, first_row + SAMP_DEV, SAMP_DEV, 0)
        return block_attention(query_block, key_block, value_block, query_ids, key_ids)
    attended = lax.map(jax.checkpoint(one_block), (query_blocks, jnp.arange(blocks, dtype=jnp.int32)))
    attended = low_back(low(attended.reshape(SAMPLES, D)))
    hidden_state = features + low_back(jnp.dot(attended, w_out, precision=highest))
    normed_two = low(layer_norm(hidden_state, norm2_gain, norm2_shift))
    pre_act = low_back(jnp.dot(normed_two, w_up, precision=highest))
    activated = low(jax.nn.gelu(pre_act, approximate=False))
    return hidden_state + jnp.dot(activated, w_down, precision=highest)

def reference(inputs, segment_ids, norm1_gain, norm1_shift, w_qkv, w_out, norm2_gain, norm2_shift, w_up, w_down, cotangent):
    params = (norm1_gain, norm1_shift, w_qkv.astype(jnp.float32), w_out.astype(jnp.float32), norm2_gain, norm2_shift, w_up.astype(jnp.float32), w_down.astype(jnp.float32))
    id_rim = jnp.full((SAMP_DEV,), -1, jnp.int32)
    padded_ids = jnp.concatenate([id_rim, segment_ids.astype(jnp.int32), id_rim])

    def column_step(running, column_pair):
        column_in, column_cot = column_pair

        def forward(features, weights):
            return column_layer(features, weights[0], weights[1], weights[2], weights[3], weights[4], weights[5], weights[6], weights[7], padded_ids)
        column_out, pullback = jax.vjp(forward, column_in.astype(jnp.float32), params)
        grad_pair = pullback(column_cot.astype(jnp.float32))
        running = jax.tree.map(lambda total_grad, new_grad: total_grad + new_grad, running, grad_pair[1])
        return (running, (column_out.astype(jnp.bfloat16), grad_pair[0]))
    zero_grads = jax.tree.map(jnp.zeros_like, params)
    summed, stacked = lax.scan(column_step, zero_grads, (inputs, cotangent))
    return (stacked[0], stacked[1], summed[0], summed[1], summed[2], summed[3], summed[4], summed[5], summed[6], summed[7])
```

```python
import jax
import jax.numpy as jnp
from jax import lax
from jax.experimental import pallas as pl
from jax.experimental.pallas import tpu as pltpu
from jax.sharding import PartitionSpec as P

HEAD_DIM = 64
HEADS_PER_GROUP = 4
GROUP_COLS = HEAD_DIM * HEADS_PER_GROUP
EPS = 1e-05
SCALE = HEAD_DIM ** (-0.5)
F32 = jnp.float32
BF16 = jnp.bfloat16
NEG = -1e30


def dot_nn(a, b):
    return lax.dot_general(a, b, (((1,), (0,)), ((), ())), preferred_element_type=F32)


def dot_nt(a, b):
    return lax.dot_general(a, b, (((1,), (1,)), ((), ())), preferred_element_type=F32)


def dot_tn(a, b):
    return lax.dot_general(a, b, (((0,), (0,)), ((), ())), preferred_element_type=F32)


def norm_parts(z):
    mean = jnp.mean(z, axis=-1, keepdims=True)
    centred = z - mean
    var = jnp.mean(centred * centred, axis=-1, keepdims=True)
    rstd = lax.rsqrt(var + EPS)
    return centred * rstd, rstd


def norm_back(grad, xhat, rstd, gain):
    gg = grad * gain
    m1 = jnp.mean(gg, axis=-1, keepdims=True)
    m2 = jnp.mean(gg * xhat, axis=-1, keepdims=True)
    return rstd * (gg - m1 - xhat * m2)


def lane_head(rows, dtype):
    lane = lax.broadcasted_iota(jnp.int32, (rows, GROUP_COLS), 1)
    return [
        ((lane >= h * HEAD_DIM) & (lane < (h + 1) * HEAD_DIM)).astype(F32).astype(dtype)
        for h in range(HEADS_PER_GROUP)
    ]


def block_diag(rows, masks):
    return jnp.concatenate([rows * m for m in masks], axis=0)


def pick_heads(full, masks, rows):
    out = full[0:rows] * masks[0]
    for h in range(1, HEADS_PER_GROUP):
        out = out + full[h * rows : (h + 1) * rows] * masks[h]
    return out


def attn_fwd_kernel(idc, idr, xp, xo, xn, w0, w1, gain, shift, qkv_ref, att_ref):
    feats, samp, width = xo.shape
    rows = feats * samp
    x = jnp.concatenate(
        [xp[...].reshape(rows, width), xo[...].reshape(rows, width), xn[...].reshape(rows, width)],
        axis=0,
    ).astype(F32)
    xhat, _ = norm_parts(x)
    normed = (xhat * gain[...] + shift[...]).astype(BF16)
    for hg, w in enumerate((w0, w1)):
        qkv = dot_nn(normed, w[...]).astype(BF16)
        qkv_ref[hg] = qkv.reshape(3, rows, 3 * GROUP_COLS)
    allowed = idc[...] == idr[1:2, :]
    m16 = lane_head(1, BF16)
    m32 = lane_head(1, F32)
    for f in range(feats):
        sl = slice(f * samp, (f + 1) * samp)
        for hg in range(2):
            q = qkv_ref[hg, 1, sl, 0:GROUP_COLS]
            k = jnp.concatenate(
                [qkv_ref[hg, w, sl, GROUP_COLS : 2 * GROUP_COLS] for w in range(3)], axis=0
            )
            v = jnp.concatenate(
                [qkv_ref[hg, w, sl, 2 * GROUP_COLS : 3 * GROUP_COLS] for w in range(3)], axis=0
            )
            s = dot_nt(k, block_diag(q, m16)) * SCALE
            s = jnp.where(allowed, s, NEG)
            top = jnp.max(s, axis=0, keepdims=True)
            e = jnp.exp(s - top)
            total = jnp.sum(e, axis=0, keepdims=True)
            p = (e * (1.0 / total)).astype(BF16)
            o = pick_heads(dot_tn(p, v), m32, samp)
            att_ref[f, :, hg * GROUP_COLS : (hg + 1) * GROUP_COLS] = o.astype(BF16)


def phi_parts(u):
    e = jnp.exp(-0.5 * (u * u))
    t = 1.0 / (1.0 + (0.3275911 * 0.7071067811865476) * jnp.abs(u))
    poly = t * (
        0.127414796
        + t * (-0.142248368 + t * (0.7107068705 + t * (-0.7265760135 + t * 0.5307027145)))
    )
    tail = poly * e
    cdf = jnp.where(u < 0, tail, 1.0 - tail)
    return cdf, u * (e * 0.3989422804014327)


def chain_kernel(
    x, att, cot, wo0, wo1, wu0, wu1, wd0, wd1, gain, shift,
    out_ref, n2_ref, act_ref, pre_ref, hgrad_ref, res_ref, dat_ref, g2_ref, s2_ref,
):
    half = wo0.shape[0]
    hidden = (
        x[...].astype(F32) + dot_nn(att[:, :half], wo0[...]) + dot_nn(att[:, half:], wo1[...])
    )
    xhat, rstd = norm_parts(hidden)
    normed = (xhat * gain[...] + shift[...]).astype(BF16)
    n2_ref[...] = normed
    c = cot[...]
    ff = wu0.shape[1]
    step = min(512, ff)
    mlp = jnp.zeros_like(hidden)
    dn2 = jnp.zeros_like(hidden)
    for part, (wu, wd) in enumerate(((wu0, wd0), (wu1, wd1))):
        for j in range(0, ff, step):
            up = wu[:, j : j + step]
            down = wd[j : j + step, :]
            u = dot_nn(normed, up)
            cdf, upd = phi_parts(u)
            act = (u * cdf).astype(BF16)
            act_ref[part, :, j : j + step] = act
            mlp = mlp + dot_nn(act, down)
            pre = (dot_nt(c, down) * (cdf + upd)).astype(BF16)
            pre_ref[part, :, j : j + step] = pre
            dn2 = dn2 + dot_nt(pre, up)
    out_ref[...] = (hidden + mlp).astype(BF16)

    @pl.when(pl.program_id(0) == 0)
    def _():
        g2_ref[...] = jnp.zeros_like(g2_ref)
        s2_ref[...] = jnp.zeros_like(s2_ref)

    g2_ref[...] += jnp.sum(dn2 * xhat, axis=0, keepdims=True)
    s2_ref[...] += jnp.sum(dn2, axis=0, keepdims=True)
    hgrad = c.astype(F32) + norm_back(dn2, xhat, rstd, gain[...])
    hgrad_ref[...] = hgrad
    res = hgrad.astype(BF16)
    res_ref[...] = res
    dat_ref[:, :half] = dot_nt(res, wo0[...]).astype(BF16)
    dat_ref[:, half:] = dot_nt(res, wo1[...]).astype(BF16)


def attn_bwd_kernel(
    idc, idr, x, qkv_ref, dp_ref, do_ref, dn_ref, hgrad, w0, w1, gain, shift,
    igrad_ref, dw_ref, g1_ref, s1_ref, acc, dqkv,
):
    feats, samp, width = x.shape
    rows = feats * samp
    m16 = lane_head(1, BF16)
    m32 = lane_head(1, F32)
    spans = ((0, 2), (0, 3), (1, 3))
    masks = [idc[a * samp : b * samp, :] == idr[g : g + 1, :] for g, (a, b) in enumerate(spans)]
    grads = (dp_ref, do_ref, dn_ref)
    for f in range(feats):
        sl = slice(f * samp, (f + 1) * samp)
        for hg in range(2):
            cols = slice(hg * GROUP_COLS, (hg + 1) * GROUP_COLS)
            k = jnp.concatenate(
                [qkv_ref[hg, w, sl, GROUP_COLS : 2 * GROUP_COLS] for w in range(3)], axis=0
            )
            v = jnp.concatenate(
                [qkv_ref[hg, w, sl, 2 * GROUP_COLS : 3 * GROUP_COLS] for w in range(3)], axis=0
            )
            dk = jnp.zeros((samp, GROUP_COLS), F32)
            dv = jnp.zeros((samp, GROUP_COLS), F32)
            for g, (a, b) in enumerate(spans):
                ks = k[a * samp : b * samp]
                vs = v[a * samp : b * samp]
                qbd = block_diag(qkv_ref[hg, g, sl, 0:GROUP_COLS], m16)
                dbd = block_diag(grads[g][f, :, cols], m16)
                s = dot_nt(ks, qbd) * SCALE
                s = jnp.where(masks[g], s, NEG)
                top = jnp.max(s, axis=0, keepdims=True)
                e = jnp.exp(s - top)
                total = jnp.sum(e, axis=0, keepdims=True)
                p = e * (1.0 / total)
                dp = dot_nt(vs, dbd)
                pd = p * dp
                delta = jnp.sum(pd, axis=0, keepdims=True)
                ds = (pd - p * delta).astype(BF16)
                own = slice((1 - a) * samp, (2 - a) * samp)
                dk = dk + dot_nn(ds[own], qbd)
                dv = dv + dot_nn(p[own].astype(BF16), dbd)
                if g == 1:
                    dq = pick_heads(dot_tn(ds, ks), m32, samp)
            dqkv[hg, sl, 0:GROUP_COLS] = (dq * SCALE).astype(BF16)
            dqkv[hg, sl, GROUP_COLS : 2 * GROUP_COLS] = (dk * SCALE).astype(BF16)
            dqkv[hg, sl, 2 * GROUP_COLS : 3 * GROUP_COLS] = dv.astype(BF16)
    xhat, rstd = norm_parts(x[...].reshape(rows, width).astype(F32))
    normed = (xhat * gain[...] + shift[...]).astype(BF16)
    dn1 = dot_nt(dqkv[0], w0[...]) + dot_nt(dqkv[1], w1[...])

    @pl.when(pl.program_id(0) == 0)
    def _():
        g1_ref[...] = jnp.zeros_like(g1_ref)
        s1_ref[...] = jnp.zeros_like(s1_ref)
        acc[...] = jnp.zeros_like(acc)

    g1_ref[...] += jnp.sum(dn1 * xhat, axis=0, keepdims=True)
    s1_ref[...] += jnp.sum(dn1, axis=0, keepdims=True)
    for hg in range(2):
        acc[hg] += dot_tn(normed, dqkv[hg])
    igrad_ref[...] = hgrad[...] + norm_back(dn1, xhat, rstd, gain[...])

    @pl.when(pl.program_id(0) == pl.num_programs(0) - 1)
    def _():
        dw_ref[...] = acc[...].astype(BF16)


def swap(x, axis, bit):
    count = lax.axis_size(axis)
    return lax.ppermute(x, axis, [(i, i ^ bit) for i in range(count)])


def halo(x, axis):
    count = lax.axis_size(axis)
    prev = lax.ppermute(x, axis, [(i, i + 1) for i in range(count - 1)])
    nxt = lax.ppermute(x, axis, [(i + 1, i) for i in range(count - 1)])
    return prev, nxt


def gather_pieces(x, axis):
    pieces = [x]
    bit = 1
    while bit < lax.axis_size(axis):
        pieces = pieces + [swap(p, axis, bit) for p in pieces]
        bit *= 2
    return pieces


def two_halves(pieces, dim):
    if len(pieces) == 2:
        return pieces
    cut = len(pieces) // 2
    return [jnp.concatenate(pieces[:cut], axis=dim), jnp.concatenate(pieces[cut:], axis=dim)]


def bit_of(axis, bit):
    return (lax.axis_index(axis) // bit) % 2 == 1


def scatter_step(pieces, axis, bit):
    mine = bit_of(axis, bit)
    out = []
    for p in pieces:
        cut = p.shape[0] // 2
        lo, hi = p[:cut], p[cut:]
        got = swap(jnp.where(mine, lo, hi), axis, bit)
        out.append((jnp.where(mine, hi, lo).astype(F32) + got.astype(F32)).astype(BF16))
    return out


def gather_step(p, axis, bit):
    mine = bit_of(axis, bit)
    got = swap(p, axis, bit)
    return jnp.concatenate([jnp.where(mine, got, p), jnp.where(mine, p, got)], axis=0)


def reduce_pieces(pieces, wide, narrow):
    count = lax.axis_size(wide)
    if count > 1:
        pieces = scatter_step(pieces, wide, 1)
    bit = lax.axis_size(narrow) // 2
    while bit >= 1:
        got = [swap(p, narrow, bit) for p in pieces[bit:]]
        pieces = [(a.astype(F32) + b.astype(F32)).astype(BF16) for a, b in zip(pieces[:bit], got)]
        bit //= 2
    bits = []
    bit = 2
    while bit < count:
        bits.append(bit)
        bit *= 2
    for bit in bits:
        pieces = scatter_step(pieces, wide, bit)
    total = pieces[0]
    for bit in reversed(bits):
        total = gather_step(total, wide, bit)
    if count > 1:
        total = gather_step(total, wide, 1)
    return total


def rows512(a):
    cols = a.shape[1]
    if cols < 512:
        return a.reshape(-1, 512)
    return jnp.concatenate([a[:, j : j + 512] for j in range(0, cols, 512)], axis=0)


def unrows512(a, rows, cols):
    if cols < 512:
        return a.reshape(rows, cols)
    return jnp.concatenate([a[j * rows : (j + 1) * rows] for j in range(cols // 512)], axis=1)


def local(
    inputs, segment_ids, norm1_gain, norm1_shift, w_qkv, w_out,
    norm2_gain, norm2_shift, w_up, w_down, cotangent,
):
    feats, samp, width = inputs.shape
    tokens = feats * samp
    blocks = lax.axis_size("narrow")
    group = max(g for g in (1, 2, 4) if feats % g == 0)
    steps = feats // group
    rows = group * samp
    head_cols = w_qkv.shape[2]

    x_prev, x_next = halo(inputs, "wide")
    qkv_halves = [
        h.reshape(width, 3 * h.shape[2]) for h in two_halves(gather_pieces(w_qkv, "narrow"), 2)
    ]
    out_halves = two_halves(gather_pieces(w_out, "narrow"), 0)
    up_halves = two_halves(gather_pieces(w_up, "narrow"), 1)
    down_halves = two_halves(gather_pieces(w_down, "narrow"), 0)

    id_rim = jnp.full((samp,), -1, jnp.int32)
    padded_ids = jnp.concatenate([id_rim, segment_ids, id_rim])
    window_ids = lax.dynamic_slice_in_dim(
        padded_ids, lax.axis_index("wide") * samp, 3 * samp, 0
    )
    id_col = window_ids[:, None]
    id_row = jnp.tile(window_ids.reshape(3, samp), (1, HEADS_PER_GROUP))
    gain1, shift1 = norm1_gain[None, :], norm1_shift[None, :]
    gain2, shift2 = norm2_gain[None, :], norm2_shift[None, :]

    def whole(a):
        return pl.BlockSpec(a.shape, lambda i: (0,) * a.ndim, pipeline_mode=pl.Buffered(1))

    cube = pl.BlockSpec((group, samp, width), lambda i: (i, 0, 0))
    flat = pl.BlockSpec((rows, width), lambda i: (i, 0))
    line = pl.BlockSpec((1, width), lambda i: (0, 0))
    qkv_block = pl.BlockSpec((2, 3, rows, 3 * GROUP_COLS), lambda i: (0, 0, i, 0))

    qkv, attended = pl.pallas_call(
        attn_fwd_kernel,
        grid=(steps,),
        in_specs=[whole(id_col), whole(id_row), cube, cube, cube]
        + [whole(a) for a in (*qkv_halves, gain1, shift1)],
        out_specs=[qkv_block, cube],
        out_shape=[
            jax.ShapeDtypeStruct((2, 3, tokens, 3 * GROUP_COLS), BF16),
            jax.ShapeDtypeStruct((feats, samp, width), BF16),
        ],
        name="attn_fwd",
    )(id_col, id_row, x_prev, inputs, x_next, *qkv_halves, gain1, shift1)

    att_flat = attended.reshape(tokens, width)
    x_flat = inputs.reshape(tokens, width)
    cot_flat = cotangent.reshape(tokens, width)
    half_ff = up_halves[0].shape[1]
    wide_block = pl.BlockSpec((2, rows, half_ff), lambda i: (0, i, 0))
    chain_args = (*out_halves, up_halves[0], up_halves[1], down_halves[0], down_halves[1], gain2, shift2)
    tok = lambda dtype: jax.ShapeDtypeStruct((tokens, width), dtype)
    vec = jax.ShapeDtypeStruct((1, width), F32)
    block_out, normed_two, activated, pre_grad, hidden_grad, residual, dattended, gain2_grad, shift2_grad = pl.pallas_call(
        chain_kernel,
        grid=(steps,),
        in_specs=[flat, flat, flat] + [whole(a) for a in chain_args],
        out_specs=[flat, flat, wide_block, wide_block, flat, flat, flat, line, line],
        out_shape=[
            tok(BF16), tok(BF16),
            jax.ShapeDtypeStruct((2, tokens, half_ff), BF16),
            jax.ShapeDtypeStruct((2, tokens, half_ff), BF16),
            tok(F32), tok(BF16), tok(BF16), vec, vec,
        ],
        name="chain",
    )(x_flat, att_flat, cot_flat, *chain_args)

    datt = dattended.reshape(feats, samp, width)
    d_prev, d_next = halo(datt, "wide")

    def pieces_of(a, dim):
        per = blocks // 2
        size = a[0].shape[dim] // per
        return [lax.slice_in_dim(h, j * size, (j + 1) * size, axis=dim) for h in a for j in range(per)]

    up_grads = pieces_of([dot_tn(normed_two, pre_grad[h]).astype(BF16) for h in range(2)], 1)
    down_grads = pieces_of([dot_tn(activated[h], cot_flat).astype(BF16) for h in range(2)], 0)
    half = width // 2
    out_grads = pieces_of(
        [dot_tn(att_flat[:, h * half : (h + 1) * half], residual).astype(BF16) for h in range(2)], 0
    )
    packs = [
        jnp.concatenate([rows512(u), d, o], axis=0)
        for u, d, o in zip(up_grads, down_grads, out_grads)
    ]
    pack = reduce_pieces(packs, "wide", "narrow")
    up_rows = rows512(jnp.zeros(w_up.shape, BF16)).shape[0]
    down_rows = w_down.shape[0]
    up_grad = unrows512(pack[:up_rows], *w_up.shape).astype(F32)
    down_grad = pack[up_rows : up_rows + down_rows].astype(F32)
    out_grad = pack[up_rows + down_rows :].astype(F32)

    input_grad, qkv_grads, gain1_grad, shift1_grad = pl.pallas_call(
        attn_bwd_kernel,
        grid=(steps,),
        in_specs=[whole(id_col), whole(id_row), cube, qkv_block, cube, cube, cube, flat]
        + [whole(a) for a in (*qkv_halves, gain1, shift1)],
        out_specs=[
            flat,
            pl.BlockSpec((2, width, 3 * GROUP_COLS), lambda i: (0, 0, 0)),
            line,
            line,
        ],
        out_shape=[
            tok(F32),
            jax.ShapeDtypeStruct((2, width, 3 * GROUP_COLS), BF16),
            vec,
            vec,
        ],
        scratch_shapes=[
            pltpu.VMEM((2, width, 3 * GROUP_COLS), F32),
            pltpu.VMEM((2, rows, 3 * GROUP_COLS), BF16),
        ],
        name="attn_bwd",
    )(id_col, id_row, inputs, qkv, d_prev, datt, d_next, hidden_grad, *qkv_halves, gain1, shift1)

    if blocks == 2:
        qkv_pieces = [qkv_grads[0], qkv_grads[1]]
    else:
        qkv_pieces = [
            p.reshape(width, 3 * head_cols)
            for p in pieces_of([qkv_grads[h].reshape(width, 3, GROUP_COLS) for h in range(2)], 2)
        ]
    qkv_grad = reduce_pieces(qkv_pieces, "wide", "narrow").reshape(width, 3, head_cols).astype(F32)
    norm_sums = lax.psum(
        jnp.concatenate([gain1_grad, shift1_grad, gain2_grad, shift2_grad], axis=0),
        ("wide", "narrow"),
    )
    return (
        block_out.reshape(feats, samp, width),
        input_grad.reshape(feats, samp, width),
        norm_sums[0],
        norm_sums[1],
        qkv_grad,
        out_grad,
        norm_sums[2],
        norm_sums[3],
        up_grad,
        down_grad,
    )


def solution(mesh):
    rows = P("narrow", "wide", None)
    placed = (
        rows, P(), P(), P(), P(None, None, "narrow"), P("narrow", None),
        P(), P(), P(None, "narrow"), P("narrow", None), rows,
    )
    outs = (
        rows, rows, P(), P(), P(None, None, "narrow"), P("narrow", None),
        P(), P(), P(None, "narrow"), P("narrow", None),
    )
    return jax.shard_map(local, mesh=mesh, in_specs=placed, out_specs=outs, check_vma=False)
```

```python
import jax
import jax.numpy as jnp
from jax import lax
from jax.experimental import pallas as pl
from jax.experimental.pallas import tpu as pltpu
from jax.sharding import PartitionSpec as P

HEAD_DIM = 64
HEADS_PER_GROUP = 4
GROUP_COLS = HEAD_DIM * HEADS_PER_GROUP
EPS = 1e-05
SCALE = HEAD_DIM ** (-0.5)
F32 = jnp.float32
BF16 = jnp.bfloat16
NEG = -1e30


def dot_nn(a, b):
    return lax.dot_general(a, b, (((1,), (0,)), ((), ())), preferred_element_type=F32)


def dot_nt(a, b):
    return lax.dot_general(a, b, (((1,), (1,)), ((), ())), preferred_element_type=F32)


def dot_tn(a, b):
    return lax.dot_general(a, b, (((0,), (0,)), ((), ())), preferred_element_type=F32)


def norm_parts(z):
    mean = jnp.mean(z, axis=-1, keepdims=True)
    centred = z - mean
    var = jnp.mean(centred * centred, axis=-1, keepdims=True)
    rstd = lax.rsqrt(var + EPS)
    return centred * rstd, rstd


def norm_back(grad, xhat, rstd, gain):
    gg = grad * gain
    m1 = jnp.mean(gg, axis=-1, keepdims=True)
    m2 = jnp.mean(gg * xhat, axis=-1, keepdims=True)
    return rstd * (gg - m1 - xhat * m2)


def lane_head(rows, dtype):
    lane = lax.broadcasted_iota(jnp.int32, (rows, GROUP_COLS), 1)
    return [
        ((lane >= h * HEAD_DIM) & (lane < (h + 1) * HEAD_DIM)).astype(F32).astype(dtype)
        for h in range(HEADS_PER_GROUP)
    ]


def block_diag(rows, masks):
    return jnp.concatenate([rows * m for m in masks], axis=0)


def pick_heads(full, masks, rows):
    out = full[0:rows] * masks[0]
    for h in range(1, HEADS_PER_GROUP):
        out = out + full[h * rows : (h + 1) * rows] * masks[h]
    return out


def attn_fwd_kernel(idc, idr, xp, xo, xn, w0, w1, gain, shift, qkv_ref, att_ref):
    feats, samp, width = xo.shape
    rows = feats * samp
    x = jnp.concatenate(
        [xp[...].reshape(rows, width), xo[...].reshape(rows, width), xn[...].reshape(rows, width)],
        axis=0,
    ).astype(F32)
    xhat, _ = norm_parts(x)
    normed = (xhat * gain[...] + shift[...]).astype(BF16)
    for hg, w in enumerate((w0, w1)):
        qkv = dot_nn(normed, w[...]).astype(BF16)
        qkv_ref[hg] = qkv.reshape(3, rows, 3 * GROUP_COLS)
    allowed = idc[...] == idr[1:2, :]
    m16 = lane_head(1, BF16)
    m32 = lane_head(1, F32)
    for f in range(feats):
        sl = slice(f * samp, (f + 1) * samp)
        for hg in range(2):
            q = qkv_ref[hg, 1, sl, 0:GROUP_COLS]
            k = jnp.concatenate(
                [qkv_ref[hg, w, sl, GROUP_COLS : 2 * GROUP_COLS] for w in range(3)], axis=0
            )
            v = jnp.concatenate(
                [qkv_ref[hg, w, sl, 2 * GROUP_COLS : 3 * GROUP_COLS] for w in range(3)], axis=0
            )
            s = dot_nt(k, block_diag(q, m16)) * SCALE
            s = jnp.where(allowed, s, NEG)
            top = jnp.max(s, axis=0, keepdims=True)
            e = jnp.exp(s - top)
            total = jnp.sum(e, axis=0, keepdims=True)
            p = (e * (1.0 / total)).astype(BF16)
            o = pick_heads(dot_tn(p, v), m32, samp)
            att_ref[f, :, hg * GROUP_COLS : (hg + 1) * GROUP_COLS] = o.astype(BF16)


def phi_parts(u):
    e = jnp.exp(-0.5 * (u * u))
    t = 1.0 / (1.0 + (0.3275911 * 0.7071067811865476) * jnp.abs(u))
    poly = t * (
        0.127414796
        + t * (-0.142248368 + t * (0.7107068705 + t * (-0.7265760135 + t * 0.5307027145)))
    )
    tail = poly * e
    cdf = jnp.where(u < 0, tail, 1.0 - tail)
    return cdf, u * (e * 0.3989422804014327)


def chain_kernel(
    x, att, cot, wo0, wo1, wu0, wu1, wd0, wd1, gain, shift,
    out_ref, n2_ref, act_ref, pre_ref, hgrad_ref, res_ref, dat_ref, g2_ref, s2_ref,
):
    half = wo0.shape[0]
    hidden = (
        x[...].astype(F32) + dot_nn(att[:, :half], wo0[...]) + dot_nn(att[:, half:], wo1[...])
    )
    xhat, rstd = norm_parts(hidden)
    normed = (xhat * gain[...] + shift[...]).astype(BF16)
    n2_ref[...] = normed
    c = cot[...]
    ff = wu0.shape[1]
    step = min(512, ff)
    mlp = jnp.zeros_like(hidden)
    dn2 = jnp.zeros_like(hidden)
    for part, (wu, wd) in enumerate(((wu0, wd0), (wu1, wd1))):
        for j in range(0, ff, step):
            up = wu[:, j : j + step]
            down = wd[j : j + step, :]
            u = dot_nn(normed, up)
            cdf, upd = phi_parts(u)
            act = (u * cdf).astype(BF16)
            act_ref[part, :, j : j + step] = act
            mlp = mlp + dot_nn(act, down)
            pre = (dot_nt(c, down) * (cdf + upd)).astype(BF16)
            pre_ref[part, :, j : j + step] = pre
            dn2 = dn2 + dot_nt(pre, up)
    out_ref[...] = (hidden + mlp).astype(BF16)

    @pl.when(pl.program_id(0) == 0)
    def _():
        g2_ref[...] = jnp.zeros_like(g2_ref)
        s2_ref[...] = jnp.zeros_like(s2_ref)

    g2_ref[...] += jnp.sum(dn2 * xhat, axis=0, keepdims=True)
    s2_ref[...] += jnp.sum(dn2, axis=0, keepdims=True)
    hgrad = c.astype(F32) + norm_back(dn2, xhat, rstd, gain[...])
    hgrad_ref[...] = hgrad
    res = hgrad.astype(BF16)
    res_ref[...] = res
    dat_ref[:, :half] = dot_nt(res, wo0[...]).astype(BF16)
    dat_ref[:, half:] = dot_nt(res, wo1[...]).astype(BF16)


def attn_bwd_kernel(
    idc, idr, x, qkv_ref, dp_ref, do_ref, dn_ref, hgrad, w0, w1, gain, shift,
    igrad_ref, dw_ref, g1_ref, s1_ref, acc, dqkv,
):
    feats, samp, width = x.shape
    rows = feats * samp
    m16 = lane_head(1, BF16)
    m32 = lane_head(1, F32)
    spans = ((0, 2), (0, 3), (1, 3))
    masks = [idc[a * samp : b * samp, :] == idr[g : g + 1, :] for g, (a, b) in enumerate(spans)]
    grads = (dp_ref, do_ref, dn_ref)
    for f in range(feats):
        sl = slice(f * samp, (f + 1) * samp)
        for hg in range(2):
            cols = slice(hg * GROUP_COLS, (hg + 1) * GROUP_COLS)
            k = jnp.concatenate(
                [qkv_ref[hg, w, sl, GROUP_COLS : 2 * GROUP_COLS] for w in range(3)], axis=0
            )
            v = jnp.concatenate(
                [qkv_ref[hg, w, sl, 2 * GROUP_COLS : 3 * GROUP_COLS] for w in range(3)], axis=0
            )
            dk = jnp.zeros((samp, GROUP_COLS), F32)
            dv = jnp.zeros((samp, GROUP_COLS), F32)
            for g, (a, b) in enumerate(spans):
                ks = k[a * samp : b * samp]
                vs = v[a * samp : b * samp]
                qbd = block_diag(qkv_ref[hg, g, sl, 0:GROUP_COLS], m16)
                dbd = block_diag(grads[g][f, :, cols], m16)
                s = dot_nt(ks, qbd) * SCALE
                s = jnp.where(masks[g], s, NEG)
                top = jnp.max(s, axis=0, keepdims=True)
                e = jnp.exp(s - top)
                total = jnp.sum(e, axis=0, keepdims=True)
                p = e * (1.0 / total)
                dp = dot_nt(vs, dbd)
                pd = p * dp
                delta = jnp.sum(pd, axis=0, keepdims=True)
                ds = (pd - p * delta).astype(BF16)
                own = slice((1 - a) * samp, (2 - a) * samp)
                dk = dk + dot_nn(ds[own], qbd)
                dv = dv + dot_nn(p[own].astype(BF16), dbd)
                if g == 1:
                    dq = pick_heads(dot_tn(ds, ks), m32, samp)
            dqkv[hg, sl, 0:GROUP_COLS] = (dq * SCALE).astype(BF16)
            dqkv[hg, sl, GROUP_COLS : 2 * GROUP_COLS] = (dk * SCALE).astype(BF16)
            dqkv[hg, sl, 2 * GROUP_COLS : 3 * GROUP_COLS] = dv.astype(BF16)
    xhat, rstd = norm_parts(x[...].reshape(rows, width).astype(F32))
    normed = (xhat * gain[...] + shift[...]).astype(BF16)
    dn1 = dot_nt(dqkv[0], w0[...]) + dot_nt(dqkv[1], w1[...])

    @pl.when(pl.program_id(0) == 0)
    def _():
        g1_ref[...] = jnp.zeros_like(g1_ref)
        s1_ref[...] = jnp.zeros_like(s1_ref)
        acc[...] = jnp.zeros_like(acc)

    g1_ref[...] += jnp.sum(dn1 * xhat, axis=0, keepdims=True)
    s1_ref[...] += jnp.sum(dn1, axis=0, keepdims=True)
    for hg in range(2):
        acc[hg] += dot_tn(normed, dqkv[hg])
    igrad_ref[...] = hgrad[...] + norm_back(dn1, xhat, rstd, gain[...])

    @pl.when(pl.program_id(0) == pl.num_programs(0) - 1)
    def _():
        dw_ref[...] = acc[...].astype(BF16)


def swap(x, axis, bit):
    count = lax.axis_size(axis)
    return lax.ppermute(x, axis, [(i, i ^ bit) for i in range(count)])


def halo(x, axis):
    count = lax.axis_size(axis)
    prev = lax.ppermute(x, axis, [(i, i + 1) for i in range(count - 1)])
    nxt = lax.ppermute(x, axis, [(i + 1, i) for i in range(count - 1)])
    return prev, nxt


def gather_pieces(x, axis):
    pieces = [x]
    bit = 1
    while bit < lax.axis_size(axis):
        pieces = pieces + [swap(p, axis, bit) for p in pieces]
        bit *= 2
    return pieces


def two_halves(pieces, dim):
    if len(pieces) == 2:
        return pieces
    cut = len(pieces) // 2
    return [jnp.concatenate(pieces[:cut], axis=dim), jnp.concatenate(pieces[cut:], axis=dim)]


def bit_of(axis, bit):
    return (lax.axis_index(axis) // bit) % 2 == 1


def scatter_step(pieces, axis, bit):
    mine = bit_of(axis, bit)
    out = []
    for p in pieces:
        cut = p.shape[0] // 2
        lo, hi = p[:cut], p[cut:]
        got = swap(jnp.where(mine, lo, hi), axis, bit)
        out.append((jnp.where(mine, hi, lo).astype(F32) + got.astype(F32)).astype(BF16))
    return out


def gather_step(p, axis, bit):
    mine = bit_of(axis, bit)
    got = swap(p, axis, bit)
    return jnp.concatenate([jnp.where(mine, got, p), jnp.where(mine, p, got)], axis=0)


def reduce_pieces(pieces, wide, narrow):
    count = lax.axis_size(wide)
    if count > 1:
        pieces = scatter_step(pieces, wide, 1)
    bit = lax.axis_size(narrow) // 2
    while bit >= 1:
        got = [swap(p, narrow, bit) for p in pieces[bit:]]
        pieces = [(a.astype(F32) + b.astype(F32)).astype(BF16) for a, b in zip(pieces[:bit], got)]
        bit //= 2
    bits = []
    bit = 2
    while bit < count:
        bits.append(bit)
        bit *= 2
    for bit in bits:
        pieces = scatter_step(pieces, wide, bit)
    total = pieces[0]
    for bit in reversed(bits):
        total = gather_step(total, wide, bit)
    if count > 1:
        total = gather_step(total, wide, 1)
    return total


def rows512(a):
    cols = a.shape[1]
    if cols < 512:
        return a.reshape(-1, 512)
    return jnp.concatenate([a[:, j : j + 512] for j in range(0, cols, 512)], axis=0)


def unrows512(a, rows, cols):
    if cols < 512:
        return a.reshape(rows, cols)
    return jnp.concatenate([a[j * rows : (j + 1) * rows] for j in range(cols // 512)], axis=1)


def local(
    inputs, segment_ids, norm1_gain, norm1_shift, w_qkv, w_out,
    norm2_gain, norm2_shift, w_up, w_down, cotangent,
):
    feats, samp, width = inputs.shape
    tokens = feats * samp
    blocks = lax.axis_size("narrow")
    group = max(g for g in (1, 2, 4) if feats % g == 0)
    steps = feats // group
    rows = group * samp
    head_cols = w_qkv.shape[2]

    x_prev, x_next = halo(inputs, "wide")
    qkv_halves = [
        h.reshape(width, 3 * h.shape[2]) for h in two_halves(gather_pieces(w_qkv, "narrow"), 2)
    ]
    out_halves = two_halves(gather_pieces(w_out, "narrow"), 0)
    up_halves = two_halves(gather_pieces(w_up, "narrow"), 1)
    down_halves = two_halves(gather_pieces(w_down, "narrow"), 0)

    id_rim = jnp.full((samp,), -1, jnp.int32)
    padded_ids = jnp.concatenate([id_rim, segment_ids, id_rim])
    window_ids = lax.dynamic_slice_in_dim(
        padded_ids, lax.axis_index("wide") * samp, 3 * samp, 0
    )
    id_col = window_ids[:, None]
    id_row = jnp.tile(window_ids.reshape(3, samp), (1, HEADS_PER_GROUP))
    gain1, shift1 = norm1_gain[None, :], norm1_shift[None, :]
    gain2, shift2 = norm2_gain[None, :], norm2_shift[None, :]

    def whole(a):
        return pl.BlockSpec(a.shape, lambda i: (0,) * a.ndim, pipeline_mode=pl.Buffered(1))

    cube = pl.BlockSpec((group, samp, width), lambda i: (i, 0, 0))
    flat = pl.BlockSpec((rows, width), lambda i: (i, 0))
    line = pl.BlockSpec((1, width), lambda i: (0, 0))
    qkv_block = pl.BlockSpec((2, 3, rows, 3 * GROUP_COLS), lambda i: (0, 0, i, 0))

    qkv, attended = pl.pallas_call(
        attn_fwd_kernel,
        grid=(steps,),
        in_specs=[whole(id_col), whole(id_row), cube, cube, cube]
        + [whole(a) for a in (*qkv_halves, gain1, shift1)],
        out_specs=[qkv_block, cube],
        out_shape=[
            jax.ShapeDtypeStruct((2, 3, tokens, 3 * GROUP_COLS), BF16),
            jax.ShapeDtypeStruct((feats, samp, width), BF16),
        ],
        name="attn_fwd",
    )(id_col, id_row, x_prev, inputs, x_next, *qkv_halves, gain1, shift1)

    att_flat = attended.reshape(tokens, width)
    x_flat = inputs.reshape(tokens, width)
    cot_flat = cotangent.reshape(tokens, width)
    half_ff = up_halves[0].shape[1]
    wide_block = pl.BlockSpec((2, rows, half_ff), lambda i: (0, i, 0))
    chain_args = (*out_halves, up_halves[0], up_halves[1], down_halves[0], down_halves[1], gain2, shift2)
    tok = lambda dtype: jax.ShapeDtypeStruct((tokens, width), dtype)
    vec = jax.ShapeDtypeStruct((1, width), F32)
    block_out, normed_two, activated, pre_grad, hidden_grad, residual, dattended, gain2_grad, shift2_grad = pl.pallas_call(
        chain_kernel,
        grid=(steps,),
        in_specs=[flat, flat, flat] + [whole(a) for a in chain_args],
        out_specs=[flat, flat, wide_block, wide_block, flat, flat, flat, line, line],
        out_shape=[
            tok(BF16), tok(BF16),
            jax.ShapeDtypeStruct((2, tokens, half_ff), BF16),
            jax.ShapeDtypeStruct((2, tokens, half_ff), BF16),
            tok(F32), tok(BF16), tok(BF16), vec, vec,
        ],
        name="chain",
    )(x_flat, att_flat, cot_flat, *chain_args)

    datt = dattended.reshape(feats, samp, width)
    d_prev, d_next = halo(datt, "wide")

    def pieces_of(a, dim):
        per = blocks // 2
        size = a[0].shape[dim] // per
        return [lax.slice_in_dim(h, j * size, (j + 1) * size, axis=dim) for h in a for j in range(per)]

    up_grads = pieces_of([dot_tn(normed_two, pre_grad[h]).astype(BF16) for h in range(2)], 1)
    down_grads = pieces_of([dot_tn(activated[h], cot_flat).astype(BF16) for h in range(2)], 0)
    half = width // 2
    out_grads = pieces_of(
        [dot_tn(att_flat[:, h * half : (h + 1) * half], residual).astype(BF16) for h in range(2)], 0
    )
    packs = [
        jnp.concatenate([rows512(u), d, o], axis=0)
        for u, d, o in zip(up_grads, down_grads, out_grads)
    ]
    pack = reduce_pieces(packs, "wide", "narrow")
    up_rows = rows512(jnp.zeros(w_up.shape, BF16)).shape[0]
    down_rows = w_down.shape[0]
    up_grad = unrows512(pack[:up_rows], *w_up.shape).astype(F32)
    down_grad = pack[up_rows : up_rows + down_rows].astype(F32)
    out_grad = pack[up_rows + down_rows :].astype(F32)

    input_grad, qkv_grads, gain1_grad, shift1_grad = pl.pallas_call(
        attn_bwd_kernel,
        grid=(steps,),
        in_specs=[whole(id_col), whole(id_row), cube, qkv_block, cube, cube, cube, flat]
        + [whole(a) for a in (*qkv_halves, gain1, shift1)],
        out_specs=[
            flat,
            pl.BlockSpec((2, width, 3 * GROUP_COLS), lambda i: (0, 0, 0)),
            line,
            line,
        ],
        out_shape=[
            tok(F32),
            jax.ShapeDtypeStruct((2, width, 3 * GROUP_COLS), BF16),
            vec,
            vec,
        ],
        scratch_shapes=[
            pltpu.VMEM((2, width, 3 * GROUP_COLS), F32),
            pltpu.VMEM((2, rows, 3 * GROUP_COLS), BF16),
        ],
        name="attn_bwd",
    )(id_col, id_row, inputs, qkv, d_prev, datt, d_next, hidden_grad, *qkv_halves, gain1, shift1)

    if blocks == 2:
        qkv_pieces = [qkv_grads[0], qkv_grads[1]]
    else:
        qkv_pieces = [
            p.reshape(width, 3 * head_cols)
            for p in pieces_of([qkv_grads[h].reshape(width, 3, GROUP_COLS) for h in range(2)], 2)
        ]
    qkv_grad = reduce_pieces(qkv_pieces, "wide", "narrow").reshape(width, 3, head_cols).astype(F32)
    norm_sums = jnp.concatenate([gain1_grad, shift1_grad, gain2_grad, shift2_grad], axis=0)
    for axis in ("wide", "narrow"):
        bit = 1
        while bit < lax.axis_size(axis):
            norm_sums = norm_sums + swap(norm_sums, axis, bit)
            bit *= 2
    return (
        block_out.reshape(feats, samp, width),
        input_grad.reshape(feats, samp, width),
        norm_sums[0],
        norm_sums[1],
        qkv_grad,
        out_grad,
        norm_sums[2],
        norm_sums[3],
        up_grad,
        down_grad,
    )


def solution(mesh):
    rows = P("narrow", "wide", None)
    placed = (
        rows, P(), P(), P(), P(None, None, "narrow"), P("narrow", None),
        P(), P(), P(None, "narrow"), P("narrow", None), rows,
    )
    outs = (
        rows, rows, P(), P(), P(None, None, "narrow"), P("narrow", None),
        P(), P(), P(None, "narrow"), P("narrow", None),
    )
    return jax.shard_map(local, mesh=mesh, in_specs=placed, out_specs=outs, check_vma=False)
```

```python
import functools

import jax
import jax.numpy as jnp
import numpy as np
from jax import lax
from jax.experimental import pallas as pl
from jax.experimental.pallas import tpu as pltpu
from jax.sharding import PartitionSpec as P

HEAD_DIM = 64
HEADS_PER_GROUP = 4
GROUP_COLS = HEAD_DIM * HEADS_PER_GROUP
EPS = 1e-05
SCALE = HEAD_DIM ** (-0.5)
F32 = jnp.float32
BF16 = jnp.bfloat16
NEG = -1e30
CHUNK = 256


def dot_nn(a, b):
    return lax.dot_general(a, b, (((1,), (0,)), ((), ())), preferred_element_type=F32)


def dot_nt(a, b):
    return lax.dot_general(a, b, (((1,), (1,)), ((), ())), preferred_element_type=F32)


def dot_tn(a, b):
    return lax.dot_general(a, b, (((0,), (0,)), ((), ())), preferred_element_type=F32)


def norm_parts(z):
    mean = jnp.mean(z, axis=-1, keepdims=True)
    centred = z - mean
    var = jnp.mean(centred * centred, axis=-1, keepdims=True)
    rstd = lax.rsqrt(var + EPS)
    return centred * rstd, rstd


def norm_back(grad, xhat, rstd, gain):
    gg = grad * gain
    m1 = jnp.mean(gg, axis=-1, keepdims=True)
    m2 = jnp.mean(gg * xhat, axis=-1, keepdims=True)
    return rstd * (gg - m1 - xhat * m2)


def lane_head(rows, dtype):
    lane = lax.broadcasted_iota(jnp.int32, (rows, GROUP_COLS), 1)
    return [
        ((lane >= h * HEAD_DIM) & (lane < (h + 1) * HEAD_DIM)).astype(F32).astype(dtype)
        for h in range(HEADS_PER_GROUP)
    ]


def block_diag(rows, masks):
    return jnp.concatenate([rows * m for m in masks], axis=0)


def pick_heads(full, masks, rows):
    out = full[0:rows] * masks[0]
    for h in range(1, HEADS_PER_GROUP):
        out = out + full[h * rows : (h + 1) * rows] * masks[h]
    return out


def rows_at(index, size):
    return pl.ds(pl.multiple_of(index * size, size), size)


def each(count, body, unroll=1):
    lax.fori_loop(0, count, lambda i, carry: (body(i), carry)[1], 0, unroll=unroll)


def attn_fwd_kernel(idc, idr, xp, xo, xn, w0, w1, gain, shift, *rest):
    qkv_ref, att_ref = rest[-2:]
    feats, samp, width = xo.shape
    rows = feats * samp
    x = jnp.concatenate(
        [xp[...].reshape(rows, width), xo[...].reshape(rows, width), xn[...].reshape(rows, width)],
        axis=0,
    ).astype(F32)
    xhat, _ = norm_parts(x)
    normed = (xhat * gain[...] + shift[...]).astype(BF16)
    for hg, w in enumerate((w0, w1)):
        qkv = dot_nn(normed, w[...]).astype(BF16)
        qkv_ref[hg] = qkv.reshape(3, rows, 3 * GROUP_COLS)
    allowed = idc[...] == idr[1:2, :]
    m16 = lane_head(1, BF16)
    m32 = lane_head(1, F32)

    def column(f):
        sl = rows_at(f, samp)
        for hg in range(2):
            q = qkv_ref[hg, 1, sl, 0:GROUP_COLS]
            k = jnp.concatenate(
                [qkv_ref[hg, w, sl, GROUP_COLS : 2 * GROUP_COLS] for w in range(3)], axis=0
            )
            v = jnp.concatenate(
                [qkv_ref[hg, w, sl, 2 * GROUP_COLS : 3 * GROUP_COLS] for w in range(3)], axis=0
            )
            s = dot_nt(k, block_diag(q, m16)) * SCALE
            s = jnp.where(allowed, s, NEG)
            top = jnp.max(s, axis=0, keepdims=True)
            e = jnp.exp(s - top)
            total = jnp.sum(e, axis=0, keepdims=True)
            p = (e * (1.0 / total)).astype(BF16)
            o = pick_heads(dot_tn(p, v), m32, samp)
            att_ref[f, :, hg * GROUP_COLS : (hg + 1) * GROUP_COLS] = o.astype(BF16)

    each(feats, column, 2)


def phi_parts(u):
    e = jnp.exp(-0.5 * (u * u))
    t = 1.0 / (1.0 + (0.3275911 * 0.7071067811865476) * jnp.abs(u))
    poly = t * (
        0.127414796
        + t * (-0.142248368 + t * (0.7107068705 + t * (-0.7265760135 + t * 0.5307027145)))
    )
    tail = poly * e
    cdf = jnp.where(u < 0, tail, 1.0 - tail)
    return cdf, u * (e * 0.3989422804014327)


def chain_kernel(others, inpack, ordered, *refs):
    table, x, att, cot, gain, shift, up_own, down_own, out_own = refs[:9]
    refs = refs[9:]
    packs, refs = refs[: 2 * others], refs[2 * others :]
    if inpack:
        extra = packs
    else:
        extra, refs = refs[: 2 * others], refs[2 * others :]
    count = 2 if ordered else 3
    out_ref, hgrad_ref, dat_ref, g2_ref, s2_ref = refs[:5]
    packed, refs = refs[5 : 5 + count], refs[5 + count :]
    (wo, upb, downb, hidden, normed, mlp, dn2, act, pre, res, gd, gu, go) = refs
    tokens, width = x.shape
    slot = upb.shape[1]
    narrow_rows = out_own.shape[0]
    half_rows = narrow_rows // 2
    chunks = tokens // CHUNK
    step = pl.program_id(0)
    core = table[0]

    def bases(unit):
        for j in range(1, others + 1):
            yield 2 * j - 2, 2 * j + core
            yield 2 * j - 1, 2 * j + 1 - core

    @pl.when(step == 0)
    def _():
        wo[:narrow_rows] = out_own[...]
        for i, base in bases(half_rows):
            wo[rows_at(base, half_rows)] = packs[i][2 * slot : 2 * slot + half_rows] if inpack else packs[i][slot : slot + half_rows]
        g2_ref[...] = jnp.zeros_like(g2_ref)
        s2_ref[...] = jnp.zeros_like(s2_ref)

        def start(i):
            sl = rows_at(i, CHUNK)
            h = x[sl].astype(F32) + dot_nn(att[sl], wo[...])
            hidden[sl] = h
            xhat, _ = norm_parts(h)
            normed[sl] = (xhat * gain[...] + shift[...]).astype(BF16)
            mlp[sl] = jnp.zeros((CHUNK, width), F32)
            dn2[sl] = jnp.zeros((CHUNK, width), F32)

        each(chunks, start)

    for i in range(2 * others + 2):

        @pl.when(step == i)
        def _(i=i):
            if i < 2:
                upb[...] = up_own[:, i * slot : (i + 1) * slot]
                downb[...] = down_own[i * slot : (i + 1) * slot]
            elif inpack:
                upb[...] = packs[i - 2][:slot]
                downb[...] = packs[i - 2][slot : 2 * slot]
            else:
                upb[...] = extra[i - 2][...]
                downb[...] = packs[i - 2][:slot]

    def tokens_of(i):
        sl = rows_at(i, CHUNK)
        u = dot_nn(normed[sl], upb[...])
        cdf, upd = phi_parts(u)
        a = (u * cdf).astype(BF16)
        act[sl] = a
        p = (dot_nt(cot[sl], downb[...]) * (cdf + upd)).astype(BF16)
        pre[sl] = p
        mlp[sl] += dot_nn(a, downb[...])
        dn2[sl] += dot_nt(p, upb[...])

    each(chunks, tokens_of)
    swapped = jnp.where(step % 2 == 0, core, 1 - core)
    base = jnp.where(step < 2, step, step - step % 2 + swapped)
    at = rows_at(base, slot)
    gd[at] = dot_tn(act[...], cot[...]).astype(BF16)
    gu[at] = dot_tn(pre[...], normed[...]).astype(BF16)

    @pl.when(step == 2 * others + 1)
    def _():
        def finish(i):
            sl = rows_at(i, CHUNK)
            h = hidden[sl]
            out_ref[sl] = (h + mlp[sl]).astype(BF16)
            xhat, rstd = norm_parts(h)
            d = dn2[sl]
            g2_ref[...] += jnp.sum(d * xhat, axis=0, keepdims=True)
            s2_ref[...] += jnp.sum(d, axis=0, keepdims=True)
            hgrad = cot[sl].astype(F32) + norm_back(d, xhat, rstd, gain[...])
            hgrad_ref[sl] = hgrad
            r = hgrad.astype(BF16)
            res[sl] = r
            dat_ref[sl] = dot_nt(r, wo[...]).astype(BF16)

        each(chunks, finish)
        go[...] = dot_tn(att[...], res[...]).astype(BF16)
        if ordered:
            blocks = (table.shape[0] - 1) // 2
            n_ff = gd.shape[0] // (2 * blocks)
            n_out = go.shape[0] // (2 * blocks)
            size = 2 * n_ff + n_out
            for side in range(2):
                for b in range(blocks):
                    src = table[1 + side * blocks + b]
                    ref = packed[side]
                    ref[b * size : b * size + n_ff] = gd[rows_at(src, n_ff)]
                    ref[b * size + n_ff : b * size + 2 * n_ff] = gu[rows_at(src, n_ff)]
                    ref[b * size + 2 * n_ff : (b + 1) * size] = go[rows_at(src, n_out)]
        else:
            packed[0][...] = gd[...]
            packed[1][...] = gu[...]
            packed[2][...] = go[...]


def attn_bwd_kernel(idc, idr, qkv_ref, dp_ref, do_ref, dn_ref, *rest):
    dqkv = rest[-1]
    feats, samp, width = do_ref.shape
    m16 = lane_head(1, BF16)
    m32 = lane_head(1, F32)
    spans = ((0, 2), (0, 3), (1, 3))
    masks = [idc[a * samp : b * samp, :] == idr[g : g + 1, :] for g, (a, b) in enumerate(spans)]
    grads = (dp_ref, do_ref, dn_ref)

    def column(f):
        sl = rows_at(f, samp)
        for hg in range(2):
            cols = slice(hg * GROUP_COLS, (hg + 1) * GROUP_COLS)
            k = jnp.concatenate(
                [qkv_ref[hg, w, sl, GROUP_COLS : 2 * GROUP_COLS] for w in range(3)], axis=0
            )
            v = jnp.concatenate(
                [qkv_ref[hg, w, sl, 2 * GROUP_COLS : 3 * GROUP_COLS] for w in range(3)], axis=0
            )
            dk = jnp.zeros((samp, GROUP_COLS), F32)
            dv = jnp.zeros((samp, GROUP_COLS), F32)
            for g, (a, b) in enumerate(spans):
                ks = k[a * samp : b * samp]
                vs = v[a * samp : b * samp]
                qbd = block_diag(qkv_ref[hg, g, sl, 0:GROUP_COLS], m16)
                dbd = block_diag(grads[g][f, :, cols], m16)
                s = dot_nt(ks, qbd) * SCALE
                s = jnp.where(masks[g], s, NEG)
                top = jnp.max(s, axis=0, keepdims=True)
                e = jnp.exp(s - top)
                total = jnp.sum(e, axis=0, keepdims=True)
                p = e * (1.0 / total)
                dp = dot_nt(vs, dbd)
                pd = p * dp
                delta = jnp.sum(pd, axis=0, keepdims=True)
                ds = (pd - p * delta).astype(BF16)
                own = slice((1 - a) * samp, (2 - a) * samp)
                dk = dk + dot_nn(ds[own], qbd)
                dv = dv + dot_nn(p[own].astype(BF16), dbd)
                if g == 1:
                    dq = pick_heads(dot_tn(ds, ks), m32, samp)
            dqkv[hg, sl, 0:GROUP_COLS] = (dq * SCALE).astype(BF16)
            dqkv[hg, sl, GROUP_COLS : 2 * GROUP_COLS] = (dk * SCALE).astype(BF16)
            dqkv[hg, sl, 2 * GROUP_COLS : 3 * GROUP_COLS] = dv.astype(BF16)

    each(feats, column, 2)


def qkv_grad_kernel(ordered, table, x, dqkv, gain, shift, *refs):
    normed, gq = refs[-2:]
    outs = refs[:-2]
    tokens, width = x.shape

    def start(i):
        sl = rows_at(i, CHUNK)
        xhat, _ = norm_parts(x[sl].astype(F32))
        normed[sl] = (xhat * gain[...] + shift[...]).astype(BF16)

    each(tokens // CHUNK, start)
    cols = dqkv.shape[2]
    for hg in range(2):
        gq[hg * cols : (hg + 1) * cols] = dot_tn(dqkv[hg], normed[...]).astype(BF16)
    if ordered:
        blocks = (table.shape[0] - 1) // 2
        size = gq.shape[0] // (2 * blocks)
        for side in range(2):
            for b in range(blocks):
                outs[side][b * size : (b + 1) * size] = gq[rows_at(table[1 + side * blocks + b], size)]
    else:
        outs[0][...] = gq[...]


def input_grad_kernel(x, hgrad, dqkv, w0, w1, gain, igrad_ref, g1_ref, s1_ref):
    xhat, rstd = norm_parts(x[...].astype(F32))
    dn1 = dot_nt(dqkv[0], w0[...]) + dot_nt(dqkv[1], w1[...])

    @pl.when(pl.program_id(0) == 0)
    def _():
        g1_ref[...] = jnp.zeros_like(g1_ref)
        s1_ref[...] = jnp.zeros_like(s1_ref)

    g1_ref[...] += jnp.sum(dn1 * xhat, axis=0, keepdims=True)
    s1_ref[...] += jnp.sum(dn1, axis=0, keepdims=True)
    igrad_ref[...] = hgrad[...] + norm_back(dn1, xhat, rstd, gain[...])


def ffn_out_kernel(n_ff, n_out, table, mine, got, up_ref, down_ref, out_ref, turned):
    size = 2 * n_ff + n_out
    blocks = mine.shape[0] // size
    for side, ref in enumerate((mine, got)):
        for b in range(blocks):
            to = table[side * blocks + b]
            down_ref[rows_at(to, n_ff)] = ref[b * size : b * size + n_ff].astype(F32)
            turned[rows_at(to, n_ff)] = ref[b * size + n_ff : b * size + 2 * n_ff].astype(F32)
            out_ref[rows_at(to, n_out)] = ref[b * size + 2 * n_ff : (b + 1) * size].astype(F32)
    up_ref[...] = turned[...].T


def qkv_out_kernel(table, mine, got, out_ref, turned):
    blocks = table.shape[0] // 2
    size = mine.shape[0] // blocks
    for side, ref in enumerate((mine, got)):
        for b in range(blocks):
            turned[rows_at(table[side * blocks + b], size)] = ref[b * size : (b + 1) * size].astype(F32)
    out_ref[...] = turned[...].T


def swap(x, axis, bit):
    count = lax.axis_size(axis)
    return lax.ppermute(x, axis, [(i, i ^ bit) for i in range(count)])


def halo(x, axis):
    count = lax.axis_size(axis)
    prev = lax.ppermute(x, axis, [(i, i + 1) for i in range(count - 1)])
    nxt = lax.ppermute(x, axis, [(i + 1, i) for i in range(count - 1)])
    return prev, nxt


def gather_pieces(x, axis):
    pieces = [x]
    bit = 1
    while bit < lax.axis_size(axis):
        pieces = pieces + [swap(p, axis, bit) for p in pieces]
        bit *= 2
    return pieces


def tied(*arrays):
    return lax.optimization_barrier(arrays)


class Plan:

    def __init__(self, wide, narrow):
        self.wide, self.narrow = wide, narrow
        nb = [("narrow", 1 << i) for i in range(narrow.bit_length() - 1)][::-1]
        wb = [("wide", 1 << i) for i in range(1, wide.bit_length() - 1)]
        first = nb + wb
        second = wb[1:2] + nb + wb[:1] + wb[2:]
        self.orders = (first, second)
        self.steps = len(first)
        self.blocks = 1 << self.steps
        self.back = [[s for s in o if s[0] == "wide"][::-1] for o in self.orders]
        self.me = lax.axis_index("wide")
        self.core = self.me % 2

    def rel(self, order):
        j = np.zeros(self.blocks, np.int32)
        r = np.zeros(self.blocks, np.int32)
        for s, (axis, bit) in enumerate(order):
            has = (np.arange(self.blocks) >> (self.steps - 1 - s)) & 1
            if axis == "narrow":
                j += has * bit
            else:
                r += has * bit
        return j, r

    def by_core(self, a, b):
        return jnp.where(self.core == 0, jnp.asarray(a, jnp.int32), jnp.asarray(b, jnp.int32))

    def sources(self):
        (j0, r0), (j1, r1) = (self.rel(o) for o in self.orders)
        high = self.me - self.core
        n0, n1 = j0 * self.wide, j1 * self.wide
        mine = self.by_core(n0, n1) + (self.by_core(r0, r1) ^ high) + self.core
        send = self.by_core(n1, n0) + (self.by_core(r1, r0) ^ high) + 1 - self.core
        return jnp.concatenate([self.core[None], mine, send]).astype(jnp.int32)

    def targets(self):
        rels = []
        for o in self.orders:
            j, r = self.rel(o)
            rels.append(r[j == 0])
        high = self.me - self.core
        mine = (self.by_core(rels[0], rels[1]) ^ high) + self.core
        got = (self.by_core(rels[1], rels[0]) ^ high) + 1 - self.core
        return jnp.concatenate([mine, got]).astype(jnp.int32)

    def mixed(self, x, steps):
        pairs = []
        for w in range(self.wide):
            axis, bit = steps[w % 2]
            for n in range(self.narrow):
                to = (w, n ^ bit) if axis == "narrow" else (w ^ bit, n)
                pairs.append((w * self.narrow + n, to[0] * self.narrow + to[1]))
        return lax.ppermute(x, ("wide", "narrow"), pairs)


class Reduction:

    def __init__(self, plan, mine, send):
        self.plan, self.parts, self.operand, self.at = plan, [mine], send, 0
        self.rows = mine.shape[0]

    def total(self, low, high):
        out = self.parts[0][low:high].astype(F32)
        for p in self.parts[1:]:
            out = out + p[low:high].astype(F32)
        return out.astype(BF16)

    def advance(self):
        plan, at = self.plan, self.at
        back = len(plan.back[0])
        if at == 0:
            got = swap(self.operand, "wide", 1)
        elif at <= plan.steps:
            got = plan.mixed(self.operand, [o[at - 1] for o in plan.orders])
        elif at <= plan.steps + back:
            got = plan.mixed(self.operand, [o[at - plan.steps - 1] for o in plan.back])
        else:
            got = swap(self.operand, "wide", 1)
        self.at = at + 1
        if at <= plan.steps:
            self.parts.append(got)
            if at == plan.steps:
                self.operand = self.total(0, self.rows >> at)
            else:
                self.operand = self.total(self.rows >> (at + 1), self.rows >> at)
        elif at <= plan.steps + back:
            self.operand = jnp.concatenate([self.operand, got], axis=0)
        else:
            self.result = (self.operand, got)

    @property
    def left(self):
        return self.plan.steps + len(self.plan.back[0]) + 2 - self.at


def lockstep(*chains):
    live = [c for c in chains if c.left > 0]
    if len(live) > 1:
        for c, o in zip(live, tied(*[c.operand for c in live])):
            c.operand = o
    for c in live:
        c.advance()


class SmallSum:
    def __init__(self, value):
        self.operand = value
        self.bits = [(a, 1 << i) for a in ("wide", "narrow") for i in range(lax.axis_size(a).bit_length() - 1)]

    def advance(self):
        self.operand = self.operand + swap(self.operand, *self.bits.pop(0))

    @property
    def left(self):
        return len(self.bits)


def local(
    inputs, segment_ids, norm1_gain, norm1_shift, w_qkv, w_out,
    norm2_gain, norm2_shift, w_up, w_down, cotangent,
):
    feats, samp, width = inputs.shape
    tokens = feats * samp
    narrow = lax.axis_size("narrow")
    wide = lax.axis_size("wide")
    plan = Plan(wide, narrow)
    core = plan.core
    part = feats // 2
    group = max(g for g in (1, 2, 4) if part % g == 0)
    steps = part // group
    rows = group * samp
    head_cols = w_qkv.shape[2]
    own_ff = w_up.shape[1]
    slot = own_ff // 2
    ff = own_ff * narrow
    inpack = slot == 512
    n_ff, n_out, n_qkv = own_ff // wide, w_out.shape[0] // wide, 3 * head_cols // wide
    ordered = narrow == 2 and n_ff % 16 == 0 and n_out % 16 == 0 and n_qkv % 16 == 0
    blocks = plan.blocks

    def core_half(a, axis):
        size = a.shape[axis] // 2
        return lax.dynamic_slice_in_dim(a, core * size, size, axis)

    halves_in = [inputs[:part], inputs[part:]]
    qkv_mine = gather_pieces(core_half(w_qkv.reshape(width, 3 * head_cols), 0), "narrow")[1:]
    prev0, next0 = halo(halves_in[0], "wide")
    up_half = core_half(w_up, 1)
    small = jnp.concatenate(
        [up_half.reshape(-1, 512), core_half(w_down, 0), core_half(w_out, 0)], axis=0
    )
    held = tied(small, *qkv_mine)
    small, qkv_mine = held[0], list(held[1:])
    pack_mine = gather_pieces(small, "narrow")[1:]
    qkv_got = [swap(p, "wide", 1) for p in qkv_mine]
    late, prev0, next0 = tied(halves_in[1], prev0, next0)
    prev1, next1 = halo(late, "wide")

    def whole_of(mine, got):
        first = jnp.where(core == 0, mine, got)
        second = jnp.where(core == 0, got, mine)
        return jnp.concatenate([first, second], axis=0)

    pieces = [w_qkv] + [
        whole_of(m, g).reshape(width, 3, head_cols) for m, g in zip(qkv_mine, qkv_got)
    ]
    cut = narrow // 2
    w0, w1 = (
        (p[0] if len(p) == 1 else jnp.concatenate(p, axis=2)).reshape(width, 3 * GROUP_COLS)
        for p in (pieces[:cut], pieces[cut:])
    )

    id_rim = jnp.full((samp,), -1, jnp.int32)
    padded_ids = jnp.concatenate([id_rim, segment_ids, id_rim])
    window_ids = lax.dynamic_slice_in_dim(padded_ids, plan.me * samp, 3 * samp, 0)
    id_col = window_ids[:, None]
    id_row = jnp.tile(window_ids.reshape(3, samp), (1, HEADS_PER_GROUP))
    gain1, shift1 = norm1_gain[None, :], norm1_shift[None, :]
    gain2, shift2 = norm2_gain[None, :], norm2_shift[None, :]
    sources, targets = plan.sources(), plan.targets()

    def whole(a):
        return pl.BlockSpec(a.shape, lambda i: (0,) * a.ndim, pipeline_mode=pl.Buffered(1))

    def cube(offset):
        return pl.BlockSpec((group, samp, width), lambda i: (i + offset, 0, 0))

    smem = pl.BlockSpec(memory_space=pltpu.SMEM)
    anywhere = pl.BlockSpec(memory_space=pl.ANY)
    line = pl.BlockSpec((1, width), lambda i: (0, 0))
    vec = jax.ShapeDtypeStruct((1, width), F32)

    def tok(dtype):
        return jax.ShapeDtypeStruct((tokens, width), dtype)

    def cost(flops, size):
        return pl.CostEstimate(flops=flops, bytes_accessed=size, transcendentals=0)

    def qkv_block(offset):
        return pl.BlockSpec((2, 3, rows, 3 * GROUP_COLS), lambda i: (0, 0, i + offset, 0))

    done = None
    for h, (before, after) in enumerate(((prev0, next0), (prev1, next1))):
        off = h * steps
        args = [id_col, id_row, before, inputs, after, w0, w1, gain1, shift1]
        specs = [whole(id_col), whole(id_row), cube(0), cube(off), cube(0)]
        specs += [whole(a) for a in (w0, w1, gain1, shift1)]
        alias = {}
        if done is not None:
            alias = {len(args): 0, len(args) + 1: 1}
            args += done
            specs += [anywhere, anywhere]
        done = pl.pallas_call(
            attn_fwd_kernel,
            grid=(steps,),
            in_specs=specs,
            out_specs=[qkv_block(off), cube(off)],
            out_shape=[
                jax.ShapeDtypeStruct((2, 3, tokens, 3 * GROUP_COLS), BF16),
                jax.ShapeDtypeStruct((feats, samp, width), BF16),
            ],
            input_output_aliases=alias,
            cost_estimate=cost(6 * 10**9 // 2, 12 << 20),
            name=f"attn_fwd_{h}",
        )(*args)
        if h == 0:
            pack_mine = list(tied(done[1], *pack_mine))[1:]
            pack_got = [swap(p, "wide", 1) for p in pack_mine]
    qkv, attended = done

    x_flat = inputs.reshape(tokens, width)
    cot_flat = cotangent.reshape(tokens, width)
    att_flat = attended.reshape(tokens, width)
    packs = [a for pair in zip(pack_mine, pack_got) for a in pair]
    args = [sources, x_flat, att_flat, cot_flat, gain2, shift2, w_up, w_down, w_out]
    if inpack:
        args += packs
    else:
        up_rows = width * slot // 512
        args += [p[up_rows:] for p in packs]
        args += [p[:up_rows].reshape(width, slot) for p in packs]
    if ordered:
        size = blocks * (2 * n_ff + n_out)
        sums = [(size, 512)] * 2
    else:
        sums = [(ff, width), (ff, width), (width, width)]
    outs = [tok(BF16), tok(F32), tok(BF16), vec, vec]
    outs += [jax.ShapeDtypeStruct(s, BF16) for s in sums]
    scratch = [
        ((width, width), BF16), ((width, slot), BF16), ((slot, width), BF16),
        ((tokens, width), F32), ((tokens, width), BF16), ((tokens, width), F32), ((tokens, width), F32),
        ((tokens, slot), BF16), ((tokens, slot), BF16), ((tokens, width), BF16),
        ((ff, width), BF16), ((ff, width), BF16), ((width, width), BF16),
    ]
    block_out, hidden_grad, dattended, gain2_grad, shift2_grad, *packed = pl.pallas_call(
        functools.partial(chain_kernel, narrow - 1, inpack, ordered),
        grid=(2 * narrow,),
        in_specs=[smem] + [whole(a) for a in args[1:]],
        out_specs=[whole(o) for o in outs],
        out_shape=outs,
        scratch_shapes=[pltpu.VMEM(*s) for s in scratch],
        cost_estimate=cost(15 * 10**9, 20 << 20),
        name="chain",
    )(*args)

    def arranged(natural):
        flat = natural.reshape(narrow * wide, natural.shape[2], 512)
        places = sources[1:].reshape(2, blocks)
        return [jnp.take(flat, places[s], axis=0).reshape(-1, 512) for s in range(2)]

    if not ordered:
        down, up, out = (p.reshape(narrow, wide, -1, 512) for p in packed)
        packed = arranged(jnp.concatenate([down, up, out], axis=2))
    big = Reduction(plan, packed[0], packed[1])

    datt = dattended.reshape(feats, samp, width)
    around = [halo(datt[:part], "wide")]
    lockstep(big)
    first, *around[0] = tied(datt[part:], *around[0])
    around.append(halo(first, "wide"))
    dqkv = None
    for h in range(2):
        off = h * steps
        before, after = around[h]
        before, after, big.operand = tied(before, after, big.operand)
        args = [id_col, id_row, qkv, before, datt, after]
        specs = [whole(id_col), whole(id_row), qkv_block(off), cube(0), cube(off), cube(0)]
        alias = {}
        if dqkv is not None:
            alias = {len(args): 0}
            args.append(dqkv)
            specs.append(anywhere)
        lockstep(big)
        dqkv = pl.pallas_call(
            attn_bwd_kernel,
            grid=(steps,),
            in_specs=specs,
            out_specs=pl.BlockSpec((2, rows, 3 * GROUP_COLS), lambda i, off=off: (0, i + off, 0)),
            out_shape=jax.ShapeDtypeStruct((2, tokens, 3 * GROUP_COLS), BF16),
            input_output_aliases=alias,
            cost_estimate=cost(10 * 10**9, 12 << 20),
            name=f"attn_bwd_{h}",
        )(*args)
    dqkv, big.operand = tied(dqkv, big.operand)
    lockstep(big)

    natural = (6 * GROUP_COLS, width)
    outs = [jax.ShapeDtypeStruct((blocks * n_qkv, 512), BF16)] * 2
    if not ordered:
        outs = [jax.ShapeDtypeStruct(natural, BF16)]
    args = [sources, x_flat, dqkv, gain1, shift1]
    packed = pl.pallas_call(
        functools.partial(qkv_grad_kernel, ordered),
        grid=(1,),
        in_specs=[smem] + [whole(a) for a in args[1:]],
        out_specs=[whole(o) for o in outs],
        out_shape=outs,
        scratch_shapes=[pltpu.VMEM((tokens, width), BF16), pltpu.VMEM(natural, BF16)],
        cost_estimate=cost(2 * 10**9, 6 << 20),
        name="qkv_grad",
    )(*args)
    if not ordered:
        turned = packed[0].reshape(2, 3, narrow // 2, head_cols, width).transpose(0, 2, 1, 3, 4)
        packed = arranged(turned.reshape(narrow, wide, n_qkv, width))
    last = Reduction(plan, packed[0], packed[1])

    flat = pl.BlockSpec((CHUNK, width), lambda i: (i, 0))
    dqkv, last.operand = tied(dqkv, last.operand)
    input_grad, gain1_grad, shift1_grad = pl.pallas_call(
        input_grad_kernel,
        grid=(tokens // CHUNK,),
        in_specs=[flat, flat, pl.BlockSpec((2, CHUNK, 3 * GROUP_COLS), lambda i: (0, i, 0))]
        + [whole(a) for a in (w0, w1, gain1)],
        out_specs=[flat, line, line],
        out_shape=[tok(F32), vec, vec],
        cost_estimate=cost(2 * 10**9, 8 << 20),
        name="input_grad",
    )(x_flat, hidden_grad, dqkv, w0, w1, gain1)
    norms = SmallSum(jnp.concatenate([gain1_grad, shift1_grad, gain2_grad, shift2_grad], axis=0))

    lockstep(last, big)
    lockstep(last, big)
    while last.left > 0 or big.left > 0 or norms.left > 0:
        lockstep(last, big, norms)

    down_rows, out_rows, qkv_rows = own_ff, w_out.shape[0], 3 * head_cols
    if ordered:
        shapes = [jax.ShapeDtypeStruct(s, F32) for s in (w_up.shape, w_down.shape, w_out.shape)]
        up_grad, down_grad, out_grad = pl.pallas_call(
            functools.partial(ffn_out_kernel, n_ff, n_out),
            grid=(1,),
            in_specs=[smem] + [whole(a) for a in big.result],
            out_specs=[whole(s) for s in shapes],
            out_shape=shapes,
            scratch_shapes=[pltpu.VMEM((own_ff, width), F32)],
            cost_estimate=cost(0, 8 << 20),
            name="ffn_out",
        )(targets, *big.result)
        shape = jax.ShapeDtypeStruct((width, qkv_rows), F32)
        qkv_grad = pl.pallas_call(
            qkv_out_kernel,
            grid=(1,),
            in_specs=[smem] + [whole(a) for a in last.result],
            out_specs=whole(shape),
            out_shape=shape,
            scratch_shapes=[pltpu.VMEM((qkv_rows, width), F32)],
            cost_estimate=cost(0, 3 << 20),
            name="qkv_out",
        )(targets, *last.result)
    else:

        def natural_rows(pair, count):
            both = jnp.concatenate(pair, axis=0).reshape(wide, -1, 512)
            places = jnp.zeros((wide,), jnp.int32).at[targets].set(jnp.arange(wide, dtype=jnp.int32))
            return jnp.take(both, places, axis=0).astype(F32)

        full = natural_rows(big.result, wide)
        down_grad = full[:, :n_ff].reshape(w_down.shape)
        up_grad = full[:, n_ff : 2 * n_ff].reshape(own_ff, width).T
        out_grad = full[:, 2 * n_ff :].reshape(w_out.shape)
        qkv_grad = natural_rows(last.result, wide).reshape(qkv_rows, width).T
    norm_sums = norms.operand
    return (
        block_out.reshape(feats, samp, width),
        input_grad.reshape(feats, samp, width),
        norm_sums[0],
        norm_sums[1],
        qkv_grad.reshape(width, 3, head_cols),
        out_grad,
        norm_sums[2],
        norm_sums[3],
        up_grad,
        down_grad,
    )


def solution(mesh):
    rows = P("narrow", "wide", None)
    placed = (
        rows, P(), P(), P(), P(None, None, "narrow"), P("narrow", None),
        P(), P(), P(None, "narrow"), P("narrow", None), rows,
    )
    outs = (
        rows, rows, P(), P(), P(None, None, "narrow"), P("narrow", None),
        P(), P(), P(None, "narrow"), P("narrow", None),
    )
    return jax.shard_map(local, mesh=mesh, in_specs=placed, out_specs=outs, check_vma=False)
```

```python
import functools

import jax
import jax.numpy as jnp
import numpy as np
from jax import lax
from jax.experimental import pallas as pl
from jax.experimental.pallas import tpu as pltpu
from jax.sharding import PartitionSpec as P

HEAD_DIM = 64
HEADS_PER_GROUP = 4
GROUP_COLS = HEAD_DIM * HEADS_PER_GROUP
EPS = 1e-05
SCALE = HEAD_DIM ** (-0.5)
F32 = jnp.float32
BF16 = jnp.bfloat16
NEG = -1e30
CHUNK = 256
UNROLL = 4


def dot_nn(a, b):
    return lax.dot_general(a, b, (((1,), (0,)), ((), ())), preferred_element_type=F32)


def dot_nt(a, b):
    return lax.dot_general(a, b, (((1,), (1,)), ((), ())), preferred_element_type=F32)


def dot_tn(a, b):
    return lax.dot_general(a, b, (((0,), (0,)), ((), ())), preferred_element_type=F32)


def norm_parts(z):
    mean = jnp.mean(z, axis=-1, keepdims=True)
    centred = z - mean
    var = jnp.mean(centred * centred, axis=-1, keepdims=True)
    rstd = lax.rsqrt(var + EPS)
    return centred * rstd, rstd


def norm_back(grad, xhat, rstd, gain):
    gg = grad * gain
    m1 = jnp.mean(gg, axis=-1, keepdims=True)
    m2 = jnp.mean(gg * xhat, axis=-1, keepdims=True)
    return rstd * (gg - m1 - xhat * m2)


def lane_head(rows, dtype):
    lane = lax.broadcasted_iota(jnp.int32, (rows, GROUP_COLS), 1)
    return [
        ((lane >= h * HEAD_DIM) & (lane < (h + 1) * HEAD_DIM)).astype(F32).astype(dtype)
        for h in range(HEADS_PER_GROUP)
    ]


def block_diag(rows, masks):
    return jnp.concatenate([rows * m for m in masks], axis=0)


def pick_heads(full, masks, rows):
    out = full[0:rows] * masks[0]
    for h in range(1, HEADS_PER_GROUP):
        out = out + full[h * rows : (h + 1) * rows] * masks[h]
    return out


def rows_at(index, size):
    return pl.ds(pl.multiple_of(index * size, size), size)


def each(count, body, unroll=1):
    lax.fori_loop(0, count, lambda i, carry: (body(i), carry)[1], 0, unroll=unroll)


def attn_fwd_kernel(idc, idr, xp, xo, xn, w0, w1, gain, shift, *rest):
    qkv_ref, att_ref = rest[-2:]
    feats, samp, width = xo.shape
    rows = feats * samp
    x = jnp.concatenate(
        [xp[...].reshape(rows, width), xo[...].reshape(rows, width), xn[...].reshape(rows, width)],
        axis=0,
    ).astype(F32)
    xhat, _ = norm_parts(x)
    normed = (xhat * gain[...] + shift[...]).astype(BF16)
    for hg, w in enumerate((w0, w1)):
        qkv = dot_nn(normed, w[...]).astype(BF16)
        qkv_ref[hg] = qkv.reshape(3, rows, 3 * GROUP_COLS)
    allowed = idc[...] == idr[1:2, :]
    m16 = lane_head(1, BF16)
    m32 = lane_head(1, F32)

    def column(f):
        sl = rows_at(f, samp)
        for hg in range(2):
            q = qkv_ref[hg, 1, sl, 0:GROUP_COLS]
            k = jnp.concatenate(
                [qkv_ref[hg, w, sl, GROUP_COLS : 2 * GROUP_COLS] for w in range(3)], axis=0
            )
            v = jnp.concatenate(
                [qkv_ref[hg, w, sl, 2 * GROUP_COLS : 3 * GROUP_COLS] for w in range(3)], axis=0
            )
            s = dot_nt(k, block_diag(q, m16)) * SCALE
            s = jnp.where(allowed, s, NEG)
            top = jnp.max(s, axis=0, keepdims=True)
            e = jnp.exp(s - top)
            total = jnp.sum(e, axis=0, keepdims=True)
            p = (e * (1.0 / total)).astype(BF16)
            o = pick_heads(dot_tn(p, v), m32, samp)
            att_ref[f, :, hg * GROUP_COLS : (hg + 1) * GROUP_COLS] = o.astype(BF16)

    each(feats, column, UNROLL)


def phi_parts(u):
    e = jnp.exp(-0.5 * (u * u))
    t = 1.0 / (1.0 + (0.3275911 * 0.7071067811865476) * jnp.abs(u))
    poly = t * (
        0.127414796
        + t * (-0.142248368 + t * (0.7107068705 + t * (-0.7265760135 + t * 0.5307027145)))
    )
    tail = poly * e
    cdf = jnp.where(u < 0, tail, 1.0 - tail)
    return cdf, u * (e * 0.3989422804014327)


def chain_kernel(others, inpack, ordered, *refs):
    table, x, att, cot, gain, shift, up_own, down_own, out_own = refs[:9]
    refs = refs[9:]
    packs, refs = refs[: 2 * others], refs[2 * others :]
    if inpack:
        extra = packs
    else:
        extra, refs = refs[: 2 * others], refs[2 * others :]
    count = 2 if ordered else 3
    out_ref, hgrad_ref, dat_ref, g2_ref, s2_ref = refs[:5]
    packed, refs = refs[5 : 5 + count], refs[5 + count :]
    (wo, upb, downb, hidden, normed, mlp, dn2, act, pre, res, gd, gu, go) = refs
    tokens, width = x.shape
    slot = upb.shape[1]
    narrow_rows = out_own.shape[0]
    half_rows = narrow_rows // 2
    chunks = tokens // CHUNK
    step = pl.program_id(0)
    core = table[0]

    def bases(unit):
        for j in range(1, others + 1):
            yield 2 * j - 2, 2 * j + core
            yield 2 * j - 1, 2 * j + 1 - core

    @pl.when(step == 0)
    def _():
        wo[:narrow_rows] = out_own[...]
        for i, base in bases(half_rows):
            wo[rows_at(base, half_rows)] = packs[i][2 * slot : 2 * slot + half_rows] if inpack else packs[i][slot : slot + half_rows]
        g2_ref[...] = jnp.zeros_like(g2_ref)
        s2_ref[...] = jnp.zeros_like(s2_ref)

        def start(i):
            sl = rows_at(i, CHUNK)
            h = x[sl].astype(F32) + dot_nn(att[sl], wo[...])
            hidden[sl] = h
            xhat, _ = norm_parts(h)
            normed[sl] = (xhat * gain[...] + shift[...]).astype(BF16)
            mlp[sl] = jnp.zeros((CHUNK, width), F32)
            dn2[sl] = jnp.zeros((CHUNK, width), F32)

        each(chunks, start)

    for i in range(2 * others + 2):

        @pl.when(step == i)
        def _(i=i):
            if i < 2:
                upb[...] = up_own[:, i * slot : (i + 1) * slot]
                downb[...] = down_own[i * slot : (i + 1) * slot]
            elif inpack:
                upb[...] = packs[i - 2][:slot]
                downb[...] = packs[i - 2][slot : 2 * slot]
            else:
                upb[...] = extra[i - 2][...]
                downb[...] = packs[i - 2][:slot]

    def tokens_of(i):
        sl = rows_at(i, CHUNK)
        u = dot_nn(normed[sl], upb[...])
        cdf, upd = phi_parts(u)
        a = (u * cdf).astype(BF16)
        act[sl] = a
        p = (dot_nt(cot[sl], downb[...]) * (cdf + upd)).astype(BF16)
        pre[sl] = p
        mlp[sl] += dot_nn(a, downb[...])
        dn2[sl] += dot_nt(p, upb[...])

    each(chunks, tokens_of)
    swapped = jnp.where(step % 2 == 0, core, 1 - core)
    base = jnp.where(step < 2, step, step - step % 2 + swapped)
    at = rows_at(base, slot)
    gd[at] = dot_tn(act[...], cot[...]).astype(BF16)
    gu[at] = dot_tn(pre[...], normed[...]).astype(BF16)

    @pl.when(step == 2 * others + 1)
    def _():
        def finish(i):
            sl = rows_at(i, CHUNK)
            h = hidden[sl]
            out_ref[sl] = (h + mlp[sl]).astype(BF16)
            xhat, rstd = norm_parts(h)
            d = dn2[sl]
            g2_ref[...] += jnp.sum(d * xhat, axis=0, keepdims=True)
            s2_ref[...] += jnp.sum(d, axis=0, keepdims=True)
            hgrad = cot[sl].astype(F32) + norm_back(d, xhat, rstd, gain[...])
            hgrad_ref[sl] = hgrad
            r = hgrad.astype(BF16)
            res[sl] = r
            dat_ref[sl] = dot_nt(r, wo[...]).astype(BF16)

        each(chunks, finish)
        go[...] = dot_tn(att[...], res[...]).astype(BF16)
        if ordered:
            blocks = (table.shape[0] - 1) // 2
            n_ff = gd.shape[0] // (2 * blocks)
            n_out = go.shape[0] // (2 * blocks)
            size = 2 * n_ff + n_out
            for side in range(2):
                for b in range(blocks):
                    src = table[1 + side * blocks + b]
                    ref = packed[side]
                    ref[b * size : b * size + n_ff] = gd[rows_at(src, n_ff)]
                    ref[b * size + n_ff : b * size + 2 * n_ff] = gu[rows_at(src, n_ff)]
                    ref[b * size + 2 * n_ff : (b + 1) * size] = go[rows_at(src, n_out)]
        else:
            packed[0][...] = gd[...]
            packed[1][...] = gu[...]
            packed[2][...] = go[...]


def bwd_pieces(qkv_ref, hg, sl):
    k = jnp.concatenate(
        [qkv_ref[hg, w, sl, GROUP_COLS : 2 * GROUP_COLS] for w in range(3)], axis=0
    )
    v = jnp.concatenate(
        [qkv_ref[hg, w, sl, 2 * GROUP_COLS : 3 * GROUP_COLS] for w in range(3)], axis=0
    )
    return k, v


def score_grads(ks, vs, qbd, dbd, mask):
    s = dot_nt(ks, qbd) * SCALE
    s = jnp.where(mask, s, NEG)
    top = jnp.max(s, axis=0, keepdims=True)
    e = jnp.exp(s - top)
    total = jnp.sum(e, axis=0, keepdims=True)
    p = e * (1.0 / total)
    pd = p * dot_nt(vs, dbd)
    delta = jnp.sum(pd, axis=0, keepdims=True)
    return (pd - p * delta).astype(BF16), p


def attn_bwd_own_kernel(idc, idr, qkv_ref, do_ref, dq_ref, dkv_ref):
    feats, samp, width = do_ref.shape
    m16 = lane_head(1, BF16)
    m32 = lane_head(1, F32)
    mask = idc[...] == idr[1:2, :]

    def column(f):
        sl = rows_at(f, samp)
        for hg in range(2):
            k, v = bwd_pieces(qkv_ref, hg, sl)
            qbd = block_diag(qkv_ref[hg, 1, sl, 0:GROUP_COLS], m16)
            dbd = block_diag(do_ref[f, :, hg * GROUP_COLS : (hg + 1) * GROUP_COLS], m16)
            ds, p = score_grads(k, v, qbd, dbd, mask)
            dq = pick_heads(dot_tn(ds, k), m32, samp)
            dq_ref[hg, sl, :] = (dq * SCALE).astype(BF16)
            dkv_ref[hg, sl, 0:GROUP_COLS] = dot_nn(ds[samp : 2 * samp], qbd)
            dkv_ref[hg, sl, GROUP_COLS : 2 * GROUP_COLS] = dot_nn(p[samp : 2 * samp].astype(BF16), dbd)

    each(feats, column, UNROLL)


def attn_bwd_near_kernel(idc, idr, qkv_ref, dp_ref, dn_ref, sum_ref, dkv_ref):
    feats, samp, width = dp_ref.shape
    m16 = lane_head(1, BF16)
    near = ((0, 0, dp_ref), (2, 1, dn_ref))
    masks = [idc[a * samp : (a + 2) * samp, :] == idr[g : g + 1, :] for g, a, _ in near]

    def column(f):
        sl = rows_at(f, samp)
        for hg in range(2):
            k, v = bwd_pieces(qkv_ref, hg, sl)
            dk = sum_ref[hg, sl, 0:GROUP_COLS]
            dv = sum_ref[hg, sl, GROUP_COLS : 2 * GROUP_COLS]
            for mask, (g, a, ref) in zip(masks, near):
                span = slice(a * samp, (a + 2) * samp)
                qbd = block_diag(qkv_ref[hg, g, sl, 0:GROUP_COLS], m16)
                dbd = block_diag(ref[f, :, hg * GROUP_COLS : (hg + 1) * GROUP_COLS], m16)
                ds, p = score_grads(k[span], v[span], qbd, dbd, mask)
                own = slice((1 - a) * samp, (2 - a) * samp)
                dk = dk + dot_nn(ds[own], qbd)
                dv = dv + dot_nn(p[own].astype(BF16), dbd)
            dkv_ref[hg, sl, 0:GROUP_COLS] = (dk * SCALE).astype(BF16)
            dkv_ref[hg, sl, GROUP_COLS : 2 * GROUP_COLS] = dv.astype(BF16)

    each(feats, column, UNROLL)


def qkv_grad_kernel(ordered, table, x, dq, dkv, gain, shift, *refs):
    normed, gq = refs[-2:]
    outs = refs[:-2]
    tokens, width = x.shape

    def start(i):
        sl = rows_at(i, CHUNK)
        xhat, _ = norm_parts(x[sl].astype(F32))
        normed[sl] = (xhat * gain[...] + shift[...]).astype(BF16)

    each(tokens // CHUNK, start)
    for hg in range(2):
        low = 3 * hg * GROUP_COLS
        gq[low : low + GROUP_COLS] = dot_tn(dq[hg], normed[...]).astype(BF16)
        gq[low + GROUP_COLS : low + 3 * GROUP_COLS] = dot_tn(dkv[hg], normed[...]).astype(BF16)
    if ordered:
        blocks = (table.shape[0] - 1) // 2
        size = gq.shape[0] // (2 * blocks)
        for side in range(2):
            for b in range(blocks):
                outs[side][b * size : (b + 1) * size] = gq[rows_at(table[1 + side * blocks + b], size)]
    else:
        outs[0][...] = gq[...]


def input_grad_kernel(x, hgrad, dq, dkv, w0, w1, gain, igrad_ref, g1_ref, s1_ref):
    xhat, rstd = norm_parts(x[...].astype(F32))
    dn1 = dot_nt(dq[0], w0[:, :GROUP_COLS]) + dot_nt(dq[1], w1[:, :GROUP_COLS])
    dn1 = dn1 + dot_nt(dkv[0], w0[:, GROUP_COLS:]) + dot_nt(dkv[1], w1[:, GROUP_COLS:])

    @pl.when(pl.program_id(0) == 0)
    def _():
        g1_ref[...] = jnp.zeros_like(g1_ref)
        s1_ref[...] = jnp.zeros_like(s1_ref)

    g1_ref[...] += jnp.sum(dn1 * xhat, axis=0, keepdims=True)
    s1_ref[...] += jnp.sum(dn1, axis=0, keepdims=True)
    igrad_ref[...] = hgrad[...] + norm_back(dn1, xhat, rstd, gain[...])


def ffn_out_kernel(n_ff, n_out, table, mine, got, up_ref, down_ref, out_ref, turned):
    size = 2 * n_ff + n_out
    blocks = mine.shape[0] // size
    for side, ref in enumerate((mine, got)):
        for b in range(blocks):
            to = table[side * blocks + b]
            down_ref[rows_at(to, n_ff)] = ref[b * size : b * size + n_ff].astype(F32)
            turned[rows_at(to, n_ff)] = ref[b * size + n_ff : b * size + 2 * n_ff].astype(F32)
            out_ref[rows_at(to, n_out)] = ref[b * size + 2 * n_ff : (b + 1) * size].astype(F32)
    up_ref[...] = turned[...].T


def qkv_out_kernel(table, mine, got, out_ref, turned):
    blocks = table.shape[0] // 2
    size = mine.shape[0] // blocks
    for side, ref in enumerate((mine, got)):
        for b in range(blocks):
            turned[rows_at(table[side * blocks + b], size)] = ref[b * size : (b + 1) * size].astype(F32)
    for j in range(3):
        cols = turned.shape[0] // 3
        out_ref[j] = turned[j * cols : (j + 1) * cols].T


def swap(x, axis, bit):
    count = lax.axis_size(axis)
    return lax.ppermute(x, axis, [(i, i ^ bit) for i in range(count)])


def halo(x, axis):
    count = lax.axis_size(axis)
    prev = lax.ppermute(x, axis, [(i, i + 1) for i in range(count - 1)])
    nxt = lax.ppermute(x, axis, [(i + 1, i) for i in range(count - 1)])
    return prev, nxt


def gather_pieces(x, axis):
    pieces = [x]
    bit = 1
    while bit < lax.axis_size(axis):
        pieces = pieces + [swap(p, axis, bit) for p in pieces]
        bit *= 2
    return pieces


def tied(*arrays):
    return lax.optimization_barrier(arrays)


class Plan:

    def __init__(self, wide, narrow):
        self.wide, self.narrow = wide, narrow
        nb = [("narrow", 1 << i) for i in range(narrow.bit_length() - 1)][::-1]
        wb = [("wide", 1 << i) for i in range(1, wide.bit_length() - 1)]
        first = nb + wb
        second = wb[1:2] + nb + wb[:1] + wb[2:]
        self.orders = (first, second)
        self.steps = len(first)
        self.blocks = 1 << self.steps
        self.back = [[s for s in o if s[0] == "wide"][::-1] for o in self.orders]
        self.me = lax.axis_index("wide")
        self.core = self.me % 2

    def rel(self, order):
        j = np.zeros(self.blocks, np.int32)
        r = np.zeros(self.blocks, np.int32)
        for s, (axis, bit) in enumerate(order):
            has = (np.arange(self.blocks) >> (self.steps - 1 - s)) & 1
            if axis == "narrow":
                j += has * bit
            else:
                r += has * bit
        return j, r

    def by_core(self, a, b):
        return jnp.where(self.core == 0, jnp.asarray(a, jnp.int32), jnp.asarray(b, jnp.int32))

    def sources(self):
        (j0, r0), (j1, r1) = (self.rel(o) for o in self.orders)
        high = self.me - self.core
        n0, n1 = j0 * self.wide, j1 * self.wide
        mine = self.by_core(n0, n1) + (self.by_core(r0, r1) ^ high) + self.core
        send = self.by_core(n1, n0) + (self.by_core(r1, r0) ^ high) + 1 - self.core
        return jnp.concatenate([self.core[None], mine, send]).astype(jnp.int32)

    def targets(self):
        rels = []
        for o in self.orders:
            j, r = self.rel(o)
            rels.append(r[j == 0])
        high = self.me - self.core
        mine = (self.by_core(rels[0], rels[1]) ^ high) + self.core
        got = (self.by_core(rels[1], rels[0]) ^ high) + 1 - self.core
        return jnp.concatenate([mine, got]).astype(jnp.int32)

    def mixed(self, x, steps):
        pairs = []
        for w in range(self.wide):
            axis, bit = steps[w % 2]
            for n in range(self.narrow):
                to = (w, n ^ bit) if axis == "narrow" else (w ^ bit, n)
                pairs.append((w * self.narrow + n, to[0] * self.narrow + to[1]))
        return lax.ppermute(x, ("wide", "narrow"), pairs)


class Reduction:

    def __init__(self, plan, mine, send):
        self.plan, self.parts, self.operand, self.at = plan, [mine], send, 0
        self.rows = mine.shape[0]

    def total(self, low, high):
        out = self.parts[0][low:high].astype(F32)
        for p in self.parts[1:]:
            out = out + p[low:high].astype(F32)
        return out.astype(BF16)

    def advance(self):
        plan, at = self.plan, self.at
        back = len(plan.back[0])
        if at == 0:
            got = swap(self.operand, "wide", 1)
        elif at <= plan.steps:
            got = plan.mixed(self.operand, [o[at - 1] for o in plan.orders])
        elif at <= plan.steps + back:
            got = plan.mixed(self.operand, [o[at - plan.steps - 1] for o in plan.back])
        else:
            got = swap(self.operand, "wide", 1)
        self.at = at + 1
        if at <= plan.steps:
            self.parts.append(got)
            if at == plan.steps:
                self.operand = self.total(0, self.rows >> at)
            else:
                self.operand = self.total(self.rows >> (at + 1), self.rows >> at)
        elif at <= plan.steps + back:
            self.operand = jnp.concatenate([self.operand, got], axis=0)
        else:
            self.result = (self.operand, got)

    @property
    def left(self):
        return self.plan.steps + len(self.plan.back[0]) + 2 - self.at


def lockstep(*chains):
    live = [c for c in chains if c.left > 0]
    if len(live) > 1:
        for c, o in zip(live, tied(*[c.operand for c in live])):
            c.operand = o
    for c in live:
        c.advance()


class SmallSum:
    def __init__(self, value):
        self.operand = value
        self.bits = [(a, 1 << i) for a in ("wide", "narrow") for i in range(lax.axis_size(a).bit_length() - 1)]

    def advance(self):
        self.operand = self.operand + swap(self.operand, *self.bits.pop(0))

    @property
    def left(self):
        return len(self.bits)


def local(
    inputs, segment_ids, norm1_gain, norm1_shift, w_qkv, w_out,
    norm2_gain, norm2_shift, w_up, w_down, cotangent,
):
    feats, samp, width = inputs.shape
    tokens = feats * samp
    narrow = lax.axis_size("narrow")
    wide = lax.axis_size("wide")
    plan = Plan(wide, narrow)
    core = plan.core
    part = feats // 2
    group = max(g for g in (1, 2, 4) if part % g == 0)
    steps = part // group
    rows = group * samp
    head_cols = w_qkv.shape[2]
    own_ff = w_up.shape[1]
    slot = own_ff // 2
    ff = own_ff * narrow
    inpack = slot == 512
    n_ff, n_out, n_qkv = own_ff // wide, w_out.shape[0] // wide, 3 * head_cols // wide
    ordered = narrow == 2 and n_ff % 16 == 0 and n_out % 16 == 0 and n_qkv % 16 == 0
    blocks = plan.blocks

    def core_half(a, axis):
        size = a.shape[axis] // 2
        return lax.dynamic_slice_in_dim(a, core * size, size, axis)

    qkv_half = core_half(w_qkv.reshape(width, 3 * head_cols), 0)
    qkv_half, early = tied(qkv_half, inputs[:part])
    qkv_mine = gather_pieces(qkv_half, "narrow")[1:]
    prev0, next0 = halo(early, "wide")
    up_half = core_half(w_up, 1)
    small = jnp.concatenate(
        [up_half.reshape(-1, 512), core_half(w_down, 0), core_half(w_out, 0)], axis=0
    )
    held = tied(small, *qkv_mine)
    small, qkv_mine = held[0], list(held[1:])
    pack_mine = gather_pieces(small, "narrow")[1:]
    qkv_got = [swap(p, "wide", 1) for p in qkv_mine]
    late, prev0, next0 = tied(inputs, prev0, next0)
    prev1, next1 = halo(late[part:], "wide")

    def whole_of(mine, got):
        first = jnp.where(core == 0, mine, got)
        second = jnp.where(core == 0, got, mine)
        return jnp.concatenate([first, second], axis=0)

    pieces = [w_qkv] + [
        whole_of(m, g).reshape(width, 3, head_cols) for m, g in zip(qkv_mine, qkv_got)
    ]
    cut = narrow // 2
    w0, w1 = (
        (p[0] if len(p) == 1 else jnp.concatenate(p, axis=2)).reshape(width, 3 * GROUP_COLS)
        for p in (pieces[:cut], pieces[cut:])
    )

    id_rim = jnp.full((samp,), -1, jnp.int32)
    padded_ids = jnp.concatenate([id_rim, segment_ids, id_rim])
    window_ids = lax.dynamic_slice_in_dim(padded_ids, plan.me * samp, 3 * samp, 0)
    id_col = window_ids[:, None]
    id_row = jnp.tile(window_ids.reshape(3, samp), (1, HEADS_PER_GROUP))
    gain1, shift1 = norm1_gain[None, :], norm1_shift[None, :]
    gain2, shift2 = norm2_gain[None, :], norm2_shift[None, :]
    sources, targets = plan.sources(), plan.targets()

    def whole(a):
        return pl.BlockSpec(a.shape, lambda i: (0,) * a.ndim, pipeline_mode=pl.Buffered(1))

    def cube(offset):
        return pl.BlockSpec((group, samp, width), lambda i: (i + offset, 0, 0))

    smem = pl.BlockSpec(memory_space=pltpu.SMEM)
    anywhere = pl.BlockSpec(memory_space=pl.ANY)
    line = pl.BlockSpec((1, width), lambda i: (0, 0))
    vec = jax.ShapeDtypeStruct((1, width), F32)

    def tok(dtype):
        return jax.ShapeDtypeStruct((tokens, width), dtype)

    def cost(flops, size):
        return pl.CostEstimate(flops=flops, bytes_accessed=size, transcendentals=0)

    def qkv_block(offset):
        return pl.BlockSpec((2, 3, rows, 3 * GROUP_COLS), lambda i: (0, 0, i + offset, 0))

    done = None
    for h, (before, after) in enumerate(((prev0, next0), (prev1, next1))):
        off = h * steps
        args = [id_col, id_row, before, inputs, after, w0, w1, gain1, shift1]
        specs = [whole(id_col), whole(id_row), cube(0), cube(off), cube(0)]
        specs += [whole(a) for a in (w0, w1, gain1, shift1)]
        alias = {}
        if done is not None:
            alias = {len(args): 0, len(args) + 1: 1}
            args += done
            specs += [anywhere, anywhere]
        done = pl.pallas_call(
            attn_fwd_kernel,
            grid=(steps,),
            in_specs=specs,
            out_specs=[qkv_block(off), cube(off)],
            out_shape=[
                jax.ShapeDtypeStruct((2, 3, tokens, 3 * GROUP_COLS), BF16),
                jax.ShapeDtypeStruct((feats, samp, width), BF16),
            ],
            input_output_aliases=alias,
            cost_estimate=cost(6 * 10**9 // 2, 12 << 20),
            name=f"attn_fwd_{h}",
        )(*args)
    held = tied(done[1], *pack_mine)
    done, pack_mine = [done[0], held[0]], list(held[1:])
    pack_got = [swap(p, "wide", 1) for p in pack_mine]
    qkv, attended = done

    x_flat = inputs.reshape(tokens, width)
    cot_flat = cotangent.reshape(tokens, width)
    att_flat = attended.reshape(tokens, width)
    packs = [a for pair in zip(pack_mine, pack_got) for a in pair]
    args = [sources, x_flat, att_flat, cot_flat, gain2, shift2, w_up, w_down, w_out]
    if inpack:
        args += packs
    else:
        up_rows = width * slot // 512
        args += [p[up_rows:] for p in packs]
        args += [p[:up_rows].reshape(width, slot) for p in packs]
    if ordered:
        size = blocks * (2 * n_ff + n_out)
        sums = [(size, 512)] * 2
    else:
        sums = [(ff, width), (ff, width), (width, width)]
    outs = [tok(BF16), tok(F32), tok(BF16), vec, vec]
    outs += [jax.ShapeDtypeStruct(s, BF16) for s in sums]
    scratch = [
        ((width, width), BF16), ((width, slot), BF16), ((slot, width), BF16),
        ((tokens, width), F32), ((tokens, width), BF16), ((tokens, width), F32), ((tokens, width), F32),
        ((tokens, slot), BF16), ((tokens, slot), BF16), ((tokens, width), BF16),
        ((ff, width), BF16), ((ff, width), BF16), ((width, width), BF16),
    ]
    block_out, hidden_grad, dattended, gain2_grad, shift2_grad, *packed = pl.pallas_call(
        functools.partial(chain_kernel, narrow - 1, inpack, ordered),
        grid=(2 * narrow,),
        in_specs=[smem] + [whole(a) for a in args[1:]],
        out_specs=[whole(o) for o in outs],
        out_shape=outs,
        scratch_shapes=[pltpu.VMEM(*s) for s in scratch],
        cost_estimate=cost(15 * 10**9, 20 << 20),
        name="chain",
    )(*args)

    def arranged(natural):
        flat = natural.reshape(narrow * wide, natural.shape[2], 512)
        places = sources[1:].reshape(2, blocks)
        return [jnp.take(flat, places[s], axis=0).reshape(-1, 512) for s in range(2)]

    if not ordered:
        down, up, out = (p.reshape(narrow, wide, -1, 512) for p in packed)
        packed = arranged(jnp.concatenate([down, up, out], axis=2))
    big = Reduction(plan, packed[0], packed[1])

    datt = dattended.reshape(feats, samp, width)
    d_prev, d_next = halo(datt, "wide")
    lockstep(big)
    group2 = group
    all_steps = feats // group2

    def pair_block(cols):
        return pl.BlockSpec((2, rows, cols), lambda i: (0, i, 0))

    dq, dkv_own = pl.pallas_call(
        attn_bwd_own_kernel,
        grid=(all_steps,),
        in_specs=[whole(id_col), whole(id_row), qkv_block(0), cube(0)],
        out_specs=[pair_block(GROUP_COLS), pair_block(2 * GROUP_COLS)],
        out_shape=[
            jax.ShapeDtypeStruct((2, tokens, GROUP_COLS), BF16),
            jax.ShapeDtypeStruct((2, tokens, 2 * GROUP_COLS), F32),
        ],
        cost_estimate=cost(10 * 10**9, 14 << 20),
        name="attn_bwd_own",
    )(id_col, id_row, qkv, datt)
    dkv_own, big.operand = tied(dkv_own, big.operand)
    lockstep(big)
    dkv = pl.pallas_call(
        attn_bwd_near_kernel,
        grid=(all_steps,),
        in_specs=[whole(id_col), whole(id_row), qkv_block(0), cube(0), cube(0), pair_block(2 * GROUP_COLS)],
        out_specs=pair_block(2 * GROUP_COLS),
        out_shape=jax.ShapeDtypeStruct((2, tokens, 2 * GROUP_COLS), BF16),
        cost_estimate=cost(10 * 10**9, 14 << 20),
        name="attn_bwd_near",
    )(id_col, id_row, qkv, d_prev, d_next, dkv_own)
    dkv, big.operand = tied(dkv, big.operand)
    lockstep(big)

    natural = (6 * GROUP_COLS, width)
    outs = [jax.ShapeDtypeStruct((blocks * n_qkv, 512), BF16)] * 2
    if not ordered:
        outs = [jax.ShapeDtypeStruct(natural, BF16)]
    args = [sources, x_flat, dq, dkv, gain1, shift1]
    packed = pl.pallas_call(
        functools.partial(qkv_grad_kernel, ordered),
        grid=(1,),
        in_specs=[smem] + [whole(a) for a in args[1:]],
        out_specs=[whole(o) for o in outs],
        out_shape=outs,
        scratch_shapes=[pltpu.VMEM((tokens, width), BF16), pltpu.VMEM(natural, BF16)],
        cost_estimate=cost(2 * 10**9, 6 << 20),
        name="qkv_grad",
    )(*args)
    if not ordered:
        turned = packed[0].reshape(2, 3, narrow // 2, head_cols, width).transpose(0, 2, 1, 3, 4)
        packed = arranged(turned.reshape(narrow, wide, n_qkv, width))
    last = Reduction(plan, packed[0], packed[1])

    flat = pl.BlockSpec((CHUNK, width), lambda i: (i, 0))
    dkv, last.operand = tied(dkv, last.operand)
    input_grad, gain1_grad, shift1_grad = pl.pallas_call(
        input_grad_kernel,
        grid=(tokens // CHUNK,),
        in_specs=[flat, flat]
        + [pl.BlockSpec((2, CHUNK, n * GROUP_COLS), lambda i: (0, i, 0)) for n in (1, 2)]
        + [whole(a) for a in (w0, w1, gain1)],
        out_specs=[flat, line, line],
        out_shape=[tok(F32), vec, vec],
        cost_estimate=cost(2 * 10**9, 8 << 20),
        name="input_grad",
    )(x_flat, hidden_grad, dq, dkv, w0, w1, gain1)
    norms = SmallSum(jnp.concatenate([gain1_grad, shift1_grad, gain2_grad, shift2_grad], axis=0))

    lockstep(last, big)
    lockstep(last, big)
    while big.left > 0:
        lockstep(last, big, norms)
    down_rows, out_rows, qkv_rows = own_ff, w_out.shape[0], 3 * head_cols
    if ordered:
        shapes = [jax.ShapeDtypeStruct(s, F32) for s in (w_up.shape, w_down.shape, w_out.shape)]
        up_grad, down_grad, out_grad = pl.pallas_call(
            functools.partial(ffn_out_kernel, n_ff, n_out),
            grid=(1,),
            in_specs=[smem] + [whole(a) for a in big.result],
            out_specs=[whole(s) for s in shapes],
            out_shape=shapes,
            scratch_shapes=[pltpu.VMEM((own_ff, width), F32)],
            cost_estimate=cost(0, 8 << 20),
            name="ffn_out",
        )(targets, *big.result)
    while last.left > 0 or norms.left > 0:
        if ordered and last.left == 1:
            last.operand, out_grad = tied(last.operand, out_grad)
        lockstep(last, norms)

    if ordered:
        shape = jax.ShapeDtypeStruct((3, width, head_cols), F32)
        qkv_grad = pl.pallas_call(
            qkv_out_kernel,
            grid=(1,),
            in_specs=[smem] + [whole(a) for a in last.result],
            out_specs=whole(shape),
            out_shape=shape,
            scratch_shapes=[pltpu.VMEM((qkv_rows, width), F32)],
            cost_estimate=cost(0, 3 << 20),
            name="qkv_out",
        )(targets, *last.result)
        qkv_grad = qkv_grad.transpose(1, 0, 2)
    else:

        def natural_rows(pair, count):
            both = jnp.concatenate(pair, axis=0).reshape(wide, -1, 512)
            places = jnp.zeros((wide,), jnp.int32).at[targets].set(jnp.arange(wide, dtype=jnp.int32))
            return jnp.take(both, places, axis=0).astype(F32)

        full = natural_rows(big.result, wide)
        down_grad = full[:, :n_ff].reshape(w_down.shape)
        up_grad = full[:, n_ff : 2 * n_ff].reshape(own_ff, width).T
        out_grad = full[:, 2 * n_ff :].reshape(w_out.shape)
        qkv_grad = natural_rows(last.result, wide).reshape(qkv_rows, width).T.reshape(width, 3, head_cols)
    norm_sums = norms.operand
    return (
        block_out.reshape(feats, samp, width),
        input_grad.reshape(feats, samp, width),
        norm_sums[0],
        norm_sums[1],
        qkv_grad,
        out_grad,
        norm_sums[2],
        norm_sums[3],
        up_grad,
        down_grad,
    )


def solution(mesh):
    rows = P("narrow", "wide", None)
    placed = (
        rows, P(), P(), P(), P(None, None, "narrow"), P("narrow", None),
        P(), P(), P(None, "narrow"), P("narrow", None), rows,
    )
    outs = (
        rows, rows, P(), P(), P(None, None, "narrow"), P("narrow", None),
        P(), P(), P(None, "narrow"), P("narrow", None),
    )
    return jax.shard_map(local, mesh=mesh, in_specs=placed, out_specs=outs, check_vma=False)
```

```python
import functools

import jax
import jax.numpy as jnp
import numpy as np
from jax import lax
from jax.experimental import pallas as pl
from jax.experimental.pallas import tpu as pltpu
from jax.sharding import PartitionSpec as P

HEAD_DIM = 64
HEADS_PER_GROUP = 4
GROUP_COLS = HEAD_DIM * HEADS_PER_GROUP
EPS = 1e-05
SCALE = HEAD_DIM ** (-0.5)
F32 = jnp.float32
BF16 = jnp.bfloat16
NEG = -1e30
CHUNK = 256


def dot_nn(a, b):
    return lax.dot_general(a, b, (((1,), (0,)), ((), ())), preferred_element_type=F32)


def dot_nt(a, b):
    return lax.dot_general(a, b, (((1,), (1,)), ((), ())), preferred_element_type=F32)


def dot_tn(a, b):
    return lax.dot_general(a, b, (((0,), (0,)), ((), ())), preferred_element_type=F32)


def norm_parts(z):
    mean = jnp.mean(z, axis=-1, keepdims=True)
    centred = z - mean
    var = jnp.mean(centred * centred, axis=-1, keepdims=True)
    rstd = lax.rsqrt(var + EPS)
    return centred * rstd, rstd


def norm_back(grad, xhat, rstd, gain):
    gg = grad * gain
    m1 = jnp.mean(gg, axis=-1, keepdims=True)
    m2 = jnp.mean(gg * xhat, axis=-1, keepdims=True)
    return rstd * (gg - m1 - xhat * m2)


def lane_head(rows, dtype):
    lane = lax.broadcasted_iota(jnp.int32, (rows, GROUP_COLS), 1)
    return [
        ((lane >= h * HEAD_DIM) & (lane < (h + 1) * HEAD_DIM)).astype(F32).astype(dtype)
        for h in range(HEADS_PER_GROUP)
    ]


def block_diag(rows, masks):
    return jnp.concatenate([rows * m for m in masks], axis=0)


def pick_heads(full, rows):
    low = lax.broadcasted_iota(jnp.int32, (rows, 2 * HEAD_DIM), 1) < HEAD_DIM
    out = []
    for pair in range(HEADS_PER_GROUP // 2):
        cols = slice(2 * pair * HEAD_DIM, 2 * (pair + 1) * HEAD_DIM)
        at = 2 * pair * rows
        out.append(jnp.where(low, full[at : at + rows, cols], full[at + rows : at + 2 * rows, cols]))
    return jnp.concatenate(out, axis=1)


def rows_at(index, size):
    return pl.ds(pl.multiple_of(index * size, size), size)


def staged(count, first, second, third, lag=2):
    a, b = {}, {}
    for t in range(count + lag):
        if t < count:
            a[t] = first(t)
        if 0 <= t - 1 < count:
            b[t - 1] = second(t - 1, *a.pop(t - 1))
        if 0 <= t - lag < count:
            third(t - lag, *b.pop(t - lag))


def each(count, body, unroll=1):
    lax.fori_loop(0, count, lambda i, carry: (body(i), carry)[1], 0, unroll=unroll)


def attn_fwd_kernel(idc, idr, xp, xo, xn, w0, w1, gain, shift, qkv_ref, att_ref):
    feats, samp, width = xo.shape
    rows = feats * samp
    x = jnp.concatenate(
        [xp[...].reshape(rows, width), xo[...].reshape(rows, width), xn[...].reshape(rows, width)],
        axis=0,
    ).astype(F32)
    xhat, _ = norm_parts(x)
    normed = (xhat * gain[...] + shift[...]).astype(BF16)
    for hg, w in enumerate((w0, w1)):
        qkv = dot_nn(normed, w[...]).astype(BF16)
        qkv_ref[hg] = qkv.reshape(3, rows, 3 * GROUP_COLS)
    allowed = idc[...] == idr[1:2, :]
    m16 = lane_head(1, BF16)
    q16 = [m * SCALE for m in m16]

    def first(i):
        f, hg = i // 2, i % 2
        sl = slice(f * samp, (f + 1) * samp)
        k, _ = bwd_pieces(qkv_ref, hg, sl)
        return (dot_nt(k, block_diag(qkv_ref[hg, 1, sl, 0:GROUP_COLS], q16)),)

    def second(i, s):
        s = jnp.where(allowed, s, NEG)
        top = jnp.max(s, axis=0, keepdims=True)
        e = jnp.exp(s - top)
        total = jnp.sum(e, axis=0, keepdims=True)
        return ((e * (1.0 / total)).astype(BF16),)

    def third(i, p):
        f, hg = i // 2, i % 2
        _, v = bwd_pieces(qkv_ref, hg, slice(f * samp, (f + 1) * samp))
        o = pick_heads(dot_tn(p, v), samp)
        att_ref[f, :, hg * GROUP_COLS : (hg + 1) * GROUP_COLS] = o.astype(BF16)

    staged(2 * feats, first, second, third, 1)


def phi_parts(u):
    e = jnp.exp(-0.5 * (u * u))
    t = 1.0 / (1.0 + (0.3275911 * 0.7071067811865476) * jnp.abs(u))
    poly = t * (
        0.127414796
        + t * (-0.142248368 + t * (0.7107068705 + t * (-0.7265760135 + t * 0.5307027145)))
    )
    tail = poly * e
    cdf = jnp.where(u < 0, tail, 1.0 - tail)
    return cdf, u * (e * 0.3989422804014327)


def chain_kernel(others, inpack, ordered, *refs):
    table, x, att, cot, gain, shift, up_own, down_own, out_own = refs[:9]
    refs = refs[9:]
    packs, refs = refs[: 2 * others], refs[2 * others :]
    if inpack:
        extra = packs
    else:
        extra, refs = refs[: 2 * others], refs[2 * others :]
    count = 2 if ordered else 3
    out_ref, hgrad_ref, dat_ref, g2_ref, s2_ref = refs[:5]
    packed, refs = refs[5 : 5 + count], refs[5 + count :]
    (wo, up_a, down_a, up_b, down_b, hidden, normed, mlp, dn2) = refs[:9]
    act_a, pre_a, act_b, pre_b, res, gd, gu, go = refs[9:]
    tokens, width = x.shape
    unit = up_a.shape[1]
    slot = up_own.shape[1] // 2
    per = slot // unit
    last = (2 * others + 2) * per // 2
    narrow_rows = out_own.shape[0]
    half_rows = narrow_rows // 2
    chunks = tokens // CHUNK
    step = pl.program_id(0)
    core = table[0]

    def bases(unit):
        for j in range(1, others + 1):
            yield 2 * j - 2, 2 * j + core
            yield 2 * j - 1, 2 * j + 1 - core

    @pl.when(step == 0)
    def _():
        wo[:narrow_rows] = out_own[...]
        for i, base in bases(half_rows):
            wo[rows_at(base, half_rows)] = packs[i][2 * slot : 2 * slot + half_rows] if inpack else packs[i][slot : slot + half_rows]
        g2_ref[...] = jnp.zeros_like(g2_ref)
        s2_ref[...] = jnp.zeros_like(s2_ref)
        for ref in (act_b, pre_b, up_b, down_b):
            ref[...] = jnp.zeros_like(ref)

        def start(i):
            sl = rows_at(i, CHUNK)
            h = x[sl].astype(F32) + dot_nn(att[sl], wo[...])
            hidden[sl] = h
            xhat, _ = norm_parts(h)
            normed[sl] = (xhat * gain[...] + shift[...]).astype(BF16)
            mlp[sl] = jnp.zeros((CHUNK, width), F32)
            dn2[sl] = jnp.zeros((CHUNK, width), F32)

        each(chunks, start)

    def load(parity, up, down):
        for pair in range(last):

            @pl.when(step == pair)
            def _():
                i, sub = divmod(2 * pair + parity, per)
                low, high = sub * unit, (sub + 1) * unit
                if i < 2:
                    low, high = low + i * slot, high + i * slot
                    up[...] = up_own[:, low:high]
                    down[...] = down_own[low:high]
                elif inpack:
                    up[...] = packs[i - 2][:slot, low:high]
                    down[...] = packs[i - 2][slot + low : slot + high]
                else:
                    up[...] = extra[i - 2][:, low:high]
                    down[...] = packs[i - 2][low:high]

    def place(item):
        i, sub = item // per, item % per
        swapped = jnp.where(i % 2 == 0, core, 1 - core)
        base = jnp.where(i < 2, i, i - i % 2 + swapped)
        return rows_at(base * per + sub, unit)

    def spread(item, up, down, act, pre):
        at = place(item)
        half = width // 2
        for i in range(chunks):
            sl = slice(i * CHUNK, (i + 1) * CHUNK)
            mlp[sl] += dot_nn(act[sl], down[...])
            dn2[sl] += dot_nt(pre[sl], up[...])
            for j in range(i, 4, chunks):
                cols = slice((j % 2) * half, (j % 2 + 1) * half)
                if j < 2:
                    gd[at, cols] = dot_tn(act[...], cot[:, cols]).astype(BF16)
                else:
                    gu[at, cols] = dot_tn(pre[...], normed[:, cols]).astype(BF16)
            yield

    def phase(up, down, act, pre, *before):
        rest = spread(*before)
        ready = {}
        for i in range(chunks + 1):
            if i < chunks:
                sl = slice(i * CHUNK, (i + 1) * CHUNK)
                ready[i] = dot_nn(normed[sl], up[...]), dot_nt(cot[sl], down[...])
            if i > 0:
                next(rest)
                u, back = ready.pop(i - 1)
                sl = slice((i - 1) * CHUNK, i * CHUNK)
                cdf, upd = phi_parts(u)
                act[sl] = (u * cdf).astype(BF16)
                pre[sl] = (back * (cdf + upd)).astype(BF16)

    load(0, up_a, down_a)

    @pl.when(step < last)
    def _():
        before = jnp.maximum(2 * step - 1, 0)
        phase(up_a, down_a, act_a, pre_a, before, up_b, down_b, act_b, pre_b)

    load(1, up_b, down_b)

    @pl.when(step < last)
    def _():
        phase(up_b, down_b, act_b, pre_b, 2 * step, up_a, down_a, act_a, pre_a)

    @pl.when(step == last)
    def _():
        for _ in spread(2 * last - 1, up_b, down_b, act_b, pre_b):
            pass

        def finish(i):
            sl = rows_at(i, CHUNK)
            h = hidden[sl]
            out_ref[sl] = (h + mlp[sl]).astype(BF16)
            xhat, rstd = norm_parts(h)
            d = dn2[sl]
            g2_ref[...] += jnp.sum(d * xhat, axis=0, keepdims=True)
            s2_ref[...] += jnp.sum(d, axis=0, keepdims=True)
            hgrad = cot[sl].astype(F32) + norm_back(d, xhat, rstd, gain[...])
            hgrad_ref[sl] = hgrad
            r = hgrad.astype(BF16)
            res[sl] = r
            dat_ref[sl] = dot_nt(r, wo[...]).astype(BF16)

        each(chunks, finish)
        go[...] = dot_tn(att[...], res[...]).astype(BF16)
        if ordered:
            blocks = (table.shape[0] - 1) // 2
            n_ff = gd.shape[0] // (2 * blocks)
            n_out = go.shape[0] // (2 * blocks)
            size = 2 * n_ff + n_out
            for side in range(2):
                for b in range(blocks):
                    src = table[1 + side * blocks + b]
                    ref = packed[side]
                    ref[b * size : b * size + n_ff] = gd[rows_at(src, n_ff)]
                    ref[b * size + n_ff : b * size + 2 * n_ff] = gu[rows_at(src, n_ff)]
                    ref[b * size + 2 * n_ff : (b + 1) * size] = go[rows_at(src, n_out)]
        else:
            packed[0][...] = gd[...]
            packed[1][...] = gu[...]
            packed[2][...] = go[...]


def bwd_pieces(qkv_ref, hg, sl):
    k = jnp.concatenate(
        [qkv_ref[hg, w, sl, GROUP_COLS : 2 * GROUP_COLS] for w in range(3)], axis=0
    )
    v = jnp.concatenate(
        [qkv_ref[hg, w, sl, 2 * GROUP_COLS : 3 * GROUP_COLS] for w in range(3)], axis=0
    )
    return k, v


def head_rows(a):
    return jnp.concatenate(
        [a[:, h * HEAD_DIM : (h + 1) * HEAD_DIM] for h in range(HEADS_PER_GROUP)], axis=0
    )


def score_grads(s, dp, mask):
    s = jnp.where(mask, s, NEG)
    top = jnp.max(s, axis=0, keepdims=True)
    e = jnp.exp(s - top)
    total = jnp.sum(e, axis=0, keepdims=True)
    p = e * (1.0 / total)
    pd = p * dp
    delta = jnp.sum(pd, axis=0, keepdims=True)
    return (pd - p * delta).astype(BF16), p


def attn_bwd_own_kernel(idc, idr, qkv_ref, do_ref, dq_ref, dkv_ref):
    feats, samp, width = do_ref.shape
    m16 = lane_head(1, BF16)
    q16 = [m * SCALE for m in m16]
    mask = idc[...] == idr[1:2, :]

    def pieces(i):
        f, hg = i // 2, i % 2
        sl = slice(f * samp, (f + 1) * samp)
        q = qkv_ref[hg, 1, sl, 0:GROUP_COLS]
        d = do_ref[f, :, hg * GROUP_COLS : (hg + 1) * GROUP_COLS]
        return hg, sl, q, d

    def first(i):
        hg, sl, q, d = pieces(i)
        k, v = bwd_pieces(qkv_ref, hg, sl)
        return dot_nt(k, block_diag(q, q16)), dot_nt(v, block_diag(d, m16))

    def second(i, s, dp):
        ds, p = score_grads(s, dp, mask)
        own = slice(samp, 2 * samp)
        return ds, head_rows(ds[own]), head_rows(p[own].astype(BF16))

    def third(i, ds, dss, ps):
        hg, sl, q, d = pieces(i)
        k, _ = bwd_pieces(qkv_ref, hg, sl)
        dq_ref[hg, sl, :] = (pick_heads(dot_tn(ds, k), samp) * SCALE).astype(BF16)
        dkv_ref[hg, sl, 0:GROUP_COLS] = pick_heads(dot_nn(dss, q), samp)
        dkv_ref[hg, sl, GROUP_COLS : 2 * GROUP_COLS] = pick_heads(dot_nn(ps, d), samp)

    staged(2 * feats, first, second, third)


def attn_bwd_near_kernel(idc, idr, qkv_ref, dp_ref, dn_ref, sum_ref, *rest):
    dkv_ref = rest[-1]
    feats, samp, width = dp_ref.shape
    m16 = lane_head(1, BF16)
    q16 = [m * SCALE for m in m16]
    near = ((0, 0, dp_ref), (2, 1, dn_ref))
    masks = [idc[a * samp : (a + 2) * samp, :] == idr[g : g + 1, :] for g, a, _ in near]

    def pieces(i, side):
        f, hg = i // 2, i % 2
        sl = slice(f * samp, (f + 1) * samp)
        g, a, ref = near[side]
        q = qkv_ref[hg, g, sl, 0:GROUP_COLS]
        d = ref[f, :, hg * GROUP_COLS : (hg + 1) * GROUP_COLS]
        return hg, sl, slice(a * samp, (a + 2) * samp), q, d

    def first(i):
        out = []
        for side in range(2):
            hg, sl, span, q, d = pieces(i, side)
            k, v = bwd_pieces(qkv_ref, hg, sl)
            out += [dot_nt(k[span], block_diag(q, q16)), dot_nt(v[span], block_diag(d, m16))]
        return out

    def second(i, s0, dp0, s1, dp1):
        dss, ps = [], []
        for side, (s, dp) in enumerate(((s0, dp0), (s1, dp1))):
            ds, p = score_grads(s, dp, masks[side])
            own = slice((1 - side) * samp, (2 - side) * samp)
            dss.append(head_rows(ds[own]))
            ps.append(head_rows(p[own].astype(BF16)))
        return jnp.concatenate(dss, axis=1), jnp.concatenate(ps, axis=1)

    def third(i, dss, ps):
        hg, sl, _, q0, d0 = pieces(i, 0)
        _, _, _, q1, d1 = pieces(i, 1)
        low, high = slice(0, GROUP_COLS), slice(GROUP_COLS, 2 * GROUP_COLS)
        dk = pick_heads(dot_nn(dss, jnp.concatenate([q0, q1], axis=0)), samp)
        dv = pick_heads(dot_nn(ps, jnp.concatenate([d0, d1], axis=0)), samp)
        dkv_ref[hg, sl, low] = ((dk + sum_ref[hg, sl, low]) * SCALE).astype(BF16)
        dkv_ref[hg, sl, high] = (dv + sum_ref[hg, sl, high]).astype(BF16)

    staged(2 * feats, first, second, third)


def qkv_grad_kernel(ordered, table, x, dq, dkv, gain, shift, *refs):
    normed, gq = refs[-2:]
    outs = refs[:-2]
    tokens, width = x.shape

    def start(i):
        sl = rows_at(i, CHUNK)
        xhat, _ = norm_parts(x[sl].astype(F32))
        normed[sl] = (xhat * gain[...] + shift[...]).astype(BF16)

    each(tokens // CHUNK, start)
    for hg in range(2):
        low = 3 * hg * GROUP_COLS
        gq[low : low + GROUP_COLS] = dot_tn(dq[hg], normed[...]).astype(BF16)
        gq[low + GROUP_COLS : low + 3 * GROUP_COLS] = dot_tn(dkv[hg], normed[...]).astype(BF16)
    if ordered:
        blocks = (table.shape[0] - 1) // 2
        size = gq.shape[0] // (2 * blocks)
        for side in range(2):
            for b in range(blocks):
                outs[side][b * size : (b + 1) * size] = gq[rows_at(table[1 + side * blocks + b], size)]
    else:
        outs[0][...] = gq[...]


def input_grad_kernel(x, hgrad, dq, dkv, w0, w1, gain, igrad_ref, g1_ref, s1_ref):
    xhat, rstd = norm_parts(x[...].astype(F32))
    dn1 = dot_nt(dq[0], w0[:, :GROUP_COLS]) + dot_nt(dq[1], w1[:, :GROUP_COLS])
    dn1 = dn1 + dot_nt(dkv[0], w0[:, GROUP_COLS:]) + dot_nt(dkv[1], w1[:, GROUP_COLS:])

    @pl.when(pl.program_id(0) == 0)
    def _():
        g1_ref[...] = jnp.zeros_like(g1_ref)
        s1_ref[...] = jnp.zeros_like(s1_ref)

    g1_ref[...] += jnp.sum(dn1 * xhat, axis=0, keepdims=True)
    s1_ref[...] += jnp.sum(dn1, axis=0, keepdims=True)
    igrad_ref[...] = hgrad[...] + norm_back(dn1, xhat, rstd, gain[...])


def ffn_out_kernel(n_ff, n_out, table, mine, got, up_ref, down_ref, out_ref, turned):
    size = 2 * n_ff + n_out
    blocks = mine.shape[0] // size
    for side, ref in enumerate((mine, got)):
        for b in range(blocks):
            to = table[side * blocks + b]
            down_ref[rows_at(to, n_ff)] = ref[b * size : b * size + n_ff].astype(F32)
            turned[rows_at(to, n_ff)] = ref[b * size + n_ff : b * size + 2 * n_ff].astype(F32)
            out_ref[rows_at(to, n_out)] = ref[b * size + 2 * n_ff : (b + 1) * size].astype(F32)
    up_ref[...] = turned[...].T


def qkv_out_kernel(table, mine, got, out_ref, turned):
    blocks = table.shape[0] // 2
    size = mine.shape[0] // blocks
    for side, ref in enumerate((mine, got)):
        for b in range(blocks):
            turned[rows_at(table[side * blocks + b], size)] = ref[b * size : (b + 1) * size].astype(F32)
    for j in range(3):
        cols = turned.shape[0] // 3
        out_ref[j] = turned[j * cols : (j + 1) * cols].T


def swap(x, axis, bit):
    count = lax.axis_size(axis)
    return lax.ppermute(x, axis, [(i, i ^ bit) for i in range(count)])


def halo(x, axis):
    count = lax.axis_size(axis)
    prev = lax.ppermute(x, axis, [(i, i + 1) for i in range(count - 1)])
    nxt = lax.ppermute(x, axis, [(i + 1, i) for i in range(count - 1)])
    return prev, nxt


def gather_pieces(x, axis):
    pieces = [x]
    bit = 1
    while bit < lax.axis_size(axis):
        pieces = pieces + [swap(p, axis, bit) for p in pieces]
        bit *= 2
    return pieces


def tied(*arrays):
    return lax.optimization_barrier(arrays)


class Plan:

    def __init__(self, wide, narrow, fours=False):
        self.wide, self.narrow, self.fours = wide, narrow, fours
        nb = [("narrow", 1 << i) for i in range(narrow.bit_length() - 1)][::-1]
        wb = [("wide", 1 << i) for i in range(1, wide.bit_length() - 1)]
        first = nb + wb
        second = wb[:1] + nb + wb[1:] if fours else wb[1:2] + nb + wb[:1] + wb[2:]
        self.orders = (first, second)
        self.steps = len(first)
        self.blocks = 1 << self.steps
        self.back = [[s for s in o if s[0] == "wide"][::-1] for o in self.orders]
        self.me = lax.axis_index("wide")
        self.core = self.me % 2

    def rel(self, order):
        j = np.zeros(self.blocks, np.int32)
        r = np.zeros(self.blocks, np.int32)
        for s, (axis, bit) in enumerate(order):
            has = (np.arange(self.blocks) >> (self.steps - 1 - s)) & 1
            if axis == "narrow":
                j += has * bit
            else:
                r += has * bit
        return j, r

    def by_core(self, a, b):
        return jnp.where(self.core == 0, jnp.asarray(a, jnp.int32), jnp.asarray(b, jnp.int32))

    def sources(self):
        (j0, r0), (j1, r1) = (self.rel(o) for o in self.orders)
        high = self.me - self.core
        n0, n1 = j0 * self.wide, j1 * self.wide
        mine = self.by_core(n0, n1) + (self.by_core(r0, r1) ^ high) + self.core
        send = self.by_core(n1, n0) + (self.by_core(r1, r0) ^ high) + 1 - self.core
        return jnp.concatenate([self.core[None], mine, send]).astype(jnp.int32)

    def targets(self):
        rels = []
        for o in self.orders:
            j, r = self.rel(o)
            rels.append(r[j == 0])
        high = self.me - self.core
        mine = (self.by_core(rels[0], rels[1]) ^ high) + self.core
        got = (self.by_core(rels[1], rels[0]) ^ high) + 1 - self.core
        return jnp.concatenate([mine, got]).astype(jnp.int32)

    def mixed(self, x, steps):
        pairs = []
        for w in range(self.wide):
            axis, bit = steps[w % 2]
            for n in range(self.narrow):
                to = (w, n ^ bit) if axis == "narrow" else (w ^ bit, n)
                pairs.append((w * self.narrow + n, to[0] * self.narrow + to[1]))
        return lax.ppermute(x, ("wide", "narrow"), pairs)


class Reduction:

    def __init__(self, plan, mine, send):
        self.plan, self.parts, self.operands, self.at = plan, [mine], [send], 0
        self.rows = mine.shape[0]
        self.work = self.stages()

    def total(self, low, high):
        out = self.parts[0][low:high].astype(F32)
        for p in self.parts[1:]:
            out = out + p[low:high].astype(F32)
        return out.astype(BF16)

    def around(self, operands):
        (_, high), (_, low) = self.plan.orders[0][-2:]
        bits = [low, high, high + low]
        return [swap(o, "wide", b) for o, b in zip(operands, bits)]

    def stages(self):
        plan, rows = self.plan, self.rows
        four = 2 if plan.fours else 0
        self.parts.append(swap(self.operands[0], "wide", 1))
        for at in range(plan.steps - four):
            self.operands = [self.total(rows >> (at + 1), rows >> at)]
            yield
            self.parts.append(plan.mixed(self.operands[0], [o[at] for o in plan.orders]))
        if four:
            size = rows >> plan.steps
            self.operands = [self.total(q * size, (q + 1) * size) for q in (1, 2, 3)]
            yield
            self.parts += self.around(self.operands)
        held = self.total(0, rows >> plan.steps)
        if four:
            self.operands = [held]
            yield
            held = jnp.concatenate([held] + self.around([self.operands[0]] * 3), axis=0)
        for at in range(four, len(plan.back[0])):
            self.operands = [held]
            yield
            got = plan.mixed(self.operands[0], [o[at] for o in plan.back])
            held = jnp.concatenate([self.operands[0], got], axis=0)
        self.operands = [held]
        yield
        self.result = (self.operands[0], swap(self.operands[0], "wide", 1))

    def advance(self):
        next(self.work, None)


def lockstep(*chains):
    if len(chains) > 1:
        held = tied([c.operands for c in chains])[0]
        for c, o in zip(chains, held):
            c.operands = list(o)
    for c in chains:
        c.advance()


def hold(value, chain):
    value, operands = tied(value, chain.operands)
    chain.operands = list(operands)
    return value


class SmallSum:
    def __init__(self, value):
        self.operands = [value]
        self.bits = [(a, 1 << i) for a in ("wide", "narrow") for i in range(lax.axis_size(a).bit_length() - 1)]

    def advance(self):
        if self.bits:
            (value,) = self.operands
            self.operands = [value + swap(value, *self.bits.pop(0))]


def local(
    inputs, segment_ids, norm1_gain, norm1_shift, w_qkv, w_out,
    norm2_gain, norm2_shift, w_up, w_down, cotangent,
):
    feats, samp, width = inputs.shape
    tokens = feats * samp
    narrow = lax.axis_size("narrow")
    wide = lax.axis_size("wide")
    plan, short = Plan(wide, narrow), Plan(wide, narrow, True)
    core = plan.core
    group = max(g for g in (1, 2, 4) if feats % (2 * g) == 0)
    steps = feats // group
    rows = group * samp
    head_cols = w_qkv.shape[2]
    own_ff = w_up.shape[1]
    slot = own_ff // 2
    ff = own_ff * narrow
    inpack = slot == 512
    unit = min(256, slot)
    n_ff, n_out, n_qkv = own_ff // wide, w_out.shape[0] // wide, 3 * head_cols // wide
    ordered = narrow == 2 and n_ff % 16 == 0 and n_out % 16 == 0 and n_qkv % 16 == 0
    blocks = plan.blocks

    def core_half(a, axis):
        size = a.shape[axis] // 2
        return lax.dynamic_slice_in_dim(a, core * size, size, axis)

    qkv_half = core_half(w_qkv.reshape(width, 3 * head_cols), 0)
    up_half = core_half(w_up, 1)
    small = jnp.concatenate(
        [up_half.reshape(-1, 512), core_half(w_down, 0), core_half(w_out, 0)], axis=0
    )
    x_prev, x_next = halo(inputs, "wide")
    qkv_mine = gather_pieces(qkv_half, "narrow")[1:]
    pack_mine = gather_pieces(small, "narrow")[1:]
    qkv_got = [swap(p, "wide", 1) for p in qkv_mine]
    def whole_of(mine, got):
        first = jnp.where(core == 0, mine, got)
        second = jnp.where(core == 0, got, mine)
        return jnp.concatenate([first, second], axis=0)

    pieces = [w_qkv] + [
        whole_of(m, g).reshape(width, 3, head_cols) for m, g in zip(qkv_mine, qkv_got)
    ]
    cut = narrow // 2
    w0, w1 = (
        (p[0] if len(p) == 1 else jnp.concatenate(p, axis=2)).reshape(width, 3 * GROUP_COLS)
        for p in (pieces[:cut], pieces[cut:])
    )

    id_rim = jnp.full((samp,), -1, jnp.int32)
    padded_ids = jnp.concatenate([id_rim, segment_ids, id_rim])
    window_ids = lax.dynamic_slice_in_dim(padded_ids, plan.me * samp, 3 * samp, 0)
    id_col = window_ids[:, None]
    id_row = jnp.tile(window_ids.reshape(3, samp), (1, HEADS_PER_GROUP))
    gain1, shift1 = norm1_gain[None, :], norm1_shift[None, :]
    gain2, shift2 = norm2_gain[None, :], norm2_shift[None, :]
    sources, targets = plan.sources(), plan.targets()
    short_sources, short_targets = short.sources(), short.targets()

    def whole(a):
        return pl.BlockSpec(a.shape, lambda i: (0,) * a.ndim, pipeline_mode=pl.Buffered(1))

    cube = pl.BlockSpec((group, samp, width), lambda i: (i, 0, 0))
    smem = pl.BlockSpec(memory_space=pltpu.SMEM)
    line = pl.BlockSpec((1, width), lambda i: (0, 0))
    vec = jax.ShapeDtypeStruct((1, width), F32)

    def tok(dtype):
        return jax.ShapeDtypeStruct((tokens, width), dtype)

    def cost(flops, size):
        return pl.CostEstimate(flops=flops, bytes_accessed=size, transcendentals=0)

    qkv_block = pl.BlockSpec((2, 3, rows, 3 * GROUP_COLS), lambda i: (0, 0, i, 0))

    args = [id_col, id_row, x_prev, inputs, x_next, w0, w1, gain1, shift1]
    qkv, attended = pl.pallas_call(
        attn_fwd_kernel,
        grid=(steps,),
        in_specs=[whole(id_col), whole(id_row), cube, cube, cube]
        + [whole(a) for a in (w0, w1, gain1, shift1)],
        out_specs=[qkv_block, cube],
        out_shape=[
            jax.ShapeDtypeStruct((2, 3, tokens, 3 * GROUP_COLS), BF16),
            jax.ShapeDtypeStruct((feats, samp, width), BF16),
        ],
        cost_estimate=cost(6 * 10**9, 24 << 20),
        name="attn_fwd",
    )(*args)
    attended, *pack_mine = tied(attended, *pack_mine)
    pack_got = [swap(p, "wide", 1) for p in pack_mine]

    x_flat = inputs.reshape(tokens, width)
    cot_flat = cotangent.reshape(tokens, width)
    att_flat = attended.reshape(tokens, width)
    packs = [a for pair in zip(pack_mine, pack_got) for a in pair]
    args = [sources, x_flat, att_flat, cot_flat, gain2, shift2, w_up, w_down, w_out]
    if inpack:
        args += packs
    else:
        up_rows = width * slot // 512
        args += [p[up_rows:] for p in packs]
        args += [p[:up_rows].reshape(width, slot) for p in packs]
    if ordered:
        size = blocks * (2 * n_ff + n_out)
        sums = [(size, 512)] * 2
    else:
        sums = [(ff, width), (ff, width), (width, width)]
    outs = [tok(BF16), tok(F32), tok(BF16), vec, vec]
    outs += [jax.ShapeDtypeStruct(s, BF16) for s in sums]
    scratch = [
        ((width, width), BF16), ((width, unit), BF16), ((unit, width), BF16),
        ((width, unit), BF16), ((unit, width), BF16),
        ((tokens, width), F32), ((tokens, width), BF16), ((tokens, width), F32), ((tokens, width), F32),
        ((tokens, unit), BF16), ((tokens, unit), BF16), ((tokens, unit), BF16), ((tokens, unit), BF16),
        ((tokens, width), BF16),
        ((ff, width), BF16), ((ff, width), BF16), ((width, width), BF16),
    ]
    block_out, hidden_grad, dattended, gain2_grad, shift2_grad, *packed = pl.pallas_call(
        functools.partial(chain_kernel, narrow - 1, inpack, ordered),
        grid=(narrow * slot // unit + 1,),
        in_specs=[smem] + [whole(a) for a in args[1:]],
        out_specs=[whole(o) for o in outs],
        out_shape=outs,
        scratch_shapes=[pltpu.VMEM(*s) for s in scratch],
        cost_estimate=cost(15 * 10**9, 20 << 20),
        name="chain",
    )(*args)

    def arranged(natural, sources):
        flat = natural.reshape(narrow * wide, natural.shape[2], 512)
        places = sources[1:].reshape(2, blocks)
        return [jnp.take(flat, places[s], axis=0).reshape(-1, 512) for s in range(2)]

    if not ordered:
        down, up, out = (p.reshape(narrow, wide, -1, 512) for p in packed)
        packed = arranged(jnp.concatenate([down, up, out], axis=2), sources)
    big = Reduction(plan, packed[0], packed[1])

    datt = dattended.reshape(feats, samp, width)
    d_prev, d_next = halo(datt, "wide")
    big.advance()

    def pair_block(cols):
        return pl.BlockSpec((2, rows, cols), lambda i: (0, i, 0))

    dq, dkv_own = pl.pallas_call(
        attn_bwd_own_kernel,
        grid=(steps,),
        in_specs=[whole(id_col), whole(id_row), qkv_block, cube],
        out_specs=[pair_block(GROUP_COLS), pair_block(2 * GROUP_COLS)],
        out_shape=[
            jax.ShapeDtypeStruct((2, tokens, GROUP_COLS), BF16),
            jax.ShapeDtypeStruct((2, tokens, 2 * GROUP_COLS), F32),
        ],
        cost_estimate=cost(10 * 10**9, 14 << 20),
        name="attn_bwd_own",
    )(id_col, id_row, qkv, datt)
    dkv, near = dkv_own, None
    for h in range(2):
        off = h * (steps // 2)

        def shifted(spec, off=off):
            return pl.BlockSpec(spec.block_shape, lambda i: spec.index_map(i + off))

        dkv = hold(dkv, big)
        big.advance()
        args = [id_col, id_row, qkv, d_prev, d_next, dkv_own if h else dkv]
        specs = [whole(id_col), whole(id_row)]
        specs += [shifted(b) for b in (qkv_block, cube, cube, pair_block(2 * GROUP_COLS))]
        if h:
            args.append(dkv)
            specs.append(pl.BlockSpec(memory_space=pl.ANY))
        dkv = pl.pallas_call(
            attn_bwd_near_kernel,
            grid=(steps // 2,),
            in_specs=specs,
            out_specs=shifted(pair_block(2 * GROUP_COLS)),
            out_shape=jax.ShapeDtypeStruct((2, tokens, 2 * GROUP_COLS), BF16),
            input_output_aliases={6: 0} if h else {},
            cost_estimate=cost(5 * 10**9, 7 << 20),
            name=f"attn_bwd_near_{h}",
        )(*args)
    dkv = hold(dkv, big)
    big.advance()

    natural = (6 * GROUP_COLS, width)
    outs = [jax.ShapeDtypeStruct((blocks * n_qkv, 512), BF16)] * 2
    if not ordered:
        outs = [jax.ShapeDtypeStruct(natural, BF16)]
    args = [short_sources, x_flat, dq, dkv, gain1, shift1]
    packed = pl.pallas_call(
        functools.partial(qkv_grad_kernel, ordered),
        grid=(1,),
        in_specs=[smem] + [whole(a) for a in args[1:]],
        out_specs=[whole(o) for o in outs],
        out_shape=outs,
        scratch_shapes=[pltpu.VMEM((tokens, width), BF16), pltpu.VMEM(natural, BF16)],
        cost_estimate=cost(2 * 10**9, 6 << 20),
        name="qkv_grad",
    )(*args)
    if not ordered:
        turned = packed[0].reshape(2, 3, narrow // 2, head_cols, width).transpose(0, 2, 1, 3, 4)
        packed = arranged(turned.reshape(narrow, wide, n_qkv, width), short_sources)
    *packed, dkv = hold([*packed, dkv], big)
    big.advance()
    last = Reduction(short, packed[0], packed[1])
    last.advance()

    flat = pl.BlockSpec((CHUNK, width), lambda i: (i, 0))
    input_grad, gain1_grad, shift1_grad = pl.pallas_call(
        input_grad_kernel,
        grid=(tokens // CHUNK,),
        in_specs=[flat, flat]
        + [pl.BlockSpec((2, CHUNK, n * GROUP_COLS), lambda i: (0, i, 0)) for n in (1, 2)]
        + [whole(a) for a in (w0, w1, gain1)],
        out_specs=[flat, line, line],
        out_shape=[tok(F32), vec, vec],
        cost_estimate=cost(2 * 10**9, 8 << 20),
        name="input_grad",
    )(x_flat, hidden_grad, dq, dkv, w0, w1, gain1)
    norms = SmallSum(jnp.concatenate([gain1_grad, shift1_grad, gain2_grad, shift2_grad], axis=0))

    lockstep(last, big, norms)
    lockstep(last, norms)
    lockstep(last, big, norms)
    lockstep(last, big, norms)
    lockstep(last, norms)
    lockstep(last, big, norms)
    for _ in range(9):
        lockstep(last, big, norms)
    down_rows, out_rows, qkv_rows = own_ff, w_out.shape[0], 3 * head_cols
    if ordered:
        shapes = [jax.ShapeDtypeStruct(s, F32) for s in (w_up.shape, w_down.shape, w_out.shape)]
        up_grad, down_grad, out_grad = pl.pallas_call(
            functools.partial(ffn_out_kernel, n_ff, n_out),
            grid=(1,),
            in_specs=[smem] + [whole(a) for a in big.result],
            out_specs=[whole(s) for s in shapes],
            out_shape=shapes,
            scratch_shapes=[pltpu.VMEM((own_ff, width), F32)],
            cost_estimate=cost(0, 8 << 20),
            name="ffn_out",
        )(targets, *big.result)
    if ordered:
        shape = jax.ShapeDtypeStruct((3, width, head_cols), F32)
        qkv_grad = pl.pallas_call(
            qkv_out_kernel,
            grid=(1,),
            in_specs=[smem] + [whole(a) for a in last.result],
            out_specs=whole(shape),
            out_shape=shape,
            scratch_shapes=[pltpu.VMEM((qkv_rows, width), F32)],
            cost_estimate=cost(0, 3 << 20),
            name="qkv_out",
        )(short_targets, *last.result)
        qkv_grad = qkv_grad.transpose(1, 0, 2)
    else:

        def natural_rows(pair, targets):
            both = jnp.concatenate(pair, axis=0).reshape(wide, -1, 512)
            places = jnp.zeros((wide,), jnp.int32).at[targets].set(jnp.arange(wide, dtype=jnp.int32))
            return jnp.take(both, places, axis=0).astype(F32)

        full = natural_rows(big.result, targets)
        down_grad = full[:, :n_ff].reshape(w_down.shape)
        up_grad = full[:, n_ff : 2 * n_ff].reshape(own_ff, width).T
        out_grad = full[:, 2 * n_ff :].reshape(w_out.shape)
        qkv_grad = natural_rows(last.result, short_targets).reshape(qkv_rows, width).T.reshape(width, 3, head_cols)
    norm_sums = norms.operands[0]
    return (
        block_out.reshape(feats, samp, width),
        input_grad.reshape(feats, samp, width),
        norm_sums[0],
        norm_sums[1],
        qkv_grad,
        out_grad,
        norm_sums[2],
        norm_sums[3],
        up_grad,
        down_grad,
    )


def solution(mesh):
    rows = P("narrow", "wide", None)
    placed = (
        rows, P(), P(), P(), P(None, None, "narrow"), P("narrow", None),
        P(), P(), P(None, "narrow"), P("narrow", None), rows,
    )
    outs = (
        rows, rows, P(), P(), P(None, None, "narrow"), P("narrow", None),
        P(), P(), P(None, "narrow"), P("narrow", None),
    )
    return jax.shard_map(local, mesh=mesh, in_specs=placed, out_specs=outs, check_vma=False)
```

```python
import functools

import jax
import jax.numpy as jnp
import numpy as np
from jax import lax
from jax.experimental import pallas as pl
from jax.experimental.pallas import tpu as pltpu
from jax.sharding import PartitionSpec as P

HEAD_DIM = 64
HEADS_PER_GROUP = 4
GROUP_COLS = HEAD_DIM * HEADS_PER_GROUP
EPS = 1e-05
SCALE = HEAD_DIM ** (-0.5)
F32 = jnp.float32
BF16 = jnp.bfloat16
NEG = -1e30
CHUNK = 256
RHYTHM = (1, 0, 1, 1, 0)


def dot_nn(a, b):
    return lax.dot_general(a, b, (((1,), (0,)), ((), ())), preferred_element_type=F32)


def dot_nt(a, b):
    return lax.dot_general(a, b, (((1,), (1,)), ((), ())), preferred_element_type=F32)


def dot_tn(a, b):
    return lax.dot_general(a, b, (((0,), (0,)), ((), ())), preferred_element_type=F32)


def norm_parts(z):
    mean = jnp.mean(z, axis=-1, keepdims=True)
    centred = z - mean
    var = jnp.mean(centred * centred, axis=-1, keepdims=True)
    rstd = lax.rsqrt(var + EPS)
    return centred * rstd, rstd


def norm_back(grad, xhat, rstd, gain):
    gg = grad * gain
    m1 = jnp.mean(gg, axis=-1, keepdims=True)
    m2 = jnp.mean(gg * xhat, axis=-1, keepdims=True)
    return rstd * (gg - m1 - xhat * m2)


def lane_head(rows, dtype):
    lane = lax.broadcasted_iota(jnp.int32, (rows, GROUP_COLS), 1)
    return [
        ((lane >= h * HEAD_DIM) & (lane < (h + 1) * HEAD_DIM)).astype(F32).astype(dtype)
        for h in range(HEADS_PER_GROUP)
    ]


def block_diag(rows, masks):
    return jnp.concatenate([rows * m for m in masks], axis=0)


def pick_heads(full, rows):
    low = lax.broadcasted_iota(jnp.int32, (rows, 2 * HEAD_DIM), 1) < HEAD_DIM
    out = []
    for pair in range(HEADS_PER_GROUP // 2):
        cols = slice(2 * pair * HEAD_DIM, 2 * (pair + 1) * HEAD_DIM)
        at = 2 * pair * rows
        out.append(jnp.where(low, full[at : at + rows, cols], full[at + rows : at + 2 * rows, cols]))
    return jnp.concatenate(out, axis=1)


def rows_at(index, size):
    return pl.ds(pl.multiple_of(index * size, size), size)


def staged(count, first, second, third, lag=2):
    a, b = {}, {}
    for t in range(count + lag):
        if t < count:
            a[t] = first(t)
        if 0 <= t - 1 < count:
            b[t - 1] = second(t - 1, *a.pop(t - 1))
        if 0 <= t - lag < count:
            third(t - lag, *b.pop(t - lag))


def each(count, body, unroll=1):
    lax.fori_loop(0, count, lambda i, carry: (body(i), carry)[1], 0, unroll=unroll)


def own_kernel(xo, w0, w1, gain, shift, own_ref, normed_ref):
    xhat, _ = norm_parts(xo[...].astype(F32))
    normed = (xhat * gain[...] + shift[...]).astype(BF16)
    normed_ref[...] = normed
    for hg, w in enumerate((w0, w1)):
        own_ref[hg] = dot_nn(normed, w[...]).astype(BF16)


def attn_fwd_kernel(idc, idr, xp, own, xn, w0, w1, gain, shift, qkv_ref, att_ref):
    feats, samp, width = xp.shape
    rows = feats * samp
    x = jnp.concatenate(
        [xp[...].reshape(rows, width), xn[...].reshape(rows, width)], axis=0
    ).astype(F32)
    xhat, _ = norm_parts(x)
    normed = (xhat * gain[...] + shift[...]).astype(BF16)
    for hg, w in enumerate((w0, w1)):
        qkv = dot_nn(normed, w[...]).astype(BF16)
        qkv_ref[hg, 0] = qkv[:rows]
        qkv_ref[hg, 1] = own[hg]
        qkv_ref[hg, 2] = qkv[rows:]
    allowed = idc[...] == idr[1:2, :]
    m16 = lane_head(1, BF16)
    q16 = [m * SCALE for m in m16]

    def first(i):
        f, hg = i // 2, i % 2
        sl = slice(f * samp, (f + 1) * samp)
        k, _ = bwd_pieces(qkv_ref, hg, sl)
        return (dot_nt(k, block_diag(qkv_ref[hg, 1, sl, 0:GROUP_COLS], q16)),)

    def second(i, s):
        s = jnp.where(allowed, s, NEG)
        top = jnp.max(s, axis=0, keepdims=True)
        e = jnp.exp(s - top)
        total = jnp.sum(e, axis=0, keepdims=True)
        return ((e * (1.0 / total)).astype(BF16),)

    def third(i, p):
        f, hg = i // 2, i % 2
        _, v = bwd_pieces(qkv_ref, hg, slice(f * samp, (f + 1) * samp))
        o = pick_heads(dot_tn(p, v), samp)
        att_ref[f, :, hg * GROUP_COLS : (hg + 1) * GROUP_COLS] = o.astype(BF16)

    staged(2 * feats, first, second, third, 1)


def phi_parts(u):
    e = jnp.exp(-0.5 * (u * u))
    t = 1.0 / (1.0 + (0.3275911 * 0.7071067811865476) * jnp.abs(u))
    poly = t * (
        0.127414796
        + t * (-0.142248368 + t * (0.7107068705 + t * (-0.7265760135 + t * 0.5307027145)))
    )
    tail = poly * e
    cdf = jnp.where(u < 0, tail, 1.0 - tail)
    return cdf, u * (e * 0.3989422804014327)


def chain_kernel(others, inpack, ordered, *refs):
    table, x, att, cot, gain, shift, up_own, down_own, out_own = refs[:9]
    refs = refs[9:]
    packs, refs = refs[: 2 * others], refs[2 * others :]
    if inpack:
        extra = packs
    else:
        extra, refs = refs[: 2 * others], refs[2 * others :]
    count = 2 if ordered else 3
    out_ref, hgrad_ref, dat_ref, g2_ref, s2_ref = refs[:5]
    packed, refs = refs[5 : 5 + count], refs[5 + count :]
    (wo, up_a, down_a, up_b, down_b, hidden, normed, mlp, dn2) = refs[:9]
    act_a, pre_a, act_b, pre_b, res, gd, gu, go = refs[9:]
    tokens, width = x.shape
    unit = up_a.shape[1]
    slot = up_own.shape[1] // 2
    per = slot // unit
    last = (2 * others + 2) * per // 2
    narrow_rows = out_own.shape[0]
    half_rows = narrow_rows // 2
    chunks = tokens // CHUNK
    step = pl.program_id(0)
    core = table[0]

    def bases(unit):
        for j in range(1, others + 1):
            yield 2 * j - 2, 2 * j + core
            yield 2 * j - 1, 2 * j + 1 - core

    @pl.when(step == 0)
    def _():
        wo[:narrow_rows] = out_own[...]
        for i, base in bases(half_rows):
            wo[rows_at(base, half_rows)] = packs[i][2 * slot : 2 * slot + half_rows] if inpack else packs[i][slot : slot + half_rows]
        g2_ref[...] = jnp.zeros_like(g2_ref)
        s2_ref[...] = jnp.zeros_like(s2_ref)
        for ref in (act_b, pre_b, up_b, down_b):
            ref[...] = jnp.zeros_like(ref)

        def start(i):
            sl = rows_at(i, CHUNK)
            h = x[sl].astype(F32) + dot_nn(att[sl], wo[...])
            hidden[sl] = h
            xhat, _ = norm_parts(h)
            normed[sl] = (xhat * gain[...] + shift[...]).astype(BF16)
            mlp[sl] = jnp.zeros((CHUNK, width), F32)
            dn2[sl] = jnp.zeros((CHUNK, width), F32)

        each(chunks, start)

    def load(parity, up, down):
        for pair in range(last):

            @pl.when(step == pair)
            def _():
                i, sub = divmod(2 * pair + parity, per)
                low, high = sub * unit, (sub + 1) * unit
                if i < 2:
                    low, high = low + i * slot, high + i * slot
                    up[...] = up_own[:, low:high]
                    down[...] = down_own[low:high]
                elif inpack:
                    up[...] = packs[i - 2][:slot, low:high]
                    down[...] = packs[i - 2][slot + low : slot + high]
                else:
                    up[...] = extra[i - 2][:, low:high]
                    down[...] = packs[i - 2][low:high]

    def place(item):
        i, sub = item // per, item % per
        swapped = jnp.where(i % 2 == 0, core, 1 - core)
        base = jnp.where(i < 2, i, i - i % 2 + swapped)
        return rows_at(base * per + sub, unit)

    def spread(item, up, down, act, pre):
        at = place(item)
        half = width // 2
        for i in range(chunks):
            sl = slice(i * CHUNK, (i + 1) * CHUNK)
            mlp[sl] += dot_nn(act[sl], down[...])
            dn2[sl] += dot_nt(pre[sl], up[...])
            for j in range(i, 4, chunks):
                cols = slice((j % 2) * half, (j % 2 + 1) * half)
                if j < 2:
                    gd[at, cols] = dot_tn(act[...], cot[:, cols]).astype(BF16)
                else:
                    gu[at, cols] = dot_tn(pre[...], normed[:, cols]).astype(BF16)
            yield

    def phase(up, down, act, pre, *before):
        rest = spread(*before)
        ready = {}
        for i in range(chunks + 1):
            if i < chunks:
                sl = slice(i * CHUNK, (i + 1) * CHUNK)
                ready[i] = dot_nn(normed[sl], up[...]), dot_nt(cot[sl], down[...])
            if i > 0:
                next(rest)
                u, back = ready.pop(i - 1)
                sl = slice((i - 1) * CHUNK, i * CHUNK)
                cdf, upd = phi_parts(u)
                act[sl] = (u * cdf).astype(BF16)
                pre[sl] = (back * (cdf + upd)).astype(BF16)

    load(0, up_a, down_a)

    @pl.when(step < last)
    def _():
        before = jnp.maximum(2 * step - 1, 0)
        phase(up_a, down_a, act_a, pre_a, before, up_b, down_b, act_b, pre_b)

    load(1, up_b, down_b)

    @pl.when(step < last)
    def _():
        phase(up_b, down_b, act_b, pre_b, 2 * step, up_a, down_a, act_a, pre_a)

    @pl.when(step == last)
    def _():
        for _ in spread(2 * last - 1, up_b, down_b, act_b, pre_b):
            pass

        def finish(i):
            sl = rows_at(i, CHUNK)
            h = hidden[sl]
            out_ref[sl] = (h + mlp[sl]).astype(BF16)
            xhat, rstd = norm_parts(h)
            d = dn2[sl]
            g2_ref[...] += jnp.sum(d * xhat, axis=0, keepdims=True)
            s2_ref[...] += jnp.sum(d, axis=0, keepdims=True)
            hgrad = cot[sl].astype(F32) + norm_back(d, xhat, rstd, gain[...])
            hgrad_ref[sl] = hgrad
            r = hgrad.astype(BF16)
            res[sl] = r
            dat_ref[sl] = dot_nt(r, wo[...]).astype(BF16)

        each(chunks, finish)
        go[...] = dot_tn(att[...], res[...]).astype(BF16)
        if ordered:
            blocks = (table.shape[0] - 1) // 2
            n_ff = gd.shape[0] // (2 * blocks)
            n_out = go.shape[0] // (2 * blocks)
            size = 2 * n_ff + n_out
            for side in range(2):
                for b in range(blocks):
                    src = table[1 + side * blocks + b]
                    ref = packed[side]
                    ref[b * size : b * size + n_ff] = gd[rows_at(src, n_ff)]
                    ref[b * size + n_ff : b * size + 2 * n_ff] = gu[rows_at(src, n_ff)]
                    ref[b * size + 2 * n_ff : (b + 1) * size] = go[rows_at(src, n_out)]
        else:
            packed[0][...] = gd[...]
            packed[1][...] = gu[...]
            packed[2][...] = go[...]


def bwd_pieces(qkv_ref, hg, sl):
    k = jnp.concatenate(
        [qkv_ref[hg, w, sl, GROUP_COLS : 2 * GROUP_COLS] for w in range(3)], axis=0
    )
    v = jnp.concatenate(
        [qkv_ref[hg, w, sl, 2 * GROUP_COLS : 3 * GROUP_COLS] for w in range(3)], axis=0
    )
    return k, v


def head_rows(a):
    return jnp.concatenate(
        [a[:, h * HEAD_DIM : (h + 1) * HEAD_DIM] for h in range(HEADS_PER_GROUP)], axis=0
    )


def score_grads(s, dp, mask):
    s = jnp.where(mask, s, NEG)
    top = jnp.max(s, axis=0, keepdims=True)
    e = jnp.exp(s - top)
    total = jnp.sum(e, axis=0, keepdims=True)
    p = e * (1.0 / total)
    pd = p * dp
    delta = jnp.sum(pd, axis=0, keepdims=True)
    return (pd - p * delta).astype(BF16), p


def attn_bwd_own_kernel(idc, idr, qkv_ref, do_ref, dq_ref, dkv_ref):
    feats, samp, width = do_ref.shape
    m16 = lane_head(1, BF16)
    q16 = [m * SCALE for m in m16]
    mask = idc[...] == idr[1:2, :]

    def pieces(i):
        f, hg = i // 2, i % 2
        sl = slice(f * samp, (f + 1) * samp)
        q = qkv_ref[hg, 1, sl, 0:GROUP_COLS]
        d = do_ref[f, :, hg * GROUP_COLS : (hg + 1) * GROUP_COLS]
        return hg, sl, q, d

    def first(i):
        hg, sl, q, d = pieces(i)
        k, v = bwd_pieces(qkv_ref, hg, sl)
        return dot_nt(k, block_diag(q, q16)), dot_nt(v, block_diag(d, m16))

    def second(i, s, dp):
        ds, p = score_grads(s, dp, mask)
        own = slice(samp, 2 * samp)
        return ds, head_rows(ds[own]), head_rows(p[own].astype(BF16))

    def third(i, ds, dss, ps):
        hg, sl, q, d = pieces(i)
        k, _ = bwd_pieces(qkv_ref, hg, sl)
        dq_ref[hg, sl, :] = (pick_heads(dot_tn(ds, k), samp) * SCALE).astype(BF16)
        dkv_ref[hg, sl, 0:GROUP_COLS] = pick_heads(dot_nn(dss, q), samp)
        dkv_ref[hg, sl, GROUP_COLS : 2 * GROUP_COLS] = pick_heads(dot_nn(ps, d), samp)

    staged(2 * feats, first, second, third)


def attn_bwd_near_kernel(idc, idr, qkv_ref, dp_ref, dn_ref, sum_ref, *rest):
    dkv_ref = rest[-1]
    feats, samp, width = dp_ref.shape
    m16 = lane_head(1, BF16)
    q16 = [m * SCALE for m in m16]
    near = ((0, 0, dp_ref), (2, 1, dn_ref))
    masks = [idc[a * samp : (a + 2) * samp, :] == idr[g : g + 1, :] for g, a, _ in near]

    def pieces(i, side):
        f, hg = i // 2, i % 2
        sl = slice(f * samp, (f + 1) * samp)
        g, a, ref = near[side]
        q = qkv_ref[hg, g, sl, 0:GROUP_COLS]
        d = ref[f, :, hg * GROUP_COLS : (hg + 1) * GROUP_COLS]
        return hg, sl, slice(a * samp, (a + 2) * samp), q, d

    def first(i):
        out = []
        for side in range(2):
            hg, sl, span, q, d = pieces(i, side)
            k, v = bwd_pieces(qkv_ref, hg, sl)
            out += [dot_nt(k[span], block_diag(q, q16)), dot_nt(v[span], block_diag(d, m16))]
        return out

    def second(i, s0, dp0, s1, dp1):
        dss, ps = [], []
        for side, (s, dp) in enumerate(((s0, dp0), (s1, dp1))):
            ds, p = score_grads(s, dp, masks[side])
            own = slice((1 - side) * samp, (2 - side) * samp)
            dss.append(head_rows(ds[own]))
            ps.append(head_rows(p[own].astype(BF16)))
        return jnp.concatenate(dss, axis=1), jnp.concatenate(ps, axis=1)

    def third(i, dss, ps):
        hg, sl, _, q0, d0 = pieces(i, 0)
        _, _, _, q1, d1 = pieces(i, 1)
        low, high = slice(0, GROUP_COLS), slice(GROUP_COLS, 2 * GROUP_COLS)
        dk = pick_heads(dot_nn(dss, jnp.concatenate([q0, q1], axis=0)), samp)
        dv = pick_heads(dot_nn(ps, jnp.concatenate([d0, d1], axis=0)), samp)
        dkv_ref[hg, sl, low] = ((dk + sum_ref[hg, sl, low]) * SCALE).astype(BF16)
        dkv_ref[hg, sl, high] = (dv + sum_ref[hg, sl, high]).astype(BF16)

    staged(2 * feats, first, second, third)


def qkv_grad_kernel(ordered, table, normed, dq, dkv, *refs):
    outs, gq = refs[:-1], refs[-1]
    hg = pl.program_id(0)
    gq[rows_at(3 * hg, GROUP_COLS)] = dot_tn(dq[0], normed[...]).astype(BF16)
    for j in range(2):
        cols = slice(j * GROUP_COLS, (j + 1) * GROUP_COLS)
        gq[rows_at(3 * hg + 1 + j, GROUP_COLS)] = dot_tn(dkv[0, :, cols], normed[...]).astype(BF16)

    @pl.when(hg == 1)
    def _():
        arrange_qkv(ordered, table, outs, gq)


def arrange_qkv(ordered, table, outs, gq):
    if ordered:
        blocks = (table.shape[0] - 1) // 2
        size = gq.shape[0] // (2 * blocks)
        for side in range(2):
            for b in range(blocks):
                outs[side][b * size : (b + 1) * size] = gq[rows_at(table[1 + side * blocks + b], size)]
    else:
        outs[0][...] = gq[...]


def input_grad_kernel(x, hgrad, dq, dkv, w0, w1, gain, igrad_ref, g1_ref, s1_ref):
    xhat, rstd = norm_parts(x[...].astype(F32))
    dn1 = dot_nt(dq[0], w0[:, :GROUP_COLS]) + dot_nt(dq[1], w1[:, :GROUP_COLS])
    dn1 = dn1 + dot_nt(dkv[0], w0[:, GROUP_COLS:]) + dot_nt(dkv[1], w1[:, GROUP_COLS:])

    @pl.when(pl.program_id(0) == 0)
    def _():
        g1_ref[...] = jnp.zeros_like(g1_ref)
        s1_ref[...] = jnp.zeros_like(s1_ref)

    g1_ref[...] += jnp.sum(dn1 * xhat, axis=0, keepdims=True)
    s1_ref[...] += jnp.sum(dn1, axis=0, keepdims=True)
    igrad_ref[...] = hgrad[...] + norm_back(dn1, xhat, rstd, gain[...])


def ffn_out_kernel(n_ff, n_out, table, mine, got, up_ref, down_ref, out_ref, turned):
    size = 2 * n_ff + n_out
    blocks = mine.shape[0] // size
    for side, ref in enumerate((mine, got)):
        for b in range(blocks):
            to = table[side * blocks + b]
            down_ref[rows_at(to, n_ff)] = ref[b * size : b * size + n_ff].astype(F32)
            turned[rows_at(to, n_ff)] = ref[b * size + n_ff : b * size + 2 * n_ff].astype(F32)
            out_ref[rows_at(to, n_out)] = ref[b * size + 2 * n_ff : (b + 1) * size].astype(F32)
    up_ref[...] = turned[...].T


def qkv_out_kernel(table, mine, got, out_ref, turned):
    blocks = table.shape[0] // 2
    size = mine.shape[0] // blocks
    for side, ref in enumerate((mine, got)):
        for b in range(blocks):
            turned[rows_at(table[side * blocks + b], size)] = ref[b * size : (b + 1) * size].astype(F32)
    for j in range(3):
        cols = turned.shape[0] // 3
        out_ref[j] = turned[j * cols : (j + 1) * cols].T


def swap(x, axis, bit):
    count = lax.axis_size(axis)
    return lax.ppermute(x, axis, [(i, i ^ bit) for i in range(count)])


def halo(x, axis):
    count = lax.axis_size(axis)
    prev = lax.ppermute(x, axis, [(i, i + 1) for i in range(count - 1)])
    nxt = lax.ppermute(x, axis, [(i + 1, i) for i in range(count - 1)])
    return prev, nxt


def gather_pieces(x, axis):
    pieces = [x]
    bit = 1
    while bit < lax.axis_size(axis):
        pieces = pieces + [swap(p, axis, bit) for p in pieces]
        bit *= 2
    return pieces


def tied(*arrays):
    return lax.optimization_barrier(arrays)


class Plan:

    def __init__(self, wide, narrow, fours=False):
        self.wide, self.narrow, self.fours = wide, narrow, fours
        nb = [("narrow", 1 << i) for i in range(narrow.bit_length() - 1)][::-1]
        wb = [("wide", 1 << i) for i in range(1, wide.bit_length() - 1)]
        first = nb + wb
        second = wb[:1] + nb + wb[1:] if fours else wb[1:2] + nb + wb[:1] + wb[2:]
        self.orders = (first, second)
        self.steps = len(first)
        self.blocks = 1 << self.steps
        self.back = [[s for s in o if s[0] == "wide"][::-1] for o in self.orders]
        self.me = lax.axis_index("wide")
        self.core = self.me % 2

    def rel(self, order):
        j = np.zeros(self.blocks, np.int32)
        r = np.zeros(self.blocks, np.int32)
        for s, (axis, bit) in enumerate(order):
            has = (np.arange(self.blocks) >> (self.steps - 1 - s)) & 1
            if axis == "narrow":
                j += has * bit
            else:
                r += has * bit
        return j, r

    def by_core(self, a, b):
        return jnp.where(self.core == 0, jnp.asarray(a, jnp.int32), jnp.asarray(b, jnp.int32))

    def sources(self):
        (j0, r0), (j1, r1) = (self.rel(o) for o in self.orders)
        high = self.me - self.core
        n0, n1 = j0 * self.wide, j1 * self.wide
        mine = self.by_core(n0, n1) + (self.by_core(r0, r1) ^ high) + self.core
        send = self.by_core(n1, n0) + (self.by_core(r1, r0) ^ high) + 1 - self.core
        return jnp.concatenate([self.core[None], mine, send]).astype(jnp.int32)

    def targets(self):
        rels = []
        for o in self.orders:
            j, r = self.rel(o)
            rels.append(r[j == 0])
        high = self.me - self.core
        mine = (self.by_core(rels[0], rels[1]) ^ high) + self.core
        got = (self.by_core(rels[1], rels[0]) ^ high) + 1 - self.core
        return jnp.concatenate([mine, got]).astype(jnp.int32)

    def mixed(self, x, steps):
        pairs = []
        for w in range(self.wide):
            axis, bit = steps[w % 2]
            for n in range(self.narrow):
                to = (w, n ^ bit) if axis == "narrow" else (w ^ bit, n)
                pairs.append((w * self.narrow + n, to[0] * self.narrow + to[1]))
        return lax.ppermute(x, ("wide", "narrow"), pairs)


class Reduction:

    def __init__(self, plan, mine, send):
        self.plan, self.parts, self.operands, self.at = plan, [mine], [send], 0
        self.rows = mine.shape[0]
        self.work = self.stages()

    def total(self, low, high):
        out = self.parts[0][low:high].astype(F32)
        for p in self.parts[1:]:
            out = out + p[low:high].astype(F32)
        return out.astype(BF16)

    def around(self, operands):
        (_, high), (_, low) = self.plan.orders[0][-2:]
        bits = [low, high, high + low]
        return [swap(o, "wide", b) for o, b in zip(operands, bits)]

    def stages(self):
        plan, rows = self.plan, self.rows
        four = 2 if plan.fours else 0
        self.parts.append(swap(self.operands[0], "wide", 1))
        for at in range(plan.steps - four):
            self.operands = [self.total(rows >> (at + 1), rows >> at)]
            yield
            self.parts.append(plan.mixed(self.operands[0], [o[at] for o in plan.orders]))
        if four:
            size = rows >> plan.steps
            self.operands = [self.total(q * size, (q + 1) * size) for q in (1, 2, 3)]
            yield
            self.parts += self.around(self.operands)
        held = self.total(0, rows >> plan.steps)
        if four:
            self.operands = [held]
            yield
            held = jnp.concatenate([held] + self.around([self.operands[0]] * 3), axis=0)
        for at in range(four, len(plan.back[0])):
            self.operands = [held]
            yield
            got = plan.mixed(self.operands[0], [o[at] for o in plan.back])
            held = jnp.concatenate([self.operands[0], got], axis=0)
        self.operands = [held]
        yield
        self.result = (self.operands[0], swap(self.operands[0], "wide", 1))

    def advance(self):
        next(self.work, None)


def lockstep(*chains):
    if len(chains) > 1:
        held = tied([c.operands for c in chains])[0]
        for c, o in zip(chains, held):
            c.operands = list(o)
    for c in chains:
        c.advance()


def hold(value, chain):
    value, operands = tied(value, chain.operands)
    chain.operands = list(operands)
    return value


class SmallSum:
    def __init__(self, value):
        self.operands = [value]
        self.bits = [(a, 1 << i) for a in ("wide", "narrow") for i in range(lax.axis_size(a).bit_length() - 1)]

    def advance(self):
        if self.bits:
            (value,) = self.operands
            self.operands = [value + swap(value, *self.bits.pop(0))]


def local(
    inputs, segment_ids, norm1_gain, norm1_shift, w_qkv, w_out,
    norm2_gain, norm2_shift, w_up, w_down, cotangent,
):
    feats, samp, width = inputs.shape
    tokens = feats * samp
    narrow = lax.axis_size("narrow")
    wide = lax.axis_size("wide")
    plan, short = Plan(wide, narrow), Plan(wide, narrow, True)
    core = plan.core
    group = max(g for g in (1, 2, 4) if feats % (2 * g) == 0)
    steps = feats // group
    rows = group * samp
    head_cols = w_qkv.shape[2]
    own_ff = w_up.shape[1]
    slot = own_ff // 2
    ff = own_ff * narrow
    inpack = slot == 512
    unit = min(256, slot)
    n_ff, n_out, n_qkv = own_ff // wide, w_out.shape[0] // wide, 3 * head_cols // wide
    ordered = narrow == 2 and n_ff % 16 == 0 and n_out % 16 == 0 and n_qkv % 16 == 0
    blocks = plan.blocks

    def core_half(a, axis):
        size = a.shape[axis] // 2
        return lax.dynamic_slice_in_dim(a, core * size, size, axis)

    qkv_half = core_half(w_qkv.reshape(width, 3 * head_cols), 0)
    up_half = core_half(w_up, 1)
    small = jnp.concatenate(
        [up_half.reshape(-1, 512), core_half(w_down, 0), core_half(w_out, 0)], axis=0
    )
    x_prev, x_next = halo(inputs, "wide")
    qkv_mine = gather_pieces(qkv_half, "narrow")[1:]
    pack_mine = gather_pieces(small, "narrow")[1:]
    qkv_got = [swap(p, "wide", 1) for p in qkv_mine]
    def whole_of(mine, got):
        first = jnp.where(core == 0, mine, got)
        second = jnp.where(core == 0, got, mine)
        return jnp.concatenate([first, second], axis=0)

    pieces = [w_qkv] + [
        whole_of(m, g).reshape(width, 3, head_cols) for m, g in zip(qkv_mine, qkv_got)
    ]
    cut = narrow // 2
    w0, w1 = (
        (p[0] if len(p) == 1 else jnp.concatenate(p, axis=2)).reshape(width, 3 * GROUP_COLS)
        for p in (pieces[:cut], pieces[cut:])
    )

    id_rim = jnp.full((samp,), -1, jnp.int32)
    padded_ids = jnp.concatenate([id_rim, segment_ids, id_rim])
    window_ids = lax.dynamic_slice_in_dim(padded_ids, plan.me * samp, 3 * samp, 0)
    id_col = window_ids[:, None]
    id_row = jnp.tile(window_ids.reshape(3, samp), (1, HEADS_PER_GROUP))
    gain1, shift1 = norm1_gain[None, :], norm1_shift[None, :]
    gain2, shift2 = norm2_gain[None, :], norm2_shift[None, :]
    sources, targets = plan.sources(), plan.targets()
    short_sources, short_targets = short.sources(), short.targets()

    def whole(a):
        return pl.BlockSpec(a.shape, lambda i: (0,) * a.ndim, pipeline_mode=pl.Buffered(1))

    cube = pl.BlockSpec((group, samp, width), lambda i: (i, 0, 0))
    smem = pl.BlockSpec(memory_space=pltpu.SMEM)
    line = pl.BlockSpec((1, width), lambda i: (0, 0))
    vec = jax.ShapeDtypeStruct((1, width), F32)

    def tok(dtype):
        return jax.ShapeDtypeStruct((tokens, width), dtype)

    def cost(flops, size):
        return pl.CostEstimate(flops=flops, bytes_accessed=size, transcendentals=0)

    qkv_block = pl.BlockSpec((2, 3, rows, 3 * GROUP_COLS), lambda i: (0, 0, i, 0))

    own_block = pl.BlockSpec((2, rows, 3 * GROUP_COLS), lambda i: (0, i, 0))
    args = [w0, w1, gain1, shift1]
    own, normed_one = pl.pallas_call(
        own_kernel,
        grid=(steps,),
        in_specs=[pl.BlockSpec((rows, width), lambda i: (i, 0))] + [whole(a) for a in args],
        out_specs=[own_block, pl.BlockSpec((rows, width), lambda i: (i, 0))],
        out_shape=[jax.ShapeDtypeStruct((2, tokens, 3 * GROUP_COLS), BF16), tok(BF16)],
        cost_estimate=cost(2 * 10**9, 6 << 20),
        name="own_qkv",
    )(inputs.reshape(tokens, width), *args)
    args = [id_col, id_row, x_prev, own, x_next, w0, w1, gain1, shift1]
    qkv, attended = pl.pallas_call(
        attn_fwd_kernel,
        grid=(steps,),
        in_specs=[whole(id_col), whole(id_row), cube, own_block, cube]
        + [whole(a) for a in (w0, w1, gain1, shift1)],
        out_specs=[qkv_block, cube],
        out_shape=[
            jax.ShapeDtypeStruct((2, 3, tokens, 3 * GROUP_COLS), BF16),
            jax.ShapeDtypeStruct((feats, samp, width), BF16),
        ],
        cost_estimate=cost(6 * 10**9, 24 << 20),
        name="attn_fwd",
    )(*args)
    attended, *pack_mine = tied(attended, *pack_mine)
    pack_got = [swap(p, "wide", 1) for p in pack_mine]

    x_flat = inputs.reshape(tokens, width)
    cot_flat = cotangent.reshape(tokens, width)
    att_flat = attended.reshape(tokens, width)
    packs = [a for pair in zip(pack_mine, pack_got) for a in pair]
    args = [sources, x_flat, att_flat, cot_flat, gain2, shift2, w_up, w_down, w_out]
    if inpack:
        args += packs
    else:
        up_rows = width * slot // 512
        args += [p[up_rows:] for p in packs]
        args += [p[:up_rows].reshape(width, slot) for p in packs]
    if ordered:
        size = blocks * (2 * n_ff + n_out)
        sums = [(size, 512)] * 2
    else:
        sums = [(ff, width), (ff, width), (width, width)]
    outs = [tok(BF16), tok(F32), tok(BF16), vec, vec]
    outs += [jax.ShapeDtypeStruct(s, BF16) for s in sums]
    scratch = [
        ((width, width), BF16), ((width, unit), BF16), ((unit, width), BF16),
        ((width, unit), BF16), ((unit, width), BF16),
        ((tokens, width), F32), ((tokens, width), BF16), ((tokens, width), F32), ((tokens, width), F32),
        ((tokens, unit), BF16), ((tokens, unit), BF16), ((tokens, unit), BF16), ((tokens, unit), BF16),
        ((tokens, width), BF16),
        ((ff, width), BF16), ((ff, width), BF16), ((width, width), BF16),
    ]
    block_out, hidden_grad, dattended, gain2_grad, shift2_grad, *packed = pl.pallas_call(
        functools.partial(chain_kernel, narrow - 1, inpack, ordered),
        grid=(narrow * slot // unit + 1,),
        in_specs=[smem] + [whole(a) for a in args[1:]],
        out_specs=[whole(o) for o in outs],
        out_shape=outs,
        scratch_shapes=[pltpu.VMEM(*s) for s in scratch],
        cost_estimate=cost(15 * 10**9, 20 << 20),
        name="chain",
    )(*args)

    def arranged(natural, sources):
        flat = natural.reshape(narrow * wide, natural.shape[2], 512)
        places = sources[1:].reshape(2, blocks)
        return [jnp.take(flat, places[s], axis=0).reshape(-1, 512) for s in range(2)]

    if not ordered:
        down, up, out = (p.reshape(narrow, wide, -1, 512) for p in packed)
        packed = arranged(jnp.concatenate([down, up, out], axis=2), sources)
    big = Reduction(plan, packed[0], packed[1])

    datt = dattended.reshape(feats, samp, width)
    d_prev, d_next = halo(datt, "wide")
    big.advance()

    def pair_block(cols):
        return pl.BlockSpec((2, rows, cols), lambda i: (0, i, 0))

    dq, dkv_own = pl.pallas_call(
        attn_bwd_own_kernel,
        grid=(steps,),
        in_specs=[whole(id_col), whole(id_row), qkv_block, cube],
        out_specs=[pair_block(GROUP_COLS), pair_block(2 * GROUP_COLS)],
        out_shape=[
            jax.ShapeDtypeStruct((2, tokens, GROUP_COLS), BF16),
            jax.ShapeDtypeStruct((2, tokens, 2 * GROUP_COLS), F32),
        ],
        cost_estimate=cost(10 * 10**9, 14 << 20),
        name="attn_bwd_own",
    )(id_col, id_row, qkv, datt)
    dkv = dkv_own
    shares = [steps // 4, steps // 2, steps // 4] if steps % 4 == 0 else [1] * steps
    for h, share in enumerate(shares):
        off = sum(shares[:h])

        def shifted(spec, off=off):
            return pl.BlockSpec(spec.block_shape, lambda i: spec.index_map(i + off))

        dkv = hold(dkv, big)
        big.advance()
        args = [id_col, id_row, qkv, d_prev, d_next, dkv_own if h else dkv]
        specs = [whole(id_col), whole(id_row)]
        specs += [shifted(b) for b in (qkv_block, cube, cube, pair_block(2 * GROUP_COLS))]
        if h:
            args.append(dkv)
            specs.append(pl.BlockSpec(memory_space=pl.ANY))
        dkv = pl.pallas_call(
            attn_bwd_near_kernel,
            grid=(share,),
            in_specs=specs,
            out_specs=shifted(pair_block(2 * GROUP_COLS)),
            out_shape=jax.ShapeDtypeStruct((2, tokens, 2 * GROUP_COLS), BF16),
            input_output_aliases={6: 0} if h else {},
            cost_estimate=cost(2 * share * 10**9, share * 3 << 20),
            name=f"attn_bwd_near_{h}",
        )(*args)
    dkv = hold(dkv, big)
    big.advance()

    natural = (6 * GROUP_COLS, width)
    outs = [jax.ShapeDtypeStruct((blocks * n_qkv, 512), BF16)] * 2
    if not ordered:
        outs = [jax.ShapeDtypeStruct(natural, BF16)]
    args = [short_sources, normed_one, dq, dkv]
    packed = pl.pallas_call(
        functools.partial(qkv_grad_kernel, ordered),
        grid=(2,),
        in_specs=[smem, whole(normed_one)]
        + [pl.BlockSpec((1, tokens, n * GROUP_COLS), lambda i: (i, 0, 0)) for n in (1, 2)],
        out_specs=[whole(o) for o in outs],
        out_shape=outs,
        scratch_shapes=[pltpu.VMEM(natural, BF16)],
        cost_estimate=cost(2 * 10**9, 6 << 20),
        name="qkv_grad",
    )(*args)
    if not ordered:
        turned = packed[0].reshape(2, 3, narrow // 2, head_cols, width).transpose(0, 2, 1, 3, 4)
        packed = arranged(turned.reshape(narrow, wide, n_qkv, width), short_sources)
    *packed, dkv = hold([*packed, dkv], big)
    big.advance()
    last = Reduction(short, packed[0], packed[1])
    last.advance()

    flat = pl.BlockSpec((CHUNK, width), lambda i: (i, 0))
    input_grad, gain1_grad, shift1_grad = pl.pallas_call(
        input_grad_kernel,
        grid=(tokens // CHUNK,),
        in_specs=[flat, flat]
        + [pl.BlockSpec((2, CHUNK, n * GROUP_COLS), lambda i: (0, i, 0)) for n in (1, 2)]
        + [whole(a) for a in (w0, w1, gain1)],
        out_specs=[flat, line, line],
        out_shape=[tok(F32), vec, vec],
        cost_estimate=cost(2 * 10**9, 8 << 20),
        name="input_grad",
    )(x_flat, hidden_grad, dq, dkv, w0, w1, gain1)
    norms = SmallSum(jnp.concatenate([gain1_grad, shift1_grad, gain2_grad, shift2_grad], axis=0))

    for beside in RHYTHM:
        lockstep(*([last, big, norms] if beside else [last, norms]))
    while not hasattr(big, "result"):
        lockstep(last, big, norms)
    if not hasattr(last, "result"):
        big.result = hold(list(big.result), last)
    lockstep(last, norms)
    qkv_rows = 3 * head_cols
    if ordered:
        shapes = [jax.ShapeDtypeStruct(s, F32) for s in (w_up.shape, w_down.shape, w_out.shape)]
        up_grad, down_grad, out_grad = pl.pallas_call(
            functools.partial(ffn_out_kernel, n_ff, n_out),
            grid=(1,),
            in_specs=[smem] + [whole(a) for a in big.result],
            out_specs=[whole(s) for s in shapes],
            out_shape=shapes,
            scratch_shapes=[pltpu.VMEM((own_ff, width), F32)],
            cost_estimate=cost(0, 8 << 20),
            name="ffn_out",
        )(targets, *big.result)
    for _ in range(8):
        lockstep(last, norms)

    if ordered:
        shape = jax.ShapeDtypeStruct((3, width, head_cols), F32)
        qkv_grad = pl.pallas_call(
            qkv_out_kernel,
            grid=(1,),
            in_specs=[smem] + [whole(a) for a in last.result],
            out_specs=whole(shape),
            out_shape=shape,
            scratch_shapes=[pltpu.VMEM((qkv_rows, width), F32)],
            cost_estimate=cost(0, 3 << 20),
            name="qkv_out",
        )(short_targets, *last.result)
        qkv_grad = qkv_grad.transpose(1, 0, 2)
    else:

        def natural_rows(pair, targets):
            both = jnp.concatenate(pair, axis=0).reshape(wide, -1, 512)
            places = jnp.zeros((wide,), jnp.int32).at[targets].set(jnp.arange(wide, dtype=jnp.int32))
            return jnp.take(both, places, axis=0).astype(F32)

        full = natural_rows(big.result, targets)
        down_grad = full[:, :n_ff].reshape(w_down.shape)
        up_grad = full[:, n_ff : 2 * n_ff].reshape(own_ff, width).T
        out_grad = full[:, 2 * n_ff :].reshape(w_out.shape)
        qkv_grad = natural_rows(last.result, short_targets).reshape(qkv_rows, width).T.reshape(width, 3, head_cols)
    norm_sums = norms.operands[0]
    return (
        block_out.reshape(feats, samp, width),
        input_grad.reshape(feats, samp, width),
        norm_sums[0],
        norm_sums[1],
        qkv_grad,
        out_grad,
        norm_sums[2],
        norm_sums[3],
        up_grad,
        down_grad,
    )


def solution(mesh):
    rows = P("narrow", "wide", None)
    placed = (
        rows, P(), P(), P(), P(None, None, "narrow"), P("narrow", None),
        P(), P(), P(None, "narrow"), P("narrow", None), rows,
    )
    outs = (
        rows, rows, P(), P(), P(None, None, "narrow"), P("narrow", None),
        P(), P(), P(None, "narrow"), P("narrow", None),
    )
    return jax.shard_map(local, mesh=mesh, in_specs=placed, out_specs=outs, check_vma=False)
```

```python
import functools

import jax
import jax.numpy as jnp
import numpy as np
from jax import lax
from jax.experimental import pallas as pl
from jax.experimental.pallas import tpu as pltpu
from jax.sharding import PartitionSpec as P

HEAD_DIM = 64
HEADS_PER_GROUP = 4
GROUP_COLS = HEAD_DIM * HEADS_PER_GROUP
EPS = 1e-05
SCALE = HEAD_DIM ** (-0.5)
F32 = jnp.float32
BF16 = jnp.bfloat16
NEG = -1e30
CHUNK = 256
RHYTHM = (1, 0, 1, 1)


def dot_nn(a, b):
    return lax.dot_general(a, b, (((1,), (0,)), ((), ())), preferred_element_type=F32)


def dot_nt(a, b):
    return lax.dot_general(a, b, (((1,), (1,)), ((), ())), preferred_element_type=F32)


def dot_tn(a, b):
    return lax.dot_general(a, b, (((0,), (0,)), ((), ())), preferred_element_type=F32)


def norm_parts(z):
    mean = jnp.mean(z, axis=-1, keepdims=True)
    centred = z - mean
    var = jnp.mean(centred * centred, axis=-1, keepdims=True)
    rstd = lax.rsqrt(var + EPS)
    return centred * rstd, rstd


def norm_back(grad, xhat, rstd, gain):
    gg = grad * gain
    m1 = jnp.mean(gg, axis=-1, keepdims=True)
    m2 = jnp.mean(gg * xhat, axis=-1, keepdims=True)
    return rstd * (gg - m1 - xhat * m2)


def lane_head(rows, dtype):
    lane = lax.broadcasted_iota(jnp.int32, (rows, GROUP_COLS), 1)
    return [
        ((lane >= h * HEAD_DIM) & (lane < (h + 1) * HEAD_DIM)).astype(F32).astype(dtype)
        for h in range(HEADS_PER_GROUP)
    ]


def block_diag(rows, masks):
    return jnp.concatenate([rows * m for m in masks], axis=0)


def pick_heads(full, rows):
    low = lax.broadcasted_iota(jnp.int32, (rows, 2 * HEAD_DIM), 1) < HEAD_DIM
    out = []
    for pair in range(HEADS_PER_GROUP // 2):
        cols = slice(2 * pair * HEAD_DIM, 2 * (pair + 1) * HEAD_DIM)
        at = 2 * pair * rows
        out.append(jnp.where(low, full[at : at + rows, cols], full[at + rows : at + 2 * rows, cols]))
    return jnp.concatenate(out, axis=1)


def rows_at(index, size):
    return pl.ds(pl.multiple_of(index * size, size), size)


def staged(count, first, second, third, lag=2):
    a, b = {}, {}
    for t in range(count + lag):
        if t < count:
            a[t] = first(t)
        if 0 <= t - 1 < count:
            b[t - 1] = second(t - 1, *a.pop(t - 1))
        if 0 <= t - lag < count:
            third(t - lag, *b.pop(t - lag))


def each(count, body, unroll=1):
    lax.fori_loop(0, count, lambda i, carry: (body(i), carry)[1], 0, unroll=unroll)


def own_kernel(xo, w0, w1, gain, shift, own_ref, normed_ref):
    xhat, _ = norm_parts(xo[...].astype(F32))
    normed = (xhat * gain[...] + shift[...]).astype(BF16)
    normed_ref[...] = normed
    for hg, w in enumerate((w0, w1)):
        own_ref[hg] = dot_nn(normed, w[...]).astype(BF16)


def attn_fwd_kernel(idc, idr, xp, own, xn, w0, w1, gain, shift, qkv_ref, att_ref):
    feats, samp, width = xp.shape
    rows = feats * samp
    x = jnp.concatenate(
        [xp[...].reshape(rows, width), xn[...].reshape(rows, width)], axis=0
    ).astype(F32)
    xhat, _ = norm_parts(x)
    normed = (xhat * gain[...] + shift[...]).astype(BF16)
    for hg, w in enumerate((w0, w1)):
        qkv = dot_nn(normed, w[...]).astype(BF16)
        qkv_ref[hg, 0] = qkv[:rows]
        qkv_ref[hg, 1] = own[hg]
        qkv_ref[hg, 2] = qkv[rows:]
    allowed = idc[...] == idr[1:2, :]
    m16 = lane_head(1, BF16)
    q16 = [m * SCALE for m in m16]

    def first(i):
        f, hg = i // 2, i % 2
        sl = slice(f * samp, (f + 1) * samp)
        k, _ = bwd_pieces(qkv_ref, hg, sl)
        return (dot_nt(k, block_diag(qkv_ref[hg, 1, sl, 0:GROUP_COLS], q16)),)

    def second(i, s):
        s = jnp.where(allowed, s, NEG)
        top = jnp.max(s, axis=0, keepdims=True)
        e = jnp.exp(s - top)
        total = jnp.sum(e, axis=0, keepdims=True)
        return ((e * (1.0 / total)).astype(BF16),)

    def third(i, p):
        f, hg = i // 2, i % 2
        _, v = bwd_pieces(qkv_ref, hg, slice(f * samp, (f + 1) * samp))
        o = pick_heads(dot_tn(p, v), samp)
        att_ref[f, :, hg * GROUP_COLS : (hg + 1) * GROUP_COLS] = o.astype(BF16)

    staged(2 * feats, first, second, third, 1)


def phi_parts(u):
    e = jnp.exp(-0.5 * (u * u))
    t = 1.0 / (1.0 + (0.3275911 * 0.7071067811865476) * jnp.abs(u))
    poly = t * (
        0.127414796
        + t * (-0.142248368 + t * (0.7107068705 + t * (-0.7265760135 + t * 0.5307027145)))
    )
    tail = poly * e
    cdf = jnp.where(u < 0, tail, 1.0 - tail)
    return cdf, u * (e * 0.3989422804014327)


def chain_kernel(others, inpack, ordered, *refs):
    table, x, att, cot, gain, shift, up_own, down_own, out_own = refs[:9]
    refs = refs[9:]
    packs, refs = refs[: 2 * others], refs[2 * others :]
    if inpack:
        extra = packs
    else:
        extra, refs = refs[: 2 * others], refs[2 * others :]
    count = 2 if ordered else 3
    out_ref, hgrad_ref, dat_ref, g2_ref, s2_ref = refs[:5]
    packed, refs = refs[5 : 5 + count], refs[5 + count :]
    (wo, up_a, down_a, up_b, down_b, hidden, normed, mlp, dn2) = refs[:9]
    act_a, pre_a, act_b, pre_b, res, gd, gu, go = refs[9:]
    tokens, width = x.shape
    unit = up_a.shape[1]
    slot = up_own.shape[1] // 2
    per = slot // unit
    last = (2 * others + 2) * per // 2
    narrow_rows = out_own.shape[0]
    half_rows = narrow_rows // 2
    chunks = tokens // CHUNK
    step = pl.program_id(0)
    core = table[0]

    def bases(unit):
        for j in range(1, others + 1):
            yield 2 * j - 2, 2 * j + core
            yield 2 * j - 1, 2 * j + 1 - core

    @pl.when(step == 0)
    def _():
        wo[:narrow_rows] = out_own[...]
        for i, base in bases(half_rows):
            wo[rows_at(base, half_rows)] = packs[i][2 * slot : 2 * slot + half_rows] if inpack else packs[i][slot : slot + half_rows]
        g2_ref[...] = jnp.zeros_like(g2_ref)
        s2_ref[...] = jnp.zeros_like(s2_ref)
        for ref in (act_b, pre_b, up_b, down_b):
            ref[...] = jnp.zeros_like(ref)

        def start(i):
            sl = rows_at(i, CHUNK)
            h = x[sl].astype(F32) + dot_nn(att[sl], wo[...])
            hidden[sl] = h
            xhat, _ = norm_parts(h)
            normed[sl] = (xhat * gain[...] + shift[...]).astype(BF16)
            mlp[sl] = jnp.zeros((CHUNK, width), F32)
            dn2[sl] = jnp.zeros((CHUNK, width), F32)

        each(chunks, start)

    def load(parity, up, down):
        for pair in range(last):

            @pl.when(step == pair)
            def _():
                i, sub = divmod(2 * pair + parity, per)
                low, high = sub * unit, (sub + 1) * unit
                if i < 2:
                    low, high = low + i * slot, high + i * slot
                    up[...] = up_own[:, low:high]
                    down[...] = down_own[low:high]
                elif inpack:
                    up[...] = packs[i - 2][:slot, low:high]
                    down[...] = packs[i - 2][slot + low : slot + high]
                else:
                    up[...] = extra[i - 2][:, low:high]
                    down[...] = packs[i - 2][low:high]

    def place(item):
        i, sub = item // per, item % per
        swapped = jnp.where(i % 2 == 0, core, 1 - core)
        base = jnp.where(i < 2, i, i - i % 2 + swapped)
        return rows_at(base * per + sub, unit)

    def spread(item, up, down, act, pre):
        at = place(item)
        half = width // 2
        for i in range(chunks):
            sl = slice(i * CHUNK, (i + 1) * CHUNK)
            mlp[sl] += dot_nn(act[sl], down[...])
            dn2[sl] += dot_nt(pre[sl], up[...])
            for j in range(i, 4, chunks):
                cols = slice((j % 2) * half, (j % 2 + 1) * half)
                if j < 2:
                    gd[at, cols] = dot_tn(act[...], cot[:, cols]).astype(BF16)
                else:
                    gu[at, cols] = dot_tn(pre[...], normed[:, cols]).astype(BF16)
            yield

    def phase(up, down, act, pre, *before):
        rest = spread(*before)
        ready = {}
        for i in range(chunks + 1):
            if i < chunks:
                sl = slice(i * CHUNK, (i + 1) * CHUNK)
                ready[i] = dot_nn(normed[sl], up[...]), dot_nt(cot[sl], down[...])
            if i > 0:
                next(rest)
                u, back = ready.pop(i - 1)
                sl = slice((i - 1) * CHUNK, i * CHUNK)
                cdf, upd = phi_parts(u)
                act[sl] = (u * cdf).astype(BF16)
                pre[sl] = (back * (cdf + upd)).astype(BF16)

    load(0, up_a, down_a)

    @pl.when(step < last)
    def _():
        before = jnp.maximum(2 * step - 1, 0)
        phase(up_a, down_a, act_a, pre_a, before, up_b, down_b, act_b, pre_b)

    load(1, up_b, down_b)

    @pl.when(step < last)
    def _():
        phase(up_b, down_b, act_b, pre_b, 2 * step, up_a, down_a, act_a, pre_a)

    @pl.when(step == last)
    def _():
        for _ in spread(2 * last - 1, up_b, down_b, act_b, pre_b):
            pass

        def finish(i):
            sl = rows_at(i, CHUNK)
            h = hidden[sl]
            out_ref[sl] = (h + mlp[sl]).astype(BF16)
            xhat, rstd = norm_parts(h)
            d = dn2[sl]
            g2_ref[...] += jnp.sum(d * xhat, axis=0, keepdims=True)
            s2_ref[...] += jnp.sum(d, axis=0, keepdims=True)
            hgrad = cot[sl].astype(F32) + norm_back(d, xhat, rstd, gain[...])
            hgrad_ref[sl] = hgrad
            r = hgrad.astype(BF16)
            res[sl] = r
            dat_ref[sl] = dot_nt(r, wo[...]).astype(BF16)

        each(chunks, finish)
        go[...] = dot_tn(att[...], res[...]).astype(BF16)
        if ordered:
            blocks = (table.shape[0] - 1) // 2
            n_ff = gd.shape[0] // (2 * blocks)
            n_out = go.shape[0] // (2 * blocks)
            size = 2 * n_ff + n_out
            for side in range(2):
                for b in range(blocks):
                    src = table[1 + side * blocks + b]
                    ref = packed[side]
                    ref[b * size : b * size + n_ff] = gd[rows_at(src, n_ff)]
                    ref[b * size + n_ff : b * size + 2 * n_ff] = gu[rows_at(src, n_ff)]
                    ref[b * size + 2 * n_ff : (b + 1) * size] = go[rows_at(src, n_out)]
        else:
            packed[0][...] = gd[...]
            packed[1][...] = gu[...]
            packed[2][...] = go[...]


def bwd_pieces(qkv_ref, hg, sl):
    k = jnp.concatenate(
        [qkv_ref[hg, w, sl, GROUP_COLS : 2 * GROUP_COLS] for w in range(3)], axis=0
    )
    v = jnp.concatenate(
        [qkv_ref[hg, w, sl, 2 * GROUP_COLS : 3 * GROUP_COLS] for w in range(3)], axis=0
    )
    return k, v


def head_rows(a):
    return jnp.concatenate(
        [a[:, h * HEAD_DIM : (h + 1) * HEAD_DIM] for h in range(HEADS_PER_GROUP)], axis=0
    )


def score_grads(s, dp, mask):
    s = jnp.where(mask, s, NEG)
    top = jnp.max(s, axis=0, keepdims=True)
    e = jnp.exp(s - top)
    total = jnp.sum(e, axis=0, keepdims=True)
    p = e * (1.0 / total)
    pd = p * dp
    delta = jnp.sum(pd, axis=0, keepdims=True)
    return (pd - p * delta).astype(BF16), p


def attn_bwd_own_kernel(idc, idr, qkv_ref, do_ref, dq_ref, dkv_ref):
    feats, samp, width = do_ref.shape
    m16 = lane_head(1, BF16)
    q16 = [m * SCALE for m in m16]
    mask = idc[...] == idr[1:2, :]

    def pieces(i):
        f, hg = i // 2, i % 2
        sl = slice(f * samp, (f + 1) * samp)
        q = qkv_ref[hg, 1, sl, 0:GROUP_COLS]
        d = do_ref[f, :, hg * GROUP_COLS : (hg + 1) * GROUP_COLS]
        return hg, sl, q, d

    def first(i):
        hg, sl, q, d = pieces(i)
        k, v = bwd_pieces(qkv_ref, hg, sl)
        return dot_nt(k, block_diag(q, q16)), dot_nt(v, block_diag(d, m16))

    def second(i, s, dp):
        ds, p = score_grads(s, dp, mask)
        own = slice(samp, 2 * samp)
        return ds, head_rows(ds[own]), head_rows(p[own].astype(BF16))

    def third(i, ds, dss, ps):
        hg, sl, q, d = pieces(i)
        k, _ = bwd_pieces(qkv_ref, hg, sl)
        dq_ref[hg, sl, :] = (pick_heads(dot_tn(ds, k), samp) * SCALE).astype(BF16)
        dkv_ref[hg, sl, 0:GROUP_COLS] = pick_heads(dot_nn(dss, q), samp)
        dkv_ref[hg, sl, GROUP_COLS : 2 * GROUP_COLS] = pick_heads(dot_nn(ps, d), samp)

    staged(2 * feats, first, second, third)


def attn_bwd_near_kernel(idc, idr, qkv_ref, dp_ref, dn_ref, sum_ref, *rest):
    dkv_ref = rest[-1]
    feats, samp, width = dp_ref.shape
    m16 = lane_head(1, BF16)
    q16 = [m * SCALE for m in m16]
    near = ((0, 0, dp_ref), (2, 1, dn_ref))
    masks = [idc[a * samp : (a + 2) * samp, :] == idr[g : g + 1, :] for g, a, _ in near]

    def pieces(i, side):
        f, hg = i // 2, i % 2
        sl = slice(f * samp, (f + 1) * samp)
        g, a, ref = near[side]
        q = qkv_ref[hg, g, sl, 0:GROUP_COLS]
        d = ref[f, :, hg * GROUP_COLS : (hg + 1) * GROUP_COLS]
        return hg, sl, slice(a * samp, (a + 2) * samp), q, d

    def first(i):
        out = []
        for side in range(2):
            hg, sl, span, q, d = pieces(i, side)
            k, v = bwd_pieces(qkv_ref, hg, sl)
            out += [dot_nt(k[span], block_diag(q, q16)), dot_nt(v[span], block_diag(d, m16))]
        return out

    def second(i, s0, dp0, s1, dp1):
        dss, ps = [], []
        for side, (s, dp) in enumerate(((s0, dp0), (s1, dp1))):
            ds, p = score_grads(s, dp, masks[side])
            own = slice((1 - side) * samp, (2 - side) * samp)
            dss.append(head_rows(ds[own]))
            ps.append(head_rows(p[own].astype(BF16)))
        return jnp.concatenate(dss, axis=1), jnp.concatenate(ps, axis=1)

    def third(i, dss, ps):
        hg, sl, _, q0, d0 = pieces(i, 0)
        _, _, _, q1, d1 = pieces(i, 1)
        low, high = slice(0, GROUP_COLS), slice(GROUP_COLS, 2 * GROUP_COLS)
        dk = pick_heads(dot_nn(dss, jnp.concatenate([q0, q1], axis=0)), samp)
        dv = pick_heads(dot_nn(ps, jnp.concatenate([d0, d1], axis=0)), samp)
        dkv_ref[hg, sl, low] = ((dk + sum_ref[hg, sl, low]) * SCALE).astype(BF16)
        dkv_ref[hg, sl, high] = (dv + sum_ref[hg, sl, high]).astype(BF16)

    staged(2 * feats, first, second, third)


def qkv_grad_kernel(ordered, table, normed, dq, dkv, *refs):
    outs, gq = refs[:-1], refs[-1]
    hg = pl.program_id(0)
    gq[rows_at(3 * hg, GROUP_COLS)] = dot_tn(dq[0], normed[...]).astype(BF16)
    for j in range(2):
        cols = slice(j * GROUP_COLS, (j + 1) * GROUP_COLS)
        gq[rows_at(3 * hg + 1 + j, GROUP_COLS)] = dot_tn(dkv[0, :, cols], normed[...]).astype(BF16)

    @pl.when(hg == 1)
    def _():
        arrange_qkv(ordered, table, outs, gq)


def arrange_qkv(ordered, table, outs, gq):
    if ordered:
        blocks = (table.shape[0] - 1) // 2
        size = gq.shape[0] // (2 * blocks)
        for side in range(2):
            for b in range(blocks):
                outs[side][b * size : (b + 1) * size] = gq[rows_at(table[1 + side * blocks + b], size)]
    else:
        outs[0][...] = gq[...]


def input_grad_kernel(x, hgrad, dq, dkv, w0, w1, gain, igrad_ref, g1_ref, s1_ref):
    xhat, rstd = norm_parts(x[...].astype(F32))
    dn1 = dot_nt(dq[0], w0[:, :GROUP_COLS]) + dot_nt(dq[1], w1[:, :GROUP_COLS])
    dn1 = dn1 + dot_nt(dkv[0], w0[:, GROUP_COLS:]) + dot_nt(dkv[1], w1[:, GROUP_COLS:])

    @pl.when(pl.program_id(0) == 0)
    def _():
        g1_ref[...] = jnp.zeros_like(g1_ref)
        s1_ref[...] = jnp.zeros_like(s1_ref)

    g1_ref[...] += jnp.sum(dn1 * xhat, axis=0, keepdims=True)
    s1_ref[...] += jnp.sum(dn1, axis=0, keepdims=True)
    igrad_ref[...] = hgrad[...] + norm_back(dn1, xhat, rstd, gain[...])


def ffn_out_kernel(n_ff, n_out, table, mine, got, up_ref, down_ref, out_ref, turned):
    size = 2 * n_ff + n_out
    blocks = mine.shape[0] // size
    for side, ref in enumerate((mine, got)):
        for b in range(blocks):
            to = table[side * blocks + b]
            down_ref[rows_at(to, n_ff)] = ref[b * size : b * size + n_ff].astype(F32)
            turned[rows_at(to, n_ff)] = ref[b * size + n_ff : b * size + 2 * n_ff].astype(F32)
            out_ref[rows_at(to, n_out)] = ref[b * size + 2 * n_ff : (b + 1) * size].astype(F32)
    up_ref[...] = turned[...].T


def qkv_out_kernel(table, mine, got, out_ref, turned):
    blocks = table.shape[0] // 2
    size = mine.shape[0] // blocks
    for side, ref in enumerate((mine, got)):
        for b in range(blocks):
            turned[rows_at(table[side * blocks + b], size)] = ref[b * size : (b + 1) * size].astype(F32)
    for j in range(3):
        cols = turned.shape[0] // 3
        out_ref[j] = turned[j * cols : (j + 1) * cols].T


def swap(x, axis, bit):
    count = lax.axis_size(axis)
    return lax.ppermute(x, axis, [(i, i ^ bit) for i in range(count)])


def halo(x, axis):
    count = lax.axis_size(axis)
    prev = lax.ppermute(x, axis, [(i, i + 1) for i in range(count - 1)])
    nxt = lax.ppermute(x, axis, [(i + 1, i) for i in range(count - 1)])
    return prev, nxt


def gather_pieces(x, axis):
    pieces = [x]
    bit = 1
    while bit < lax.axis_size(axis):
        pieces = pieces + [swap(p, axis, bit) for p in pieces]
        bit *= 2
    return pieces


def tied(*arrays):
    return lax.optimization_barrier(arrays)


class Plan:

    def __init__(self, wide, narrow, fours=False):
        self.wide, self.narrow, self.fours = wide, narrow, fours
        nb = [("narrow", 1 << i) for i in range(narrow.bit_length() - 1)][::-1]
        wb = [("wide", 1 << i) for i in range(1, wide.bit_length() - 1)]
        first = nb + wb
        second = wb[:1] + nb + wb[1:] if fours else wb[1:2] + nb + wb[:1] + wb[2:]
        self.orders = (first, second)
        self.steps = len(first)
        self.blocks = 1 << self.steps
        self.back = [[s for s in o if s[0] == "wide"][::-1] for o in self.orders]
        self.me = lax.axis_index("wide")
        self.core = self.me % 2

    def rel(self, order):
        j = np.zeros(self.blocks, np.int32)
        r = np.zeros(self.blocks, np.int32)
        for s, (axis, bit) in enumerate(order):
            has = (np.arange(self.blocks) >> (self.steps - 1 - s)) & 1
            if axis == "narrow":
                j += has * bit
            else:
                r += has * bit
        return j, r

    def by_core(self, a, b):
        return jnp.where(self.core == 0, jnp.asarray(a, jnp.int32), jnp.asarray(b, jnp.int32))

    def sources(self):
        (j0, r0), (j1, r1) = (self.rel(o) for o in self.orders)
        high = self.me - self.core
        n0, n1 = j0 * self.wide, j1 * self.wide
        mine = self.by_core(n0, n1) + (self.by_core(r0, r1) ^ high) + self.core
        send = self.by_core(n1, n0) + (self.by_core(r1, r0) ^ high) + 1 - self.core
        return jnp.concatenate([self.core[None], mine, send]).astype(jnp.int32)

    def targets(self):
        rels = []
        for o in self.orders:
            j, r = self.rel(o)
            rels.append(r[j == 0])
        high = self.me - self.core
        mine = (self.by_core(rels[0], rels[1]) ^ high) + self.core
        got = (self.by_core(rels[1], rels[0]) ^ high) + 1 - self.core
        return jnp.concatenate([mine, got]).astype(jnp.int32)

    def mixed(self, x, steps):
        pairs = []
        for w in range(self.wide):
            axis, bit = steps[w % 2]
            for n in range(self.narrow):
                to = (w, n ^ bit) if axis == "narrow" else (w ^ bit, n)
                pairs.append((w * self.narrow + n, to[0] * self.narrow + to[1]))
        return lax.ppermute(x, ("wide", "narrow"), pairs)


class Reduction:

    def __init__(self, plan, mine, send):
        self.plan, self.parts, self.operands, self.at = plan, [mine], [send], 0
        self.rows = mine.shape[0]
        self.work = self.stages()

    def total(self, low, high):
        out = self.parts[0][low:high].astype(F32)
        for p in self.parts[1:]:
            out = out + p[low:high].astype(F32)
        return out.astype(BF16)

    def around(self, operands):
        (_, high), (_, low) = self.plan.orders[0][-2:]
        bits = [low, high, high + low]
        return [swap(o, "wide", b) for o, b in zip(operands, bits)]

    def stages(self):
        plan, rows = self.plan, self.rows
        four = 2 if plan.fours else 0
        self.parts.append(swap(self.operands[0], "wide", 1))
        for at in range(plan.steps - four):
            self.operands = [self.total(rows >> (at + 1), rows >> at)]
            yield
            self.parts.append(plan.mixed(self.operands[0], [o[at] for o in plan.orders]))
        if four:
            size = rows >> plan.steps
            self.operands = [self.total(q * size, (q + 1) * size) for q in (1, 2, 3)]
            yield
            self.parts += self.around(self.operands)
        held = self.total(0, rows >> plan.steps)
        if four:
            self.operands = [held]
            yield
            held = jnp.concatenate([held] + self.around([self.operands[0]] * 3), axis=0)
        for at in range(four, len(plan.back[0])):
            self.operands = [held]
            yield
            got = plan.mixed(self.operands[0], [o[at] for o in plan.back])
            held = jnp.concatenate([self.operands[0], got], axis=0)
        self.operands = [held]
        yield
        self.result = (self.operands[0], swap(self.operands[0], "wide", 1))

    def advance(self):
        next(self.work, None)


def lockstep(*chains):
    if len(chains) > 1:
        held = tied([c.operands for c in chains])[0]
        for c, o in zip(chains, held):
            c.operands = list(o)
    for c in chains:
        c.advance()


def hold(value, chain):
    value, operands = tied(value, chain.operands)
    chain.operands = list(operands)
    return value


class SmallSum:
    def __init__(self, value):
        self.operands = [value]
        self.bits = [(a, 1 << i) for a in ("wide", "narrow") for i in range(lax.axis_size(a).bit_length() - 1)]

    def advance(self):
        if self.bits:
            (value,) = self.operands
            self.operands = [value + swap(value, *self.bits.pop(0))]


def local(
    inputs, segment_ids, norm1_gain, norm1_shift, w_qkv, w_out,
    norm2_gain, norm2_shift, w_up, w_down, cotangent,
):
    feats, samp, width = inputs.shape
    tokens = feats * samp
    narrow = lax.axis_size("narrow")
    wide = lax.axis_size("wide")
    plan, short = Plan(wide, narrow), Plan(wide, narrow, True)
    core = plan.core
    group = max(g for g in (1, 2, 4) if feats % (2 * g) == 0)
    steps = feats // group
    rows = group * samp
    head_cols = w_qkv.shape[2]
    own_ff = w_up.shape[1]
    slot = own_ff // 2
    ff = own_ff * narrow
    inpack = slot == 512
    unit = min(256, slot)
    n_ff, n_out, n_qkv = own_ff // wide, w_out.shape[0] // wide, 3 * head_cols // wide
    ordered = narrow == 2 and n_ff % 16 == 0 and n_out % 16 == 0 and n_qkv % 16 == 0
    blocks = plan.blocks

    def core_half(a, axis):
        size = a.shape[axis] // 2
        return lax.dynamic_slice_in_dim(a, core * size, size, axis)

    qkv_half = core_half(w_qkv.reshape(width, 3 * head_cols), 0)
    up_half = core_half(w_up, 1)
    small = jnp.concatenate(
        [up_half.reshape(-1, 512), core_half(w_down, 0), core_half(w_out, 0)], axis=0
    )
    x_prev, x_next = halo(inputs, "wide")
    qkv_mine = gather_pieces(qkv_half, "narrow")[1:]
    pack_mine = gather_pieces(small, "narrow")[1:]
    qkv_got = [swap(p, "wide", 1) for p in qkv_mine]
    def whole_of(mine, got):
        first = jnp.where(core == 0, mine, got)
        second = jnp.where(core == 0, got, mine)
        return jnp.concatenate([first, second], axis=0)

    pieces = [w_qkv] + [
        whole_of(m, g).reshape(width, 3, head_cols) for m, g in zip(qkv_mine, qkv_got)
    ]
    cut = narrow // 2
    w0, w1 = (
        (p[0] if len(p) == 1 else jnp.concatenate(p, axis=2)).reshape(width, 3 * GROUP_COLS)
        for p in (pieces[:cut], pieces[cut:])
    )

    id_rim = jnp.full((samp,), -1, jnp.int32)
    padded_ids = jnp.concatenate([id_rim, segment_ids, id_rim])
    window_ids = lax.dynamic_slice_in_dim(padded_ids, plan.me * samp, 3 * samp, 0)
    id_col = window_ids[:, None]
    id_row = jnp.tile(window_ids.reshape(3, samp), (1, HEADS_PER_GROUP))
    gain1, shift1 = norm1_gain[None, :], norm1_shift[None, :]
    gain2, shift2 = norm2_gain[None, :], norm2_shift[None, :]
    sources, targets = plan.sources(), plan.targets()
    short_sources, short_targets = short.sources(), short.targets()

    def whole(a):
        return pl.BlockSpec(a.shape, lambda i: (0,) * a.ndim, pipeline_mode=pl.Buffered(1))

    cube = pl.BlockSpec((group, samp, width), lambda i: (i, 0, 0))
    smem = pl.BlockSpec(memory_space=pltpu.SMEM)
    line = pl.BlockSpec((1, width), lambda i: (0, 0))
    vec = jax.ShapeDtypeStruct((1, width), F32)

    def tok(dtype):
        return jax.ShapeDtypeStruct((tokens, width), dtype)

    def cost(flops, size):
        return pl.CostEstimate(flops=flops, bytes_accessed=size, transcendentals=0)

    qkv_block = pl.BlockSpec((2, 3, rows, 3 * GROUP_COLS), lambda i: (0, 0, i, 0))

    own_block = pl.BlockSpec((2, rows, 3 * GROUP_COLS), lambda i: (0, i, 0))
    args = [w0, w1, gain1, shift1]
    own, normed_one = pl.pallas_call(
        own_kernel,
        grid=(steps,),
        in_specs=[pl.BlockSpec((rows, width), lambda i: (i, 0))] + [whole(a) for a in args],
        out_specs=[own_block, pl.BlockSpec((rows, width), lambda i: (i, 0))],
        out_shape=[jax.ShapeDtypeStruct((2, tokens, 3 * GROUP_COLS), BF16), tok(BF16)],
        cost_estimate=cost(2 * 10**9, 6 << 20),
        name="own_qkv",
    )(inputs.reshape(tokens, width), *args)
    args = [id_col, id_row, x_prev, own, x_next, w0, w1, gain1, shift1]
    qkv, attended = pl.pallas_call(
        attn_fwd_kernel,
        grid=(steps,),
        in_specs=[whole(id_col), whole(id_row), cube, own_block, cube]
        + [whole(a) for a in (w0, w1, gain1, shift1)],
        out_specs=[qkv_block, cube],
        out_shape=[
            jax.ShapeDtypeStruct((2, 3, tokens, 3 * GROUP_COLS), BF16),
            jax.ShapeDtypeStruct((feats, samp, width), BF16),
        ],
        cost_estimate=cost(6 * 10**9, 24 << 20),
        name="attn_fwd",
    )(*args)
    attended, *pack_mine = tied(attended, *pack_mine)
    pack_got = [swap(p, "wide", 1) for p in pack_mine]

    x_flat = inputs.reshape(tokens, width)
    cot_flat = cotangent.reshape(tokens, width)
    att_flat = attended.reshape(tokens, width)
    packs = [a for pair in zip(pack_mine, pack_got) for a in pair]
    args = [sources, x_flat, att_flat, cot_flat, gain2, shift2, w_up, w_down, w_out]
    if inpack:
        args += packs
    else:
        up_rows = width * slot // 512
        args += [p[up_rows:] for p in packs]
        args += [p[:up_rows].reshape(width, slot) for p in packs]
    if ordered:
        size = blocks * (2 * n_ff + n_out)
        sums = [(size, 512)] * 2
    else:
        sums = [(ff, width), (ff, width), (width, width)]
    outs = [tok(BF16), tok(F32), tok(BF16), vec, vec]
    outs += [jax.ShapeDtypeStruct(s, BF16) for s in sums]
    scratch = [
        ((width, width), BF16), ((width, unit), BF16), ((unit, width), BF16),
        ((width, unit), BF16), ((unit, width), BF16),
        ((tokens, width), F32), ((tokens, width), BF16), ((tokens, width), F32), ((tokens, width), F32),
        ((tokens, unit), BF16), ((tokens, unit), BF16), ((tokens, unit), BF16), ((tokens, unit), BF16),
        ((tokens, width), BF16),
        ((ff, width), BF16), ((ff, width), BF16), ((width, width), BF16),
    ]
    block_out, hidden_grad, dattended, gain2_grad, shift2_grad, *packed = pl.pallas_call(
        functools.partial(chain_kernel, narrow - 1, inpack, ordered),
        grid=(narrow * slot // unit + 1,),
        in_specs=[smem] + [whole(a) for a in args[1:]],
        out_specs=[whole(o) for o in outs],
        out_shape=outs,
        scratch_shapes=[pltpu.VMEM(*s) for s in scratch],
        cost_estimate=cost(15 * 10**9, 20 << 20),
        name="chain",
    )(*args)

    def arranged(natural, sources):
        flat = natural.reshape(narrow * wide, natural.shape[2], 512)
        places = sources[1:].reshape(2, blocks)
        return [jnp.take(flat, places[s], axis=0).reshape(-1, 512) for s in range(2)]

    if not ordered:
        down, up, out = (p.reshape(narrow, wide, -1, 512) for p in packed)
        packed = arranged(jnp.concatenate([down, up, out], axis=2), sources)
    big = Reduction(plan, packed[0], packed[1])

    datt = dattended.reshape(feats, samp, width)
    d_prev, d_next = halo(datt, "wide")
    big.advance()

    def pair_block(cols):
        return pl.BlockSpec((2, rows, cols), lambda i: (0, i, 0))

    dq, dkv_own = pl.pallas_call(
        attn_bwd_own_kernel,
        grid=(steps,),
        in_specs=[whole(id_col), whole(id_row), qkv_block, cube],
        out_specs=[pair_block(GROUP_COLS), pair_block(2 * GROUP_COLS)],
        out_shape=[
            jax.ShapeDtypeStruct((2, tokens, GROUP_COLS), BF16),
            jax.ShapeDtypeStruct((2, tokens, 2 * GROUP_COLS), F32),
        ],
        cost_estimate=cost(10 * 10**9, 14 << 20),
        name="attn_bwd_own",
    )(id_col, id_row, qkv, datt)
    dkv = dkv_own
    shares = [steps // 4, steps // 2, steps // 4] if steps % 4 == 0 else [1] * steps
    for h, share in enumerate(shares):
        off = sum(shares[:h])

        def shifted(spec, off=off):
            return pl.BlockSpec(spec.block_shape, lambda i: spec.index_map(i + off))

        dkv = hold(dkv, big)
        big.advance()
        args = [id_col, id_row, qkv, d_prev, d_next, dkv_own if h else dkv]
        specs = [whole(id_col), whole(id_row)]
        specs += [shifted(b) for b in (qkv_block, cube, cube, pair_block(2 * GROUP_COLS))]
        if h:
            args.append(dkv)
            specs.append(pl.BlockSpec(memory_space=pl.ANY))
        dkv = pl.pallas_call(
            attn_bwd_near_kernel,
            grid=(share,),
            in_specs=specs,
            out_specs=shifted(pair_block(2 * GROUP_COLS)),
            out_shape=jax.ShapeDtypeStruct((2, tokens, 2 * GROUP_COLS), BF16),
            input_output_aliases={6: 0} if h else {},
            cost_estimate=cost(2 * share * 10**9, share * 3 << 20),
            name=f"attn_bwd_near_{h}",
        )(*args)
    dkv = hold(dkv, big)
    big.advance()

    natural = (6 * GROUP_COLS, width)
    outs = [jax.ShapeDtypeStruct((blocks * n_qkv, 512), BF16)] * 2
    if not ordered:
        outs = [jax.ShapeDtypeStruct(natural, BF16)]
    args = [short_sources, normed_one, dq, dkv]
    packed = pl.pallas_call(
        functools.partial(qkv_grad_kernel, ordered),
        grid=(2,),
        in_specs=[smem, whole(normed_one)]
        + [pl.BlockSpec((1, tokens, n * GROUP_COLS), lambda i: (i, 0, 0)) for n in (1, 2)],
        out_specs=[whole(o) for o in outs],
        out_shape=outs,
        scratch_shapes=[pltpu.VMEM(natural, BF16)],
        cost_estimate=cost(2 * 10**9, 6 << 20),
        name="qkv_grad",
    )(*args)
    if not ordered:
        turned = packed[0].reshape(2, 3, narrow // 2, head_cols, width).transpose(0, 2, 1, 3, 4)
        packed = arranged(turned.reshape(narrow, wide, n_qkv, width), short_sources)
    *packed, dkv = hold([*packed, dkv], big)
    big.advance()
    last = Reduction(short, packed[0], packed[1])
    last.advance()

    flat = pl.BlockSpec((CHUNK, width), lambda i: (i, 0))
    input_grad, gain1_grad, shift1_grad = pl.pallas_call(
        input_grad_kernel,
        grid=(tokens // CHUNK,),
        in_specs=[flat, flat]
        + [pl.BlockSpec((2, CHUNK, n * GROUP_COLS), lambda i: (0, i, 0)) for n in (1, 2)]
        + [whole(a) for a in (w0, w1, gain1)],
        out_specs=[flat, line, line],
        out_shape=[tok(F32), vec, vec],
        cost_estimate=cost(2 * 10**9, 8 << 20),
        name="input_grad",
    )(x_flat, hidden_grad, dq, dkv, w0, w1, gain1)
    norms = SmallSum(jnp.concatenate([gain1_grad, shift1_grad, gain2_grad, shift2_grad], axis=0))

    for beside in RHYTHM:
        lockstep(*([last, big, norms] if beside else [last, norms]))
    while not hasattr(big, "result"):
        lockstep(last, big, norms)
    if not hasattr(last, "result"):
        big.result = hold(list(big.result), last)
    lockstep(last, norms)
    qkv_rows = 3 * head_cols
    if ordered:
        shapes = [jax.ShapeDtypeStruct(s, F32) for s in (w_up.shape, w_down.shape, w_out.shape)]
        up_grad, down_grad, out_grad = pl.pallas_call(
            functools.partial(ffn_out_kernel, n_ff, n_out),
            grid=(1,),
            in_specs=[smem] + [whole(a) for a in big.result],
            out_specs=[whole(s) for s in shapes],
            out_shape=shapes,
            scratch_shapes=[pltpu.VMEM((own_ff, width), F32)],
            cost_estimate=cost(0, 8 << 20),
            name="ffn_out",
        )(targets, *big.result)
    if ordered:
        out_grad = hold(out_grad, last)
    for _ in range(8):
        lockstep(last, norms)

    if ordered:
        shape = jax.ShapeDtypeStruct((3, width, head_cols), F32)
        qkv_grad = pl.pallas_call(
            qkv_out_kernel,
            grid=(1,),
            in_specs=[smem] + [whole(a) for a in last.result],
            out_specs=whole(shape),
            out_shape=shape,
            scratch_shapes=[pltpu.VMEM((qkv_rows, width), F32)],
            cost_estimate=cost(0, 3 << 20),
            name="qkv_out",
        )(short_targets, *last.result)
        qkv_grad = qkv_grad.transpose(1, 0, 2)
    else:

        def natural_rows(pair, targets):
            both = jnp.concatenate(pair, axis=0).reshape(wide, -1, 512)
            places = jnp.zeros((wide,), jnp.int32).at[targets].set(jnp.arange(wide, dtype=jnp.int32))
            return jnp.take(both, places, axis=0).astype(F32)

        full = natural_rows(big.result, targets)
        down_grad = full[:, :n_ff].reshape(w_down.shape)
        up_grad = full[:, n_ff : 2 * n_ff].reshape(own_ff, width).T
        out_grad = full[:, 2 * n_ff :].reshape(w_out.shape)
        qkv_grad = natural_rows(last.result, short_targets).reshape(qkv_rows, width).T.reshape(width, 3, head_cols)
    norm_sums = norms.operands[0]
    return (
        block_out.reshape(feats, samp, width),
        input_grad.reshape(feats, samp, width),
        norm_sums[0],
        norm_sums[1],
        qkv_grad,
        out_grad,
        norm_sums[2],
        norm_sums[3],
        up_grad,
        down_grad,
    )


def solution(mesh):
    rows = P("narrow", "wide", None)
    placed = (
        rows, P(), P(), P(), P(None, None, "narrow"), P("narrow", None),
        P(), P(), P(None, "narrow"), P("narrow", None), rows,
    )
    outs = (
        rows, rows, P(), P(), P(None, None, "narrow"), P("narrow", None),
        P(), P(), P(None, "narrow"), P("narrow", None),
    )
    return jax.shard_map(local, mesh=mesh, in_specs=placed, out_specs=outs, check_vma=False)
```
